32 devices in a mesh: dp: 8 (over z, x), tensor: 4 (over y, core).
Axes of the slice: x: 2, y: 2, z: 4, core: 2. Of those that a mesh axis runs over, the one named last changes fastest.
Arguments:
- layer_input: float32 [16384, 1024], P(('dp', 'tensor')), may hold values from -6 to 6
- segment_ids: int32 [8, 1024], P('dp'), may hold values from 0 to 3, never falling along the last dimension, each value on 1 to 512 neighbouring positions
- ln_attn_gain: float32 [2, 1024], replicated, may hold values from 0.5 to 1.5
- w_query: float32 [2, 1024, 1024], P(None, 'dp', 'tensor'), may hold values from -0.1875 to 0.1875
- w_key: float32 [2, 1024, 1024], P(None, 'dp', 'tensor'), may hold values from -0.1875 to 0.1875
- w_value: float32 [2, 1024, 1024], P(None, 'dp', 'tensor'), may hold values from -0.1875 to 0.1875
- head_scale: float32 [2, 16], replicated, may hold values from 0.5 to 1.5
- w_out: float32 [2, 1024, 1024], P(None, 'tensor', 'dp'), may hold values from -0.1875 to 0.1875
- ln_post_gain: float32 [2, 1024], replicated, may hold values from 0.5 to 1.5
- ln_ffn_gain: float32 [2, 1024], replicated, may hold values from 0.5 to 1.5
- w_up: float32 [2, 1024, 4096], P(None, 'dp', 'tensor'), may hold values from -0.1875 to 0.1875
- ln_mid_gain: float32 [2, 4096], replicated, may hold values from 0.5 to 1.5
- w_down: float32 [2, 4096, 1024], P(None, 'tensor', 'dp'), may hold values from -0.09375 to 0.09375
- out_cotangent: float32 [16384, 1024], P(('dp', 'tensor')), may hold values from -6 to 6
Outputs:
- block_output: float32 [16384, 1024], P(('dp', 'tensor'))
- input_grad: float32 [16384, 1024], P(('dp', 'tensor'))
- grad_ln_attn_gain: float32 [2, 1024], replicated
- grad_w_query: float32 [2, 1024, 1024], P(None, 'dp', 'tensor')
- grad_w_key: float32 [2, 1024, 1024], P(None, 'dp', 'tensor')
- grad_w_value: float32 [2, 1024, 1024], P(None, 'dp', 'tensor')
- grad_head_scale: float32 [2, 16], replicated
- grad_w_out: float32 [2, 1024, 1024], P(None, 'tensor', 'dp')
- grad_ln_post_gain: float32 [2, 1024], replicated
- grad_ln_ffn_gain: float32 [2, 1024], replicated
- grad_w_up: float32 [2, 1024, 4096], P(None, 'dp', 'tensor')
- grad_ln_mid_gain: float32 [2, 4096], replicated
- grad_w_down: float32 [2, 4096, 1024], P(None, 'tensor', 'dp')
The draws below stay inside these ranges and needn't reach their ends.
Inputs may be any that keep to these rules, and one draw needn't show every extreme that they name: `segment_ids`: along each row numbers never fall; each of the 4 continuations has 1 to 512 positions, and one has exactly 512.
All inputs are finite; a program needn't handle non-finite values.
Results may differ from the reference program's by a relative error of at most 0.017.
The reference program's roundings to bfloat16 on the way count: a program that leaves them out, or rounds other values in their place, can miss the bound.
Values may be sent and summed in bfloat16 or wider, within the bound.
A program may use at most 256 MiB of HBM per device.

```python
import math
import jax
import jax.numpy as jnp
import numpy as np
from jax import lax

D = 1024
H = 16
HD = 64
FF = 4096
LAYERS = 2
PROMPT = 1024
CONT = 512
NCONT = 4
CREGION = 1024
GTOK = 2048
GROUPS = 8
TOKENS = 16384


def shard_levels(stream_key, shape, pieces, least, largest):
    level = 1.0
    for axis_at, blocks in pieces:
        steps = jax.random.uniform(jax.random.fold_in(jax.random.fold_in(stream_key, 6), axis_at), (blocks,), jnp.float32, least / len(pieces), largest / len(pieces))
        level = level * jnp.repeat(jnp.exp(steps), shape[axis_at] // blocks).reshape((-1,) + (1,) * (len(shape) - 1 - axis_at))
    return level


def length_profile(number_of, total, most, slope):
    portions = [(1 << 20) // math.isqrt(rank ** slope) + 1 for rank in range(2, number_of + 1)]
    rest, counts = total - most - (number_of - 1), [1] * (number_of - 1)
    while rest > 0:
        free = [i for i in range(number_of - 1) if counts[i] < most]
        pool, left = sum([portions[i] for i in free]), rest
        for i in free:
            more = min(most - counts[i], max(1, left * portions[i] // pool), rest)
            counts[i] = counts[i] + more
            rest = rest - more
    return np.array([most] + counts)


def ragged(key, count, total, limit, slope):
    if count == 2:
        one = jax.random.randint(key, (), max(1, total - limit), min(limit, total - 1) + 1)
        return jnp.stack([one, total - one])
    tallies = jnp.asarray(length_profile(count, total, limit, slope), jnp.int32)
    couples = (count - 1) // 2
    giver, taker = tallies[1:1 + 2 * couples:2], tallies[2:2 + 2 * couples:2]
    room = jnp.minimum(giver - 1, limit - taker)
    passed = jax.random.randint(jax.random.fold_in(key, 1), (couples,), 0, 1 << 20) % (room + 1)
    tallies = tallies.at[1:1 + 2 * couples:2].set(giver - passed).at[2:2 + 2 * couples:2].set(taker + passed)
    return tallies[jax.random.permutation(jax.random.fold_in(key, 2), count)]


def centred(rng, shape, spread, most, pieces=(), held_as=jnp.bfloat16):
    values = spread * jax.random.normal(rng, shape, jnp.float32)
    if pieces:
        values = values * shard_levels(rng, shape, pieces, -0.22, 0.18)
    return jnp.clip(values, -most, most).astype(held_as)


def setup_inputs(seed: int = 0) -> dict:
    streams_of = jax.random.split(jax.random.key(seed), 15)
    return {
        "layer_input": centred(streams_of[0], (TOKENS, D), 1.0, 6.0, ((0, 32),), jnp.float32),
        "segment_ids": jax.vmap(lambda own: jnp.searchsorted(jnp.cumsum(ragged(own, NCONT, CREGION, CONT, 0)), jnp.arange(CREGION), side="right"))(jax.random.split(streams_of[1], GROUPS)).reshape((GROUPS, CREGION)).astype(jnp.int32),
        "ln_attn_gain": jnp.clip(1.0 + 0.1 * jax.random.normal(streams_of[2], (LAYERS, D), jnp.float32), 0.5, 1.5),
        "w_query": centred(streams_of[3], (LAYERS, D, D), D ** -0.5, 0.1875, ((1, 8), (2, 4)), jnp.float32),
        "w_key": centred(streams_of[4], (LAYERS, D, D), D ** -0.5, 0.1875, ((1, 8), (2, 4)), jnp.float32),
        "w_value": centred(streams_of[5], (LAYERS, D, D), D ** -0.5, 0.1875, ((1, 8), (2, 4)), jnp.float32),
        "head_scale": jnp.clip(jax.random.uniform(streams_of[6], (LAYERS, H), jnp.float32, 0.5, 1.5), 0.5, 1.5),
        "w_out": centred(streams_of[7], (LAYERS, D, D), D ** -0.5, 0.1875, ((1, 4), (2, 8)), jnp.float32),
        "ln_post_gain": jnp.clip(1.0 + 0.1 * jax.random.normal(streams_of[8], (LAYERS, D), jnp.float32), 0.5, 1.5),
        "ln_ffn_gain": jnp.clip(1.0 + 0.1 * jax.random.normal(streams_of[9], (LAYERS, D), jnp.float32), 0.5, 1.5),
        "w_up": centred(streams_of[10], (LAYERS, D, FF), D ** -0.5, 0.1875, ((1, 8), (2, 4)), jnp.float32),
        "ln_mid_gain": jnp.clip(1.0 + 0.1 * jax.random.normal(streams_of[11], (LAYERS, FF), jnp.float32), 0.5, 1.5),
        "w_down": centred(streams_of[12], (LAYERS, FF, D), FF ** -0.5, 0.09375, ((1, 4), (2, 8)), jnp.float32),
        "out_cotangent": centred(streams_of[13], (TOKENS, D), 1.0, 6.0, ((0, 32),), jnp.float32),
    }


NORM_EPSILON = 1e-05
MASKED_SCORE = -1e+30
BEST_PRECISION = lax.Precision.HIGHEST

@jax.custom_vjp
def low(v):
    return lax.optimization_barrier(v.astype(jnp.bfloat16)).astype(jnp.float32)

@jax.custom_vjp
def low_back(v):
    return v

def low_keep(v):
    return (low(v), None)

def low_pass(kept, grad):
    return (grad,)

def back_keep(v):
    return (v, None)

def back_low(kept, grad):
    return (low(grad),)
low.defvjp(low_keep, low_pass)
low_back.defvjp(back_keep, back_low)

def tanh_gelu(inputs):
    return 0.5 * inputs * (1.0 + jnp.tanh(0.7978845608028654 * (inputs + 0.044715 * inputs * inputs * inputs)))

def normalize(values):
    center = values - lax.optimization_barrier(jnp.mean(values, -1, keepdims=True))
    return center * lax.rsqrt(lax.optimization_barrier(jnp.mean(center * center, -1, keepdims=True)) + NORM_EPSILON)

def matmul(left, right):
    return jnp.dot(left, right, precision=BEST_PRECISION, preferred_element_type=jnp.float32)

def attend(queries, all_keys, values, seg_full):
    length = queries.shape[0]
    block_size = min(512, length)
    blocks = length // block_size
    key_pos = jnp.arange(length, dtype=jnp.int32)

    def one_block(block_item):
        query_block, offset = block_item
        query_pos = offset + jnp.arange(block_size, dtype=jnp.int32)
        query_seg = lax.dynamic_slice_in_dim(seg_full, offset, block_size)
        allowed = (key_pos[None, :] <= query_pos[:, None]) & ((key_pos[None, :] < PROMPT) | (query_seg[:, None] == seg_full[None, :]))
        scores = low_back(jnp.einsum('qhd,khd->hqk', query_block, all_keys, precision=BEST_PRECISION) * 0.125)
        scores = jnp.where(allowed[None], scores, MASKED_SCORE)
        highest = lax.optimization_barrier(jnp.max(scores, -1, keepdims=True))
        exponents = jnp.exp(scores - highest)
        weights_low = low(exponents / lax.optimization_barrier(jnp.sum(exponents, -1, keepdims=True)))
        return jnp.einsum('hqk,khd->qhd', weights_low, values, precision=BEST_PRECISION)
    offsets = jnp.arange(blocks, dtype=jnp.int32) * block_size
    stacked = queries.reshape(blocks, block_size, queries.shape[1], queries.shape[2])
    mixture = lax.map(jax.checkpoint(one_block), (stacked, offsets))
    return mixture.reshape(length, queries.shape[1] * queries.shape[2])

def run_group(weights, group_rows, seg_row):
    attn_gain, w_query, w_key, w_value, head_scale, w_out, post_gain, ffn_gain, w_up, mid_gain, w_down = weights
    seg_full = jnp.concatenate([jnp.full((PROMPT,), -1, dtype=jnp.int32), seg_row.astype(jnp.int32)])
    head_shape = (GTOK, H, HD)
    stream = group_rows
    for layer_index in range(LAYERS):
        h_attn = low(normalize(stream) * attn_gain[layer_index])
        queries = low(low_back(matmul(h_attn, w_query[layer_index]))).reshape(head_shape)
        all_keys = low(low_back(matmul(h_attn, w_key[layer_index]))).reshape(head_shape)
        values = low(low_back(matmul(h_attn, w_value[layer_index]))).reshape(head_shape)
        mixture = low_back(attend(queries, all_keys, values, seg_full))
        scaled = low(mixture * jnp.repeat(head_scale[layer_index], HD))
        attn_out = low_back(matmul(scaled, w_out[layer_index]))
        middle = stream + normalize(attn_out) * post_gain[layer_index]
        h_ffn = low(normalize(middle) * ffn_gain[layer_index])
        hidden_pre = low_back(matmul(h_ffn, w_up[layer_index]))
        hidden_out = low(normalize(tanh_gelu(hidden_pre)) * mid_gain[layer_index])
        stream = middle + low_back(matmul(hidden_out, w_down[layer_index]))
    return stream

def forward(stream_in, segment_ids, params):
    rounded = (params[0], low(params[1]), low(params[2]), low(params[3]), params[4], low(params[5]), params[6], params[7], low(params[8]), params[9], low(params[10]))
    group_rows = stream_in.reshape(GROUPS, GTOK, D)

    def one_group(carry, group_item):
        return (carry, jax.checkpoint(run_group)(rounded, group_item[0], group_item[1]))
    _, outputs = lax.scan(one_group, jnp.zeros((), jnp.float32), (group_rows, segment_ids))
    return outputs.reshape(GROUPS * GTOK, D)

def reference(layer_input, segment_ids, ln_attn_gain, w_query, w_key, w_value, head_scale, w_out, ln_post_gain, ln_ffn_gain, w_up, ln_mid_gain, w_down, out_cotangent):
    params = (ln_attn_gain, w_query, w_key, w_value, head_scale, w_out, ln_post_gain, ln_ffn_gain, w_up, ln_mid_gain, w_down)

    def wrapped(stream_in, weights):
        return forward(stream_in, segment_ids, weights)
    block_output, pullback = jax.vjp(wrapped, layer_input, params)
    input_grad, grads = pullback(out_cotangent)
    return (block_output, input_grad, grads[0], grads[1], grads[2], grads[3], grads[4], grads[5], grads[6], grads[7], grads[8], grads[9], grads[10])
```

```python
import functools

import jax
import jax.numpy as jnp
from jax import lax
from jax.experimental import pallas as pl
from jax.experimental.pallas import tpu as pltpu
from jax.sharding import PartitionSpec as P

H = 16
HD = 64
LAYERS = 2
PROMPT = 1024
BLOCK = 512

NORM_EPSILON = 1e-05
MASKED_SCORE = -1e30
F32 = jnp.float32
BF16 = jnp.bfloat16
VMEM_LIMIT = 67_000_000


def tanh_gelu(inputs):
    return (
        0.5
        * inputs
        * (1.0 + jnp.tanh(0.7978845608028654 * (inputs + 0.044715 * inputs * inputs * inputs)))
    )


def normalize(values):
    center = values - jnp.mean(values, -1, keepdims=True)
    factor = lax.rsqrt(jnp.mean(center * center, -1, keepdims=True) + NORM_EPSILON)
    return (center * factor, factor)


def norm_back(grad_norm, normed, factor):
    return factor * (
        grad_norm
        - jnp.mean(grad_norm, -1, keepdims=True)
        - normed * jnp.mean(grad_norm * normed, -1, keepdims=True)
    )


def dot_nn(left, right):
    return lax.dot_general(left, right, (((1,), (0,)), ((), ())), preferred_element_type=F32)


def dot_tn(left, right):
    return lax.dot_general(left, right, (((0,), (0,)), ((), ())), preferred_element_type=F32)


def dot_nt(left, right):
    return lax.dot_general(left, right, (((1,), (1,)), ((), ())), preferred_element_type=F32)


def bit_masks(size):
    masks = []
    while size > 1:
        size //= 2
        masks.append(size)
    return masks


def relative_order(masks):
    order = [0]
    for mask in masks:
        order = order + [mask | other for other in order]
    return order


def swap(array, axis, mask):
    size = lax.axis_size(axis)
    return lax.ppermute(array, axis, [(i, i ^ mask) for i in range(size)])


class Places:
    def __init__(self):
        self.dp_size = lax.axis_size("dp")
        self.tensor_size = lax.axis_size("tensor")
        dp_index = lax.axis_index("dp").astype(jnp.int32)
        self.tensor_index = lax.axis_index("tensor").astype(jnp.int32)
        self.tensor_masks = bit_masks(self.tensor_size)
        masks = bit_masks(self.dp_size)
        self.far_masks = relative_order(masks[:-1])
        self.near_mask = masks[-1]
        dp_order = self.far_masks + [mask | self.near_mask for mask in self.far_masks]
        self.tensor_order = relative_order(self.tensor_masks)
        tensor_inverse = [self.tensor_order.index(i) for i in range(self.tensor_size)]
        self.dp_places = jnp.array(dp_order, jnp.int32) ^ dp_index
        self.tensor_places = jnp.array(self.tensor_order, jnp.int32) ^ self.tensor_index
        spots = jnp.arange(self.tensor_size, dtype=jnp.int32) ^ self.tensor_index
        self.tensor_sources = jnp.array(tensor_inverse, jnp.int32)[spots]


def gather_far(shard, places):
    others = [swap(shard, "dp", mask) for mask in places.far_masks[1:]]
    return jnp.stack([shard] + others)


def gather_near(part, places):
    return [part, swap(part, "dp", places.near_mask)]


def gather_tensor(parts, masks):
    for mask in masks:
        parts = parts + [jax.tree.map(lambda x, m=mask: swap(x, "tensor", m), p) for p in parts]
    return parts


def gather_late_tensor(shard, places):
    pieces = gather_near(gather_far(shard, places), places)
    return gather_tensor([pieces], places.tensor_masks)


def gather_late_near(shard, places):
    parts = gather_tensor([gather_far(shard, places)], places.tensor_masks[:-1])
    pieces = [gather_near(part, places) for part in parts]
    return gather_tensor(pieces, places.tensor_masks[-1:])


def add_low(kept, arrived):
    return (kept.astype(F32) + arrived.astype(F32)).astype(BF16)


def add_halves(kept, arrived):
    return add_low(kept[0], arrived[0]), add_low(kept[1], arrived[1])


def sum_far(kept, arrived, places):
    blocks = [add_low(kept[i], arrived[i]) for i in range(kept.shape[0])]
    return sum_blocks(blocks, places)


def sum_blocks(blocks, places):
    total = blocks[0].astype(F32)
    for block, mask in zip(blocks[1:], places.far_masks[1:]):
        total = total + swap(block, "dp", mask).astype(F32)
    return total


def scatter_pair(kept, sent, hops, places):
    arrived = swap(sent, *hops[0])
    for hop in hops[1:]:
        kept, sent = add_halves(kept, arrived)
        arrived = swap(sent, *hop)
    return sum_far(kept, arrived, places)


def sum_everywhere(vector):
    for axis in ("tensor", "dp"):
        for mask in reversed(bit_masks(lax.axis_size(axis))):
            vector = vector + swap(vector, axis, mask)
    return vector


def block_rows(place_ref, at, rows):
    return pl.ds(pl.multiple_of(place_ref[at] * rows, rows), rows)


def start_rows(spot, blocks, columns, target, semaphore):
    count, _, rows, _ = blocks.shape
    for at in range(count):
        pltpu.make_async_copy(
            blocks.at[at, spot, :, columns], target.at[at * rows : (at + 1) * rows, :], semaphore
        ).start()


def wait_whole(target, semaphore):
    pltpu.make_async_copy(target, target, semaphore).wait()


def each_rows(total, chunk, body):
    def step(at, carry):
        body(pl.ds(pl.multiple_of(at * chunk, chunk), chunk))
        return carry

    lax.fori_loop(0, total // chunk, step, 0)


def fold_lanes(values):
    total = values[:, :128]
    for lane in range(128, values.shape[1], 128):
        total = total + values[:, lane : lane + 128]
    return total


def fold_rows(values):
    return jnp.sum(values.reshape(values.shape[0] // 8, 8, values.shape[1]), axis=0)


CHUNK = 16


def ffn_forward_kernel(parts, last, place_ref, *refs):
    refs = list(refs)

    def take(count):
        taken = refs[:count]
        del refs[:count]
        return taken

    (stream_ref,) = take(1)
    a_refs = take(parts)
    (matrix_ref,) = take(1)
    post_ref, ffn_ref, mid_ref, next_ref = take(4)
    out_ref, middle_ref, next_stream_ref, h_ffn_ref, mean_ref, factor_ref = take(6)
    pre_ref, h_mid_ref = take(2)
    h_next_ref = None if last else take(1)[0]
    w_up, w_out, w_down, active, pre_buf, mid_buf, sums, squares = take(8)
    up_sem, out_sem, down_sem, pre_sem, mid_sem = take(5)
    rows, depth = stream_ref.shape
    wide = w_up.shape[2]
    narrow = w_out.shape[2]
    hidden = parts * wide

    up_columns, down_columns = pl.ds(0, wide), pl.ds(wide, wide)
    out_columns = pl.ds(2 * wide, narrow)
    for at in range(parts):
        start_rows(place_ref[at], matrix_ref, out_columns, w_out.at[at], out_sem)
    for at in range(parts):
        start_rows(place_ref[at], matrix_ref, up_columns, w_up.at[at], up_sem.at[at])
    for at in range(parts):
        start_rows(place_ref[at], matrix_ref, down_columns, w_down.at[at], down_sem.at[at])
    wait_whole(w_out, out_sem)
    out_ref[...] = sum(dot_nt(a_refs[at][...], w_out[at]) for at in range(parts))

    def middle_rows(here):
        normed, _ = normalize(out_ref[here, :])
        middle = stream_ref[here, :] + normed * post_ref[...]
        middle_ref[here, :] = middle
        normed, _ = normalize(middle)
        h_ffn_ref[here, :] = (normed * ffn_ref[...]).astype(BF16)

    each_rows(rows, CHUNK, middle_rows)
    sums[...] = jnp.zeros_like(sums)
    squares[...] = jnp.zeros_like(squares)
    for at in range(parts):
        slot = at % 2
        wait_whole(w_up.at[at], up_sem.at[at])
        if at >= 2:
            pltpu.make_async_copy(
                pre_buf.at[slot], pre_ref.at[at - 2], pre_sem.at[slot]
            ).wait()
        pre_buf[slot] = dot_nn(h_ffn_ref[...], w_up[at])
        pltpu.make_async_copy(pre_buf.at[slot], pre_ref.at[at], pre_sem.at[slot]).start()

        def active_rows(here, at=at, slot=slot):
            value = tanh_gelu(pre_buf[slot, here, :])
            active[at, here, :] = value
            sums[here, :] += fold_lanes(value)
            squares[here, :] += fold_lanes(value * value)

        each_rows(rows, CHUNK, active_rows)
    mean = jnp.sum(sums[...], axis=1, keepdims=True) / hidden
    spread = jnp.sum(squares[...], axis=1, keepdims=True) / hidden - mean * mean
    mean_ref[...] = jnp.broadcast_to(mean, mean_ref.shape)
    factor_ref[...] = jnp.broadcast_to(lax.rsqrt(spread + NORM_EPSILON), factor_ref.shape)
    for at in range(parts):
        slot = at % 2
        if at >= 2:
            pltpu.make_async_copy(
                mid_buf.at[slot], h_mid_ref.at[at - 2], mid_sem.at[slot]
            ).wait()

        def mid_rows(here, at=at, slot=slot):
            normed = (active[at, here, :] - mean_ref[here, :1]) * factor_ref[here, :1]
            mid_buf[slot, here, :] = (normed * mid_ref[at : at + 1, :]).astype(BF16)

        each_rows(rows, CHUNK, mid_rows)
        pltpu.make_async_copy(mid_buf.at[slot], h_mid_ref.at[at], mid_sem.at[slot]).start()
        wait_whole(w_down.at[at], down_sem.at[at])
        product = dot_nt(mid_buf[slot], w_down[at])
        if at == 0:
            next_stream_ref[...] = middle_ref[...] + product
        else:
            next_stream_ref[...] += product
    if not last:

        def next_rows(here):
            normed, _ = normalize(next_stream_ref[here, :])
            h_next_ref[here, :] = (normed * next_ref[...]).astype(BF16)

        each_rows(rows, CHUNK, next_rows)
    for at in range(max(parts - 2, 0), parts):
        slot = at % 2
        pltpu.make_async_copy(pre_buf.at[slot], pre_ref.at[at], pre_sem.at[slot]).wait()
        pltpu.make_async_copy(mid_buf.at[slot], h_mid_ref.at[at], mid_sem.at[slot]).wait()


def ffn_forward(places, stream, a_parts, matrices, post, ffn, mid, following, last):
    rows, depth = stream.shape
    parts, wide = mid.shape
    narrow = a_parts[0].shape[1]
    vmem = pl.BlockSpec(memory_space=pltpu.VMEM)
    hbm = pl.BlockSpec(memory_space=pl.ANY)
    full = jax.ShapeDtypeStruct((rows, depth), F32)
    low = jax.ShapeDtypeStruct((rows, depth), BF16)
    stat = jax.ShapeDtypeStruct((rows, 128), F32)
    outs = [full, full, full, low, stat, stat] + [
        jax.ShapeDtypeStruct((parts, rows, wide), F32),
        jax.ShapeDtypeStruct((parts, rows, wide), BF16),
    ]
    out_specs = [vmem] * 6 + [hbm] * 2
    if not last:
        outs, out_specs = outs + [low], out_specs + [vmem]
    dma = pltpu.SemaphoreType.DMA
    return pl.pallas_call(
        functools.partial(ffn_forward_kernel, parts, last),
        in_specs=[pl.BlockSpec(memory_space=pltpu.SMEM)]
        + [vmem] * (1 + parts)
        + [hbm]
        + [vmem] * 4,
        out_specs=out_specs,
        out_shape=outs,
        scratch_shapes=[
            pltpu.VMEM((parts, depth, wide), BF16),
            pltpu.VMEM((parts, depth, narrow), BF16),
            pltpu.VMEM((parts, depth, wide), BF16),
            pltpu.VMEM((parts, rows, wide), F32),
            pltpu.VMEM((2, rows, wide), F32),
            pltpu.VMEM((2, rows, wide), BF16),
            pltpu.VMEM((rows, 128), F32),
            pltpu.VMEM((rows, 128), F32),
            dma((parts,)),
            dma,
            dma((parts,)),
            dma((2,)),
            dma((2,)),
        ],
        compiler_params=pltpu.CompilerParams(vmem_limit_bytes=VMEM_LIMIT),
        cost_estimate=pl.CostEstimate(
            flops=2 * rows * depth * parts * (2 * wide + narrow),
            bytes_accessed=40 << 20,
            transcendentals=rows * parts * wide,
        ),
        name="ffn_forward",
    )(
        places.tensor_places,
        stream,
        *a_parts,
        matrices,
        post[None],
        ffn[None],
        mid,
        following[None],
    )


def ffn_backward_kernel(parts, place_ref, *refs):
    refs = list(refs)

    def take(count):
        taken = refs[:count]
        del refs[:count]
        return taken

    grad_ref, out_ref, middle_ref, mean_ref, factor_ref, pre_ref = take(6)
    (matrix_ref,) = take(1)
    post_ref, ffn_ref, mid_ref, scale_ref = take(4)
    low_ref, grad_middle_ref, grad_out_ref = take(3)
    dout_refs = take(parts)
    grad_pre_ref, mid_sum_ref, ffn_sum_ref, post_sum_ref = take(4)
    weights, w_out, grad_normed, normed_four, slope, pre_buf, product, low_buf = take(8)
    first, second = take(2)
    weight_sem, out_sem, pre_sem, low_sem = take(4)
    rows, depth = grad_ref.shape
    wide = weights.shape[2]
    narrow = w_out.shape[2]
    hidden = parts * wide

    def read_pre(at):
        return pltpu.make_async_copy(pre_ref.at[at], pre_buf.at[at % 2], pre_sem.at[at % 2])

    up_columns, down_columns = pl.ds(0, wide), pl.ds(wide, wide)
    out_columns = pl.ds(2 * wide, narrow)
    for at in range(parts):
        start_rows(place_ref[at], matrix_ref, down_columns, weights.at[at], weight_sem.at[at])
        if at < 2:
            read_pre(at).start()
    for at in range(parts):
        start_rows(place_ref[at], matrix_ref, out_columns, w_out.at[at], out_sem)
    low_ref[...] = grad_ref[...].astype(BF16)
    first[...] = jnp.zeros_like(first)
    second[...] = jnp.zeros_like(second)
    mid_sum_ref[...] = jnp.zeros_like(mid_sum_ref)
    ffn_sum_ref[...] = jnp.zeros_like(ffn_sum_ref)
    post_sum_ref[...] = jnp.zeros_like(post_sum_ref)
    for at in range(parts):
        wait_whole(weights.at[at], weight_sem.at[at])
        product[...] = dot_nn(low_ref[...], weights[at])
        start_rows(place_ref[at], matrix_ref, up_columns, weights.at[at], weight_sem.at[at])
        read_pre(at).wait()

        def hidden_rows(here, at=at):
            value = pre_buf[at % 2, here, :]
            squared = value * value
            bend = jnp.tanh(0.7978845608028654 * (value + 0.044715 * squared * value))
            raised = 0.5 * (1.0 + bend)
            normed = (value * raised - mean_ref[here, :1]) * factor_ref[here, :1]
            steep = 0.7978845608028654 * (1.0 + 0.134145 * squared)
            slope[at, here, :] = raised + 0.5 * value * (1.0 - bend * bend) * steep
            normed_four[at, here, :] = normed
            grad = product[here, :]
            mid_sum_ref[at] += fold_rows(grad * normed)
            grad = grad * mid_ref[at : at + 1, :]
            grad_normed[at, here, :] = grad
            first[here, :] += fold_lanes(grad)
            second[here, :] += fold_lanes(grad * normed)

        each_rows(rows, CHUNK, hidden_rows)
        if at + 2 < parts:
            read_pre(at + 2).start()
    first[...] = jnp.broadcast_to(
        jnp.sum(first[...], axis=1, keepdims=True) / hidden, first.shape
    )
    second[...] = jnp.broadcast_to(
        jnp.sum(second[...], axis=1, keepdims=True) / hidden, second.shape
    )

    def write_low(at):
        return pltpu.make_async_copy(low_buf.at[at % 2], grad_pre_ref.at[at], low_sem.at[at % 2])

    for at in range(parts):
        if at >= 2:
            write_low(at - 2).wait()

        def pre_rows(here, at=at):
            grad = grad_normed[at, here, :] - first[here, :1]
            grad = factor_ref[here, :1] * (grad - normed_four[at, here, :] * second[here, :1])
            low_buf[at % 2, here, :] = (grad * slope[at, here, :]).astype(BF16)

        each_rows(rows, CHUNK, pre_rows)
        write_low(at).start()
        wait_whole(weights.at[at], weight_sem.at[at])
        part = dot_nt(low_buf[at % 2], weights[at])
        if at == 0:
            product[...] = part
        else:
            product[...] += part

    def middle_rows(here):
        grad = product[here, :]
        normed, factor = normalize(middle_ref[here, :])
        ffn_sum_ref[...] += fold_rows(grad * normed)
        grad = grad_ref[here, :] + norm_back(grad * ffn_ref[...], normed, factor)
        grad_middle_ref[here, :] = grad
        normed, factor = normalize(out_ref[here, :])
        post_sum_ref[...] += fold_rows(grad * normed)
        grad_out_ref[here, :] = norm_back(grad * post_ref[...], normed, factor).astype(BF16)

    each_rows(rows, CHUNK, middle_rows)
    wait_whole(w_out, out_sem)
    for at in range(parts):
        grad = dot_nn(grad_out_ref[...], w_out[at])
        dout_refs[at][...] = (grad * scale_ref[at : at + 1, :]).astype(BF16)
    for at in range(max(parts - 2, 0), parts):
        write_low(at).wait()


def ffn_backward(places, grad, out, middle, mean, factor, pre, matrices, post, ffn, mid, scale):
    rows, depth = grad.shape
    parts, wide = mid.shape
    narrow = scale.shape[1]
    vmem = pl.BlockSpec(memory_space=pltpu.VMEM)
    hbm = pl.BlockSpec(memory_space=pl.ANY)
    low = jax.ShapeDtypeStruct((rows, depth), BF16)
    sums = jax.ShapeDtypeStruct((8, depth), F32)
    dma = pltpu.SemaphoreType.DMA
    return pl.pallas_call(
        functools.partial(ffn_backward_kernel, parts),
        in_specs=[pl.BlockSpec(memory_space=pltpu.SMEM)]
        + [vmem] * 5
        + [hbm] * 2
        + [vmem] * 4,
        out_specs=[vmem] * (3 + parts) + [hbm] + [vmem] * 3,
        out_shape=[low, jax.ShapeDtypeStruct((rows, depth), F32), low]
        + [jax.ShapeDtypeStruct((rows, narrow), BF16)] * parts
        + [
            jax.ShapeDtypeStruct((parts, rows, wide), BF16),
            jax.ShapeDtypeStruct((parts, 8, wide), F32),
            sums,
            sums,
        ],
        scratch_shapes=[
            pltpu.VMEM((parts, depth, wide), BF16),
            pltpu.VMEM((parts, depth, narrow), BF16),
            pltpu.VMEM((parts, rows, wide), F32),
            pltpu.VMEM((parts, rows, wide), F32),
            pltpu.VMEM((parts, rows, wide), F32),
            pltpu.VMEM((2, rows, wide), F32),
            pltpu.VMEM((rows, depth), F32),
            pltpu.VMEM((2, rows, wide), BF16),
            pltpu.VMEM((rows, 128), F32),
            pltpu.VMEM((rows, 128), F32),
            dma((parts,)),
            dma,
            dma((2,)),
            dma((2,)),
        ],
        compiler_params=pltpu.CompilerParams(vmem_limit_bytes=VMEM_LIMIT),
        cost_estimate=pl.CostEstimate(
            flops=2 * rows * depth * parts * (2 * wide + narrow),
            bytes_accessed=44 << 20,
            transcendentals=rows * parts * wide,
        ),
        name="ffn_backward",
    )(
        places.tensor_places,
        grad,
        out,
        middle,
        mean,
        factor,
        pre,
        matrices,
        post[None],
        ffn[None],
        mid,
        scale,
    )


def turned(place_ref, source, plain, target, rows):
    plain[...] = source[...].astype(F32).T.astype(BF16)
    for at in range(target.shape[0] // rows):
        target[at * rows : (at + 1) * rows, :] = plain[block_rows(place_ref, at, rows), :]


def matrix_grads_kernel(parts, place_ref, *refs):
    low_ref, h_ffn_ref, grad_out_ref = refs[:3]
    grad_pre_ref, h_mid_ref, a_ref = refs[3:6]
    up_keep, up_send, down_keep, down_send = refs[6:10]
    low_turned, h_turned, out_turned, low_plain, h_plain, out_plain = refs[10:]
    step = pl.program_id(0)
    depth = low_turned.shape[0]
    count, rows = up_keep.shape[2:4]
    wide = h_mid_ref.shape[2]

    @pl.when(step == 0)
    def _():
        turned(place_ref, low_ref, low_plain, low_turned, rows)
        turned(place_ref, h_ffn_ref, h_plain, h_turned, rows)
        turned(place_ref, grad_out_ref, out_plain, out_turned, rows)

    def fill(up_ref, down_ref):
        shape = (2, count, rows, -1)
        grad = dot_nn(h_turned[...], grad_pre_ref[0]).astype(BF16)
        up_ref[0, :, :, :, :wide] = grad.reshape(shape)
        grad = dot_nn(out_turned[...], a_ref[0]).astype(BF16)
        up_ref[0, :, :, :, wide:] = grad.reshape(shape)
        grad = dot_nn(low_turned[...], h_mid_ref[0]).astype(BF16)
        down_ref[:, 0] = grad.reshape(shape)

    @pl.when(step < parts // 2)
    def _():
        fill(up_keep, down_keep)

    @pl.when(step >= parts // 2)
    def _():
        fill(up_send, down_send)


def matrix_grads_of(places, low, h_ffn, grad_out, grad_pre, h_mid, a_parts):
    rows, depth = low.shape
    parts, _, wide = h_mid.shape
    narrow = a_parts[0].shape[1]
    half = parts // 2
    count = places.dp_size // 2
    block = depth // places.dp_size
    a_all = jnp.stack(a_parts)
    whole = pl.BlockSpec((rows, depth), lambda i, place: (0, 0))
    each = pl.BlockSpec((1, rows, wide), lambda i, place: (i, 0, 0))
    up = (half, 2, count, block, wide + narrow)
    down = (2, half, count, block, wide)
    up_block = (1, 2, count, block, wide + narrow)
    down_block = (2, 1, count, block, wide)
    return pl.pallas_call(
        functools.partial(matrix_grads_kernel, parts),
        grid_spec=pltpu.PrefetchScalarGridSpec(
            num_scalar_prefetch=1,
            grid=(parts,),
            in_specs=[whole] * 3
            + [each] * 2
            + [pl.BlockSpec((1, rows, narrow), lambda i, place: (i, 0, 0))],
            out_specs=[
                pl.BlockSpec(up_block, lambda i, p: (jnp.minimum(i, half - 1), 0, 0, 0, 0)),
                pl.BlockSpec(up_block, lambda i, p: (jnp.maximum(i - half, 0), 0, 0, 0, 0)),
                pl.BlockSpec(down_block, lambda i, p: (0, jnp.minimum(i, half - 1), 0, 0, 0)),
                pl.BlockSpec(down_block, lambda i, p: (0, jnp.maximum(i - half, 0), 0, 0, 0)),
            ],
            scratch_shapes=[pltpu.VMEM((depth, rows), BF16)] * 6,
        ),
        out_shape=[
            jax.ShapeDtypeStruct(up, BF16),
            jax.ShapeDtypeStruct(up, BF16),
            jax.ShapeDtypeStruct(down, BF16),
            jax.ShapeDtypeStruct(down, BF16),
        ],
        compiler_params=pltpu.CompilerParams(vmem_limit_bytes=VMEM_LIMIT),
        cost_estimate=pl.CostEstimate(
            flops=2 * rows * depth * parts * (2 * wide + narrow),
            bytes_accessed=30 << 20,
            transcendentals=0,
        ),
        name="matrix_grads",
    )(places.dp_places, low, h_ffn, grad_out, grad_pre, h_mid, a_all)


def whole_grads_kernel(parts, place_ref, *refs):
    del place_ref
    low_ref, h_ffn_ref, grad_out_ref, grad_pre_ref, h_mid_ref, a_ref, matrix_ref = refs[:7]
    low_turned, h_turned, out_turned = refs[7:]
    wide = h_mid_ref.shape[2]
    shape = matrix_ref.shape[:3] + (-1,)

    @pl.when(pl.program_id(0) == 0)
    def _():
        for source, target in (
            (low_ref, low_turned), (h_ffn_ref, h_turned), (grad_out_ref, out_turned)
        ):
            target[...] = source[...].astype(F32).T.astype(BF16)

    grad = dot_nn(h_turned[...], grad_pre_ref[0]).astype(BF16)
    matrix_ref[:, :, :, :wide] = grad.reshape(shape)
    grad = dot_nn(low_turned[...], h_mid_ref[0]).astype(BF16)
    matrix_ref[:, :, :, wide : 2 * wide] = grad.reshape(shape)
    grad = dot_nn(out_turned[...], a_ref[0]).astype(BF16)
    matrix_ref[:, :, :, 2 * wide :] = grad.reshape(shape)


def whole_grads(places, low, h_ffn, grad_out, grad_pre, h_mid, a_parts):
    rows, depth = low.shape
    parts, _, wide = h_mid.shape
    narrow = a_parts[0].shape[1]
    block = depth // places.dp_size
    columns = 2 * wide + narrow
    whole = pl.BlockSpec((rows, depth), lambda i, place: (0, 0))
    each = pl.BlockSpec((1, rows, wide), lambda i, place: (i, 0, 0))
    return pl.pallas_call(
        functools.partial(whole_grads_kernel, parts),
        grid_spec=pltpu.PrefetchScalarGridSpec(
            num_scalar_prefetch=1,
            grid=(parts,),
            in_specs=[whole] * 3
            + [each] * 2
            + [pl.BlockSpec((1, rows, narrow), lambda i, place: (i, 0, 0))],
            out_specs=pl.BlockSpec(
                (places.dp_size, 1, block, columns), lambda i, place: (0, place[i], 0, 0)
            ),
            scratch_shapes=[pltpu.VMEM((depth, rows), BF16)] * 3,
        ),
        out_shape=jax.ShapeDtypeStruct((places.dp_size, parts, block, columns), BF16),
        compiler_params=pltpu.CompilerParams(vmem_limit_bytes=VMEM_LIMIT),
        cost_estimate=pl.CostEstimate(
            flops=2 * rows * depth * parts * columns,
            bytes_accessed=30 << 20,
            transcendentals=0,
        ),
        name="whole_grads",
    )(places.tensor_places, low, h_ffn, grad_out, grad_pre, h_mid, jnp.stack(a_parts))


def attn_grads_kernel(parts, place_ref, *refs):
    h_refs = refs[:parts]
    packed_ref, keep_ref, send_ref, total = refs[parts:]
    count, rows, _ = keep_ref.shape
    tokens = packed_ref.shape[0] // parts
    for part in range(parts):
        flipped = h_refs[part][...].astype(F32).T.astype(BF16)
        grad = dot_nn(flipped, packed_ref[part * tokens : (part + 1) * tokens, :])
        if part == 0:
            total[...] = grad
        else:
            total[...] += grad
    for at in range(count):
        keep_ref[at] = total[block_rows(place_ref, at, rows), :].astype(BF16)
        send_ref[at] = total[block_rows(place_ref, count + at, rows), :].astype(BF16)


def attn_grads(places, h_parts, packed):
    parts = len(h_parts)
    tokens, depth = h_parts[0].shape
    columns = packed.shape[1]
    count = places.dp_size // 2
    block = depth // places.dp_size
    vmem = pl.BlockSpec(memory_space=pltpu.VMEM)
    return pl.pallas_call(
        functools.partial(attn_grads_kernel, parts),
        in_specs=[pl.BlockSpec(memory_space=pltpu.SMEM)] + [vmem] * (parts + 1),
        out_specs=[vmem] * 2,
        out_shape=[jax.ShapeDtypeStruct((count, block, columns), BF16)] * 2,
        scratch_shapes=[
            pltpu.VMEM((depth, columns), F32),
        ],
        compiler_params=pltpu.CompilerParams(vmem_limit_bytes=VMEM_LIMIT),
        cost_estimate=pl.CostEstimate(
            flops=2 * tokens * parts * depth * columns,
            bytes_accessed=8 << 20,
            transcendentals=0,
        ),
        name="attn_grads",
    )(places.dp_places, *h_parts, packed)


def half_mask(shape, head):
    lane = lax.broadcasted_iota(jnp.int32, shape, len(shape) - 1)
    return (lane // HD) == (head % 2)


def place_rows(place_ref, pieces, target):
    for half, piece in enumerate(pieces):
        count, rows, _ = piece.shape
        for at in range(count):
            target[block_rows(place_ref, half * count + at, rows), :] = piece[at]


def forward_kernel(block_ref, place_ref, *refs):
    parts = block_ref.shape[0]
    rows_refs = refs[:parts]
    pieces = refs[parts : parts + 2]
    column_ref, row_ref, scale_ref = refs[parts + 2 : parts + 5]
    query_ref, key_ref, value_ref, mixture_ref, logsum_ref = refs[parts + 5 : parts + 10]
    scaled_refs = refs[parts + 10 : -2]
    score_ref, weight_ref = refs[-2:]
    width = query_ref.shape[1]
    length = query_ref.shape[0]
    rows = length // parts

    place_rows(place_ref, pieces, weight_ref)
    for part in range(parts):
        at = pl.ds(pl.multiple_of(block_ref[part] * rows, rows), rows)
        packed = dot_nn(rows_refs[part][...], weight_ref[...])
        query_ref[at, :] = packed[:, :width].astype(BF16) * jnp.asarray(0.125, BF16)
        key_ref[at, :] = packed[:, width : 2 * width].astype(BF16)
        value_ref[at, :] = packed[:, 2 * width :].astype(BF16)

    for query_block in range(length // BLOCK):
        here = pl.ds(query_block * BLOCK, BLOCK)

        def one_head(head, logsums, query_block=query_block, here=here):
            lanes = pl.ds(pl.multiple_of((head // 2) * 128, 128), 128)
            own = half_mask((BLOCK, 128), head)
            query = jnp.where(own, query_ref[here, lanes], jnp.asarray(0, BF16))
            highest = jnp.full((BLOCK, 128), MASKED_SCORE, F32)
            for key_block in range(query_block + 1):
                there = pl.ds(key_block * BLOCK, BLOCK)
                scores = dot_nt(query, key_ref[there, lanes])
                if key_block == query_block or key_block * BLOCK >= PROMPT:
                    first = lax.broadcasted_iota(jnp.int32, (BLOCK, BLOCK), 0)
                    second = lax.broadcasted_iota(jnp.int32, (BLOCK, BLOCK), 1)
                    seen = None
                    if key_block == query_block:
                        seen = second <= first
                    if key_block * BLOCK >= PROMPT:
                        query_at = pl.ds(query_block * BLOCK - PROMPT, BLOCK)
                        key_at = pl.ds(key_block * BLOCK - PROMPT, BLOCK)
                        same = column_ref[query_at, :] == row_ref[:, key_at]
                        seen = same if seen is None else seen & same
                    scores = jnp.where(seen, scores, MASKED_SCORE)
                score_ref[:, there] = scores
                for lane in range(0, BLOCK, 128):
                    highest = jnp.maximum(highest, scores[:, lane : lane + 128])
            top = jnp.max(highest, axis=1, keepdims=True)
            total = jnp.zeros((BLOCK, 128), F32)
            mixed = jnp.zeros((BLOCK, 128), F32)
            for key_block in range(query_block + 1):
                there = pl.ds(key_block * BLOCK, BLOCK)
                weights = jnp.exp(score_ref[:, there] - top)
                for lane in range(0, BLOCK, 128):
                    total = total + weights[:, lane : lane + 128]
                mixed = mixed + dot_nn(weights.astype(BF16), value_ref[there, lanes])
            denominator = jnp.sum(total, axis=1, keepdims=True)
            mixed = mixed / denominator
            mixture_ref[here, lanes] = jnp.where(own, mixed, mixture_ref[here, lanes])
            lane = lax.broadcasted_iota(jnp.int32, (BLOCK, 128), 1)
            return jnp.where(lane == head, top + jnp.log(denominator), logsums)

        logsums = lax.fori_loop(0, width // HD, one_head, jnp.zeros((BLOCK, 128), F32))
        logsum_ref[:, here] = logsums.T[: logsum_ref.shape[0], :]

    for part in range(parts):
        at = pl.ds(pl.multiple_of(block_ref[part] * rows, rows), rows)
        scaled_refs[part][...] = (mixture_ref[at, :] * scale_ref[...]).astype(BF16)


def attend_forward(places, rows, pieces, seg_column, seg_row, scale):
    parts = len(rows)
    length = parts * rows[0].shape[0]
    width = pieces[0].shape[2] // 3
    depth = rows[0].shape[1]
    heads = width // HD
    pairs = length * length * 5 // 8
    whole = pl.BlockSpec(memory_space=pltpu.VMEM)
    return pl.pallas_call(
        forward_kernel,
        in_specs=[pl.BlockSpec(memory_space=pltpu.SMEM)] * 2 + [whole] * (parts + 5),
        out_specs=[whole] * (5 + parts),
        out_shape=[jax.ShapeDtypeStruct((length, width), BF16)] * 3
        + [
            jax.ShapeDtypeStruct((length, width), F32),
            jax.ShapeDtypeStruct((8, length), F32),
        ]
        + [jax.ShapeDtypeStruct((length // parts, width), BF16)] * parts,
        scratch_shapes=[
            pltpu.VMEM((BLOCK, length), F32),
            pltpu.VMEM((depth, 3 * width), BF16),
        ],
        compiler_params=pltpu.CompilerParams(vmem_limit_bytes=VMEM_LIMIT),
        cost_estimate=pl.CostEstimate(
            flops=2 * length * depth * 3 * width + heads * pairs * 4 * 256,
            bytes_accessed=20 << 20,
            transcendentals=heads * pairs,
        ),
        name="attend_forward",
    )(places.tensor_places, places.dp_places, *rows, *pieces, seg_column, seg_row, scale)


def backward_kernel(block_ref, place_ref, open_ref, edge_ref, *refs):
    parts = block_ref.shape[0]
    grad_refs = refs[:parts]
    query_ref, key_ref, value_ref, mixture_ref, logsum_ref = refs[parts : parts + 5]
    column_ref, row_ref = refs[parts + 5 : parts + 7]
    pieces = refs[parts + 7 : parts + 9]
    packed_ref, inner_sum_ref, keep_ref, send_ref = refs[parts + 9 : parts + 13]
    dout_ref, inner_ref, dq_ref, dk_ref, dv_ref, weight_ref = refs[parts + 13 :]
    length, width = query_ref.shape
    rows = length // parts

    for part in range(parts):
        at = pl.ds(pl.multiple_of(block_ref[part] * rows, rows), rows)
        dout_ref[at, :] = grad_refs[part][...]
    picks = lax.broadcasted_iota(jnp.int32, (8, width), 1) // HD == lax.broadcasted_iota(
        jnp.int32, (8, width), 0
    )
    picks = jnp.where(picks, 1.0, 0.0)
    inner_sum = jnp.zeros((8, 128), F32)
    for part in range(length // BLOCK):
        at = pl.ds(part * BLOCK, BLOCK)
        product = dout_ref[at, :].astype(F32) * mixture_ref[at, :]
        inner = lax.dot_general(
            picks,
            product,
            (((1,), (1,)), ((), ())),
            precision=lax.Precision.HIGHEST,
            preferred_element_type=F32,
        )
        inner_ref[:, at] = inner
        for lane in range(0, BLOCK, 128):
            inner_sum = inner_sum + inner[:, lane : lane + 128]
    inner_sum_ref[...] = inner_sum
    dq_ref[...] = jnp.zeros_like(dq_ref)
    dk_ref[...] = jnp.zeros_like(dk_ref)
    dv_ref[...] = jnp.zeros_like(dv_ref)

    def one_pair(head, key_block, query_block, edge):
        lanes = pl.ds(pl.multiple_of((head // 2) * 128, 128), 128)
        there = pl.ds(pl.multiple_of(key_block * BLOCK, BLOCK), BLOCK)
        here = pl.ds(pl.multiple_of(query_block * BLOCK, BLOCK), BLOCK)
        own = half_mask((BLOCK, 128), head)
        none = jnp.asarray(0, BF16)
        query = jnp.where(own, query_ref[here, lanes], none)
        dout = jnp.where(own, dout_ref[here, lanes], none)
        key = key_ref[there, lanes]
        scores = dot_nt(key, query)
        weights = jnp.exp(scores - logsum_ref[pl.ds(head, 1), here])
        if edge:
            key_at = key_block * BLOCK + lax.broadcasted_iota(jnp.int32, (BLOCK, BLOCK), 0)
            query_at = query_block * BLOCK + lax.broadcasted_iota(jnp.int32, (BLOCK, BLOCK), 1)
            same = column_ref[there, :] == row_ref[:, here]
            weights = jnp.where((key_at <= query_at) & same, weights, 0.0)
        dv_ref[there, lanes] += dot_nn(weights.astype(BF16), dout)
        grad = dot_nt(value_ref[there, lanes], dout)
        grad = (weights * (grad - inner_ref[pl.ds(head, 1), here])).astype(BF16)
        dk_ref[there, lanes] += dot_nn(grad, query)
        dq_ref[here, lanes] += dot_tn(grad, jnp.where(own, key, none))

    def one_head(head, carry):
        def open_pair(at, inside):
            one_pair(head, open_ref[2 * at], open_ref[2 * at + 1], False)
            return inside

        def edge_pair(at, inside):
            one_pair(head, edge_ref[2 * at], edge_ref[2 * at + 1], True)
            return inside

        lax.fori_loop(0, open_ref.shape[0] // 2, open_pair, 0)
        lax.fori_loop(0, edge_ref.shape[0] // 2, edge_pair, 0)
        return carry

    lax.fori_loop(0, width // HD, one_head, 0)
    for part in range(parts):
        at = pl.ds(pl.multiple_of(block_ref[part] * rows, rows), rows)
        to = pl.ds(part * rows, rows)
        packed_ref[to, :width] = (dq_ref[at, :] * 0.125).astype(BF16)
        packed_ref[to, width : 2 * width] = dk_ref[at, :].astype(BF16)
        packed_ref[to, 2 * width :] = dv_ref[at, :].astype(BF16)
    place_rows(place_ref, pieces, weight_ref)
    for part in range(parts):
        grad = dot_nt(packed_ref[part * rows : (part + 1) * rows, :], weight_ref[...])
        half = parts // 2
        target = keep_ref if part < half else send_ref
        target[part % half] = grad.astype(BF16)


def attend_backward(
    places, grads, queries, keys, values, mixture, logsum, seg_column, seg_row, pieces
):
    parts = len(grads)
    length, width = queries.shape
    heads = width // HD
    depth = pieces[0].shape[0] * pieces[0].shape[1] * 2
    opened, edges = [], []
    for query_block in range(length // BLOCK):
        for key_block in range(query_block + 1):
            if key_block == query_block or key_block * BLOCK >= PROMPT:
                edges += [key_block, query_block]
            else:
                opened += [key_block, query_block]
    whole = pl.BlockSpec(memory_space=pltpu.VMEM)
    scalars = pl.BlockSpec(memory_space=pltpu.SMEM)
    pairs = length * length * 5 // 8
    return pl.pallas_call(
        backward_kernel,
        in_specs=[scalars] * 4 + [whole] * (parts + 9),
        out_specs=[whole] * 4,
        out_shape=[
            jax.ShapeDtypeStruct((length, 3 * width), BF16),
            jax.ShapeDtypeStruct((8, 128), F32),
            jax.ShapeDtypeStruct((parts // 2, length // parts, depth), BF16),
            jax.ShapeDtypeStruct((parts // 2, length // parts, depth), BF16),
        ],
        scratch_shapes=[
            pltpu.VMEM((length, width), BF16),
            pltpu.VMEM((8, length), F32),
            pltpu.VMEM((length, width), F32),
            pltpu.VMEM((length, width), F32),
            pltpu.VMEM((length, width), F32),
            pltpu.VMEM((depth, 3 * width), BF16),
        ],
        compiler_params=pltpu.CompilerParams(vmem_limit_bytes=VMEM_LIMIT),
        cost_estimate=pl.CostEstimate(
            flops=heads * pairs * 10 * 256 + 2 * length * depth * 3 * width,
            bytes_accessed=16 << 20,
            transcendentals=heads * pairs,
        ),
        name="attend_backward",
    )(
        places.tensor_places,
        places.dp_places,
        jnp.array(opened, jnp.int32),
        jnp.array(edges, jnp.int32),
        *grads,
        queries,
        keys,
        values,
        mixture,
        logsum,
        seg_column,
        seg_row,
        *pieces,
    )


def local(
    layer_input,
    segment_ids,
    ln_attn_gain,
    w_query,
    w_key,
    w_value,
    head_scale,
    w_out,
    ln_post_gain,
    ln_ffn_gain,
    w_up,
    ln_mid_gain,
    w_down,
    out_cotangent,
):
    places = Places()
    tensor_size = places.tensor_size
    tensor_order = places.tensor_order
    tensor_masks = places.tensor_masks
    local_heads = H // tensor_size
    width = local_heads * HD
    parts = range(tensor_size)

    seg_row = segment_ids[0][None, :]
    seg_column = segment_ids[0][:, None]
    prompt = jnp.zeros((PROMPT,), jnp.int32)
    long_row = jnp.concatenate([prompt, segment_ids[0]])[None, :]
    long_column = jnp.concatenate([prompt, segment_ids[0]])[:, None]

    attn_shards, matrix_set = [], []
    for layer in range(LAYERS):
        packed = jnp.concatenate([w_query[layer], w_key[layer], w_value[layer]], axis=1)
        attn_shards.append(packed.astype(BF16))
        packed = jnp.concatenate([w_up[layer], w_down[layer].T, w_out[layer].T], axis=1)
        packed = packed.astype(BF16)
        whole = lax.all_gather(packed, ("dp", "tensor"), axis=0, tiled=False)
        matrix_set.append(whole.reshape(places.dp_size, tensor_size, *packed.shape))
    attn_set = [gather_near(gather_far(attn_shards[0], places), places)]

    def exchange(blocks):
        return [
            block if at == 0 else swap(block, "tensor", tensor_order[at])
            for at, block in enumerate(blocks)
        ]

    stream = layer_input
    normed_one, _ = normalize(stream)
    h_attn = (normed_one * ln_attn_gain[0]).astype(BF16)
    saved = []
    for layer in range(LAYERS):
        last = layer == LAYERS - 1
        if layer > 0:
            shard, _ = lax.optimization_barrier((attn_shards[layer], logsum))
            attn_set.append(gather_near(gather_far(shard, places), places))
        h_parts = gather_tensor([h_attn], tensor_masks)
        scale_all = head_scale[layer].reshape(tensor_size, local_heads)
        scale_rel = jnp.repeat(scale_all[places.tensor_places], HD, axis=1)
        queries, keys, values, mixture, logsum, *a_parts = attend_forward(
            places, h_parts, attn_set[layer], seg_column, seg_row, scale_rel[:1]
        )
        a_parts = exchange(a_parts)
        gain_mid = ln_mid_gain[layer].reshape(tensor_size, -1)[places.tensor_places]
        stream_in = stream
        attn_out, middle, stream, h_ffn, mean, factor, pre, h_mid, *h_next = ffn_forward(
            places, stream, a_parts, matrix_set[layer], ln_post_gain[layer], ln_ffn_gain[layer],
            gain_mid, ln_attn_gain[(layer + 1) % LAYERS], last,
        )
        if not last:
            h_attn = h_next[0]
        saved.append(
            (
                stream_in, h_parts, queries, keys, values, mixture, logsum, scale_rel, a_parts,
                attn_out, middle, h_ffn, mean, factor, gain_mid, pre, h_mid,
            )
        )

    grad_stream = out_cotangent
    matrix_grads = [None] * LAYERS
    small_grads = [None] * LAYERS
    core_hop = ("tensor", tensor_masks[-1])
    side_hops = [("tensor", mask) for mask in reversed(tensor_masks[:-1])]
    near_hop = ("dp", places.near_mask)
    for layer in reversed(range(LAYERS)):
        (
            stream_in, h_parts, queries, keys, values, mixture, logsum, scale_rel, a_parts,
            attn_out, middle, h_ffn, mean, factor, gain_mid, pre, h_mid,
        ) = saved[layer]
        grad_low, grad_middle, grad_out, *rest = ffn_backward(
            places, grad_stream, attn_out, middle, mean, factor, pre, matrix_set[layer],
            ln_post_gain[layer], ln_ffn_gain[layer], gain_mid, scale_rel,
        )
        dout_parts = exchange(rest[:tensor_size])
        grad_pre, mid_sum, ffn_sum, post_sum = rest[tensor_size:]
        wide = h_mid.shape[2]
        if layer > 0:
            whole = whole_grads(places, grad_low, h_ffn, grad_out, grad_pre, h_mid, a_parts)
            dout_parts, whole = lax.optimization_barrier((dout_parts, whole))
            whole = whole.reshape(-1, *whole.shape[2:])
            rows = lax.psum_scatter(whole, ("dp", "tensor"), scatter_dimension=0, tiled=False)
            rows = rows.astype(F32)
            up_rows, down_rows, out_rows = (
                rows[:, :wide], rows[:, wide : 2 * wide], rows[:, 2 * wide :]
            )
        else:
            up_keep, up_send, down_keep, down_send = matrix_grads_of(
                places, grad_low, h_ffn, grad_out, grad_pre, h_mid, a_parts
            )
            dout_parts, up_send, down_send = lax.optimization_barrier(
                (dout_parts, up_send, down_send)
            )
            hops = [core_hop] + side_hops + [near_hop]
            upper_rows = scatter_pair(up_keep, up_send, hops, places)
            up_rows, out_rows = upper_rows[:, :wide], upper_rows[:, wide:]
            hops = [core_hop, near_hop] + side_hops
            down_rows = scatter_pair(down_keep, down_send, hops, places)
        packed, inner_sum, keep, send = attend_backward(
            places, dout_parts, queries, keys, values, mixture, logsum, long_column, long_row,
            attn_set[layer],
        )
        grad_head = jnp.sum(inner_sum[:local_heads], 1) / scale_rel[0, ::HD]
        arrived = swap(send, *core_hop)
        for hop in side_hops:
            keep, send = add_halves(keep, arrived)
            arrived = swap(send, *hop)
        grad_h = keep.astype(F32) + arrived.astype(F32)
        attn_keep, attn_send = attn_grads(places, h_parts, packed)
        normed_one, factor_one = normalize(stream_in)
        grad_attn_gain = jnp.sum(grad_h * normed_one, 0)
        grad_stream = grad_middle + norm_back(
            grad_h * ln_attn_gain[layer], normed_one, factor_one
        )
        attn_rows = scatter_pair(attn_keep, attn_send, [near_hop], places)
        matrix_grads[layer] = (
            attn_rows[:, :width],
            attn_rows[:, width : 2 * width],
            attn_rows[:, 2 * width :],
            out_rows.T,
            up_rows,
            down_rows.T,
        )
        grad_head_all = lax.dynamic_update_slice_in_dim(
            jnp.zeros((H,), F32), grad_head, places.tensor_index * local_heads, 0
        )
        grad_mid_all = jnp.sum(mid_sum, 1)[places.tensor_sources].reshape(-1)
        small_grads[layer] = (
            grad_attn_gain, grad_head_all, jnp.sum(post_sum, 0), jnp.sum(ffn_sum, 0),
            grad_mid_all,
        )
    sizes = [part.shape[0] for part in small_grads[0]]
    vector = jnp.concatenate([part for layer in range(LAYERS) for part in small_grads[layer]])
    count = vector.shape[0]
    vector = jnp.pad(vector, (0, -count % 1024)).reshape(-1, 128)
    vector = sum_everywhere(vector).reshape(-1)
    smalls, start = [], 0
    for layer in range(LAYERS):
        found = []
        for size in sizes:
            found.append(lax.slice_in_dim(vector, start, start + size))
            start += size
        smalls.append(found)
    small = [jnp.stack([smalls[layer][at] for layer in range(LAYERS)]) for at in range(5)]
    stacked = [
        jnp.stack([matrix_grads[layer][at] for layer in range(LAYERS)]) for at in range(6)
    ]
    return (
        stream, grad_stream, small[0], stacked[0], stacked[1], stacked[2], small[1], stacked[3],
        small[2], small[3], stacked[4], small[4], stacked[5],
    )


def solution(mesh):
    rows = P(("dp", "tensor"), None)
    first = P(None, "dp", "tensor")
    second = P(None, "tensor", "dp")
    in_specs = (
        rows, P("dp", None), P(), first, first, first, P(), second, P(), P(), first, P(), second,
        rows,
    )
    out_specs = (
        rows, rows, P(), first, first, first, P(), second, P(), P(), first, P(), second,
    )
    return jax.shard_map(local, mesh=mesh, in_specs=in_specs, out_specs=out_specs, check_vma=False)
```

```python
import functools

import jax
import jax.numpy as jnp
from jax import lax
from jax.experimental import pallas as pl
from jax.experimental.pallas import tpu as pltpu
from jax.sharding import PartitionSpec as P

H = 16
HD = 64
LAYERS = 2
PROMPT = 1024
BLOCK = 512

NORM_EPSILON = 1e-05
MASKED_SCORE = -1e30
F32 = jnp.float32
BF16 = jnp.bfloat16
VMEM_LIMIT = 67_000_000


def tanh_gelu(inputs):
    return (
        0.5
        * inputs
        * (1.0 + jnp.tanh(0.7978845608028654 * (inputs + 0.044715 * inputs * inputs * inputs)))
    )


def normalize(values):
    center = values - jnp.mean(values, -1, keepdims=True)
    factor = lax.rsqrt(jnp.mean(center * center, -1, keepdims=True) + NORM_EPSILON)
    return (center * factor, factor)


def norm_back(grad_norm, normed, factor):
    return factor * (
        grad_norm
        - jnp.mean(grad_norm, -1, keepdims=True)
        - normed * jnp.mean(grad_norm * normed, -1, keepdims=True)
    )


def dot_nn(left, right):
    return lax.dot_general(left, right, (((1,), (0,)), ((), ())), preferred_element_type=F32)


def dot_tn(left, right):
    return lax.dot_general(left, right, (((0,), (0,)), ((), ())), preferred_element_type=F32)


def dot_nt(left, right):
    return lax.dot_general(left, right, (((1,), (1,)), ((), ())), preferred_element_type=F32)


def bit_masks(size):
    masks = []
    while size > 1:
        size //= 2
        masks.append(size)
    return masks


def relative_order(masks):
    order = [0]
    for mask in masks:
        order = order + [mask | other for other in order]
    return order


def swap(array, axis, mask):
    size = lax.axis_size(axis)
    return lax.ppermute(array, axis, [(i, i ^ mask) for i in range(size)])


class Places:
    def __init__(self):
        self.dp_size = lax.axis_size("dp")
        self.tensor_size = lax.axis_size("tensor")
        dp_index = lax.axis_index("dp").astype(jnp.int32)
        self.tensor_index = lax.axis_index("tensor").astype(jnp.int32)
        self.tensor_masks = bit_masks(self.tensor_size)
        masks = bit_masks(self.dp_size)
        self.far_masks = relative_order(masks[:-1])
        self.near_mask = masks[-1]
        self.far_hops = [("dp", mask) for mask in reversed(masks[:-1])]
        dp_order = self.far_masks + [mask | self.near_mask for mask in self.far_masks]
        self.tensor_order = relative_order(self.tensor_masks)
        tensor_inverse = [self.tensor_order.index(i) for i in range(self.tensor_size)]
        self.dp_places = jnp.array(dp_order, jnp.int32) ^ dp_index
        self.tensor_places = jnp.array(self.tensor_order, jnp.int32) ^ self.tensor_index
        spots = jnp.arange(self.tensor_size, dtype=jnp.int32) ^ self.tensor_index
        self.tensor_sources = jnp.array(tensor_inverse, jnp.int32)[spots]


def gather_far(shard, places):
    others = [swap(shard, "dp", mask) for mask in places.far_masks[1:]]
    return jnp.stack([shard] + others)


def gather_near(part, places):
    return [part, swap(part, "dp", places.near_mask)]


def gather_tensor(parts, masks):
    for mask in masks:
        parts = parts + [jax.tree.map(lambda x, m=mask: swap(x, "tensor", m), p) for p in parts]
    return parts


def gather_late_tensor(shard, places):
    pieces = gather_near(gather_far(shard, places), places)
    return gather_tensor([pieces], places.tensor_masks)


def gather_late_near(shard, places):
    parts = gather_tensor([gather_far(shard, places)], places.tensor_masks[:-1])
    pieces = [gather_near(part, places) for part in parts]
    return gather_tensor(pieces, places.tensor_masks[-1:])


def add_low(kept, arrived):
    return (kept.astype(F32) + arrived.astype(F32)).astype(BF16)


def add_halves(kept, arrived):
    half = kept.shape[0] // 2
    return add_low(kept[:half], arrived[:half]), add_low(kept[half:], arrived[half:])


def scatter_rest(kept, arrived, hops):
    for hop in hops:
        if kept.shape[0] == 1:
            kept, arrived = kept[0], arrived[0]
        kept, sent = add_halves(kept, arrived)
        arrived = swap(sent, *hop)
    total = kept.astype(F32) + arrived.astype(F32)
    return total.reshape(total.shape[-2:])


def sum_everywhere(vector):
    for axis in ("tensor", "dp"):
        for mask in reversed(bit_masks(lax.axis_size(axis))):
            vector = vector + swap(vector, axis, mask)
    return vector


def block_rows(place_ref, at, rows):
    return pl.ds(pl.multiple_of(place_ref[at] * rows, rows), rows)


def start_rows(spot, blocks, columns, target, semaphore):
    count, _, rows, _ = blocks.shape
    for at in range(count):
        pltpu.make_async_copy(
            blocks.at[at, spot, :, columns], target.at[at * rows : (at + 1) * rows, :], semaphore
        ).start()


def wait_whole(target, semaphore):
    pltpu.make_async_copy(target, target, semaphore).wait()


def each_rows(total, chunk, body):
    for start in range(0, total, chunk):
        body(pl.ds(start, chunk))


def lanes(values, width):
    return jnp.concatenate([values] * (width // 128), axis=1)


def fold_lanes(values):
    total = values[:, :128]
    for lane in range(128, values.shape[1], 128):
        total = total + values[:, lane : lane + 128]
    return total


def fold_rows(values):
    return jnp.sum(values.reshape(values.shape[0] // 8, 8, values.shape[1]), axis=0)


CHUNK = 16


def ffn_forward_kernel(parts, last, place_ref, *refs):
    refs = list(refs)

    def take(count):
        taken = refs[:count]
        del refs[:count]
        return taken

    (stream_ref,) = take(1)
    a_refs = take(parts)
    (matrix_ref,) = take(1)
    post_ref, ffn_ref, mid_ref, next_ref = take(4)
    out_ref, middle_ref, next_stream_ref, h_ffn_ref, mean_ref, factor_ref = take(6)
    pre_ref, h_mid_ref = take(2)
    h_next_ref = None if last else take(1)[0]
    w_up, w_out, w_down, active, pre_buf, mid_buf, sums, squares = take(8)
    up_sem, out_sem, down_sem, pre_sem, mid_sem = take(5)
    rows, depth = stream_ref.shape
    wide = w_up.shape[2]
    narrow = w_out.shape[2]
    hidden = parts * wide

    up_columns, down_columns = pl.ds(0, wide), pl.ds(wide, wide)
    out_columns = pl.ds(2 * wide, narrow)
    for at in range(parts):
        start_rows(place_ref[at], matrix_ref, out_columns, w_out.at[at], out_sem)
    for at in range(parts):
        start_rows(place_ref[at], matrix_ref, up_columns, w_up.at[at], up_sem.at[at])
    for at in range(parts):
        start_rows(place_ref[at], matrix_ref, down_columns, w_down.at[at], down_sem.at[at])
    wait_whole(w_out, out_sem)
    out_ref[...] = sum(dot_nt(a_refs[at][...], w_out[at]) for at in range(parts))

    def middle_rows(here):
        normed, _ = normalize(out_ref[here, :])
        middle = stream_ref[here, :] + normed * post_ref[...]
        middle_ref[here, :] = middle
        normed, _ = normalize(middle)
        h_ffn_ref[here, :] = (normed * ffn_ref[...]).astype(BF16)

    each_rows(rows, CHUNK, middle_rows)
    sums[...] = jnp.zeros_like(sums)
    squares[...] = jnp.zeros_like(squares)

    def write_pre(at):
        return pltpu.make_async_copy(pre_buf.at[at % 2], pre_ref.at[at], pre_sem.at[at % 2])

    def write_mid(at):
        return pltpu.make_async_copy(mid_buf.at[at % 2], h_mid_ref.at[at], mid_sem.at[at % 2])

    wait_whole(w_up.at[0], up_sem.at[0])
    pre_buf[0] = dot_nn(h_ffn_ref[...], w_up[0])
    for at in range(parts):
        write_pre(at).start()
        if at + 1 < parts:
            wait_whole(w_up.at[at + 1], up_sem.at[at + 1])
            if at >= 1:
                write_pre(at - 1).wait()
            pre_buf[(at + 1) % 2] = dot_nn(h_ffn_ref[...], w_up[at + 1])

        def active_rows(here, at=at):
            value = tanh_gelu(pre_buf[at % 2, here, :])
            active[at, here, :] = value
            sums[here, :] += fold_lanes(value)
            squares[here, :] += fold_lanes(value * value)

        each_rows(rows, CHUNK, active_rows)
    mean = jnp.sum(sums[...], axis=1, keepdims=True) / hidden
    spread = jnp.sum(squares[...], axis=1, keepdims=True) / hidden - mean * mean
    mean_ref[...] = jnp.broadcast_to(mean, mean_ref.shape)
    factor_ref[...] = jnp.broadcast_to(lax.rsqrt(spread + NORM_EPSILON), factor_ref.shape)

    def mid_part(at):
        def mid_rows(here):
            normed = active[at, here, :] - lanes(mean_ref[here, :], wide)
            normed = normed * lanes(factor_ref[here, :], wide)
            mid_buf[at % 2, here, :] = (normed * mid_ref[at : at + 1, :]).astype(BF16)

        each_rows(rows, CHUNK, mid_rows)

    mid_part(0)
    for at in range(parts):
        write_mid(at).start()
        wait_whole(w_down.at[at], down_sem.at[at])
        if 1 <= at < parts - 1:
            write_mid(at - 1).wait()
        product = dot_nt(mid_buf[at % 2], w_down[at])
        if at == 0:
            next_stream_ref[...] = middle_ref[...] + product
        else:
            next_stream_ref[...] += product
        if at + 1 < parts:
            mid_part(at + 1)
    if not last:

        def next_rows(here):
            normed, _ = normalize(next_stream_ref[here, :])
            h_next_ref[here, :] = (normed * next_ref[...]).astype(BF16)

        each_rows(rows, CHUNK, next_rows)
    for at in range(max(parts - 2, 0), parts):
        write_pre(at).wait()
        write_mid(at).wait()


def ffn_forward(places, stream, a_parts, matrices, post, ffn, mid, following, last):
    rows, depth = stream.shape
    parts, wide = mid.shape
    narrow = a_parts[0].shape[1]
    vmem = pl.BlockSpec(memory_space=pltpu.VMEM)
    hbm = pl.BlockSpec(memory_space=pl.ANY)
    full = jax.ShapeDtypeStruct((rows, depth), F32)
    low = jax.ShapeDtypeStruct((rows, depth), BF16)
    stat = jax.ShapeDtypeStruct((rows, 128), F32)
    outs = [full, full, full, low, stat, stat] + [
        jax.ShapeDtypeStruct((parts, rows, wide), F32),
        jax.ShapeDtypeStruct((parts, rows, wide), BF16),
    ]
    out_specs = [vmem] * 6 + [hbm] * 2
    if not last:
        outs, out_specs = outs + [low], out_specs + [vmem]
    dma = pltpu.SemaphoreType.DMA
    return pl.pallas_call(
        functools.partial(ffn_forward_kernel, parts, last),
        in_specs=[pl.BlockSpec(memory_space=pltpu.SMEM)]
        + [vmem] * (1 + parts)
        + [hbm]
        + [vmem] * 4,
        out_specs=out_specs,
        out_shape=outs,
        scratch_shapes=[
            pltpu.VMEM((parts, depth, wide), BF16),
            pltpu.VMEM((parts, depth, narrow), BF16),
            pltpu.VMEM((parts, depth, wide), BF16),
            pltpu.VMEM((parts, rows, wide), F32),
            pltpu.VMEM((2, rows, wide), F32),
            pltpu.VMEM((2, rows, wide), BF16),
            pltpu.VMEM((rows, 128), F32),
            pltpu.VMEM((rows, 128), F32),
            dma((parts,)),
            dma,
            dma((parts,)),
            dma((2,)),
            dma((2,)),
        ],
        compiler_params=pltpu.CompilerParams(vmem_limit_bytes=VMEM_LIMIT),
        cost_estimate=pl.CostEstimate(
            flops=2 * rows * depth * parts * (2 * wide + narrow),
            bytes_accessed=40 << 20,
            transcendentals=rows * parts * wide,
        ),
        name="ffn_forward",
    )(
        places.tensor_places,
        stream,
        *a_parts,
        matrices,
        post[None],
        ffn[None],
        mid,
        following[None],
    )


def ffn_backward_kernel(parts, place_ref, *refs):
    refs = list(refs)

    def take(count):
        taken = refs[:count]
        del refs[:count]
        return taken

    grad_ref, out_ref, middle_ref, mean_ref, factor_ref, pre_ref = take(6)
    (matrix_ref,) = take(1)
    post_ref, ffn_ref, mid_ref, scale_ref = take(4)
    low_ref, grad_middle_ref, grad_out_ref = take(3)
    dout_refs = take(parts)
    grad_pre_ref, mid_sum_ref, ffn_sum_ref, post_sum_ref = take(4)
    weights, w_out, grad_normed, normed_four, slope, pre_buf, product, low_buf = take(8)
    first, second = take(2)
    weight_sem, out_sem, pre_sem, low_sem = take(4)
    rows, depth = grad_ref.shape
    wide = weights.shape[2]
    narrow = w_out.shape[2]
    hidden = parts * wide

    def read_pre(at):
        return pltpu.make_async_copy(pre_ref.at[at], pre_buf.at[at % 2], pre_sem.at[at % 2])

    up_columns, down_columns = pl.ds(0, wide), pl.ds(wide, wide)
    out_columns = pl.ds(2 * wide, narrow)
    for at in range(parts):
        start_rows(place_ref[at], matrix_ref, down_columns, weights.at[at], weight_sem.at[at])
        if at < 2:
            read_pre(at).start()
    for at in range(parts):
        start_rows(place_ref[at], matrix_ref, out_columns, w_out.at[at], out_sem)
    low_ref[...] = grad_ref[...].astype(BF16)
    first[...] = jnp.zeros_like(first)
    second[...] = jnp.zeros_like(second)
    mid_sum_ref[...] = jnp.zeros_like(mid_sum_ref)
    ffn_sum_ref[...] = jnp.zeros_like(ffn_sum_ref)
    post_sum_ref[...] = jnp.zeros_like(post_sum_ref)
    wait_whole(weights.at[0], weight_sem.at[0])
    product[0] = dot_nn(low_ref[...], weights[0])
    for at in range(parts):
        start_rows(place_ref[at], matrix_ref, up_columns, weights.at[at], weight_sem.at[at])
        read_pre(at).wait()
        if at + 1 < parts:
            wait_whole(weights.at[at + 1], weight_sem.at[at + 1])
            product[(at + 1) % 2] = dot_nn(low_ref[...], weights[at + 1])

        def hidden_rows(here, at=at):
            value = pre_buf[at % 2, here, :]
            squared = value * value
            bend = jnp.tanh(value * (0.7978845608028654 + 0.035677408136300125 * squared))
            raised = 0.5 + 0.5 * bend
            normed = value * raised - lanes(mean_ref[here, :], wide)
            normed = normed * lanes(factor_ref[here, :], wide)
            steep = value * (0.7978845608028654 + 0.10703222440890037 * squared)
            slope[at, here, :] = raised + 0.5 * steep * (1.0 - bend * bend)
            normed_four[at, here, :] = normed.astype(BF16)
            grad = product[at % 2, here, :]
            mid_sum_ref[at] += fold_rows(grad * normed)
            grad = grad * mid_ref[at : at + 1, :]
            grad_normed[at, here, :] = grad
            first[here, :] += fold_lanes(grad)
            second[here, :] += fold_lanes(grad * normed)

        each_rows(rows, CHUNK, hidden_rows)
        if at + 2 < parts:
            read_pre(at + 2).start()
    first[...] = jnp.broadcast_to(
        jnp.sum(first[...], axis=1, keepdims=True) / hidden, first.shape
    )
    second[...] = jnp.broadcast_to(
        jnp.sum(second[...], axis=1, keepdims=True) / hidden, second.shape
    )

    def write_low(at):
        return pltpu.make_async_copy(low_buf.at[at % 2], grad_pre_ref.at[at], low_sem.at[at % 2])

    def low_part(at):
        def pre_rows(here):
            normed = normed_four[at, here, :].astype(F32)
            grad = grad_normed[at, here, :] - lanes(first[here, :], wide)
            grad = grad - normed * lanes(second[here, :], wide)
            grad = grad * slope[at, here, :] * lanes(factor_ref[here, :], wide)
            low_buf[at % 2, here, :] = grad.astype(BF16)

        each_rows(rows, CHUNK, pre_rows)

    low_part(0)
    for at in range(parts):
        write_low(at).start()
        wait_whole(weights.at[at], weight_sem.at[at])
        if 1 <= at < parts - 1:
            write_low(at - 1).wait()
        part = dot_nt(low_buf[at % 2], weights[at])
        if at == 0:
            product[0] = part
        else:
            product[0] += part
        if at + 1 < parts:
            low_part(at + 1)

    def middle_rows(here):
        grad = product[0, here, :]
        normed, factor = normalize(middle_ref[here, :])
        ffn_sum_ref[...] += fold_rows(grad * normed)
        grad = grad_ref[here, :] + norm_back(grad * ffn_ref[...], normed, factor)
        grad_middle_ref[here, :] = grad
        normed, factor = normalize(out_ref[here, :])
        post_sum_ref[...] += fold_rows(grad * normed)
        grad_out_ref[here, :] = norm_back(grad * post_ref[...], normed, factor).astype(BF16)

    each_rows(rows, CHUNK, middle_rows)
    wait_whole(w_out, out_sem)
    for at in range(parts):
        grad = dot_nn(grad_out_ref[...], w_out[at])
        dout_refs[at][...] = (grad * scale_ref[at : at + 1, :]).astype(BF16)
    for at in range(max(parts - 2, 0), parts):
        write_low(at).wait()


def ffn_backward(places, grad, out, middle, mean, factor, pre, matrices, post, ffn, mid, scale):
    rows, depth = grad.shape
    parts, wide = mid.shape
    narrow = scale.shape[1]
    vmem = pl.BlockSpec(memory_space=pltpu.VMEM)
    hbm = pl.BlockSpec(memory_space=pl.ANY)
    low = jax.ShapeDtypeStruct((rows, depth), BF16)
    sums = jax.ShapeDtypeStruct((8, depth), F32)
    dma = pltpu.SemaphoreType.DMA
    return pl.pallas_call(
        functools.partial(ffn_backward_kernel, parts),
        in_specs=[pl.BlockSpec(memory_space=pltpu.SMEM)]
        + [vmem] * 5
        + [hbm] * 2
        + [vmem] * 4,
        out_specs=[vmem] * (3 + parts) + [hbm] + [vmem] * 3,
        out_shape=[low, jax.ShapeDtypeStruct((rows, depth), F32), low]
        + [jax.ShapeDtypeStruct((rows, narrow), BF16)] * parts
        + [
            jax.ShapeDtypeStruct((parts, rows, wide), BF16),
            jax.ShapeDtypeStruct((parts, 8, wide), F32),
            sums,
            sums,
        ],
        scratch_shapes=[
            pltpu.VMEM((parts, depth, wide), BF16),
            pltpu.VMEM((parts, depth, narrow), BF16),
            pltpu.VMEM((parts, rows, wide), F32),
            pltpu.VMEM((parts, rows, wide), BF16),
            pltpu.VMEM((parts, rows, wide), F32),
            pltpu.VMEM((2, rows, wide), F32),
            pltpu.VMEM((2, rows, depth), F32),
            pltpu.VMEM((2, rows, wide), BF16),
            pltpu.VMEM((rows, 128), F32),
            pltpu.VMEM((rows, 128), F32),
            dma((parts,)),
            dma,
            dma((2,)),
            dma((2,)),
        ],
        compiler_params=pltpu.CompilerParams(vmem_limit_bytes=VMEM_LIMIT),
        cost_estimate=pl.CostEstimate(
            flops=2 * rows * depth * parts * (2 * wide + narrow),
            bytes_accessed=44 << 20,
            transcendentals=rows * parts * wide,
        ),
        name="ffn_backward",
    )(
        places.tensor_places,
        grad,
        out,
        middle,
        mean,
        factor,
        pre,
        matrices,
        post[None],
        ffn[None],
        mid,
        scale,
    )


def turned(place_ref, source, plain, target, rows):
    plain[...] = source[...].astype(BF16).astype(F32).T.astype(BF16)
    for at in range(target.shape[0] // rows):
        target[at * rows : (at + 1) * rows, :] = plain[block_rows(place_ref, at, rows), :]


def up_grads_kernel(parts, place_ref, *refs):
    h_ffn_ref, grad_out_ref, grad_pre_ref, a_ref, keep_ref, send_ref = refs[:6]
    h_turned, out_turned, h_plain, out_plain = refs[6:]
    step = pl.program_id(0)
    count, rows = keep_ref.shape[2:4]
    wide = grad_pre_ref.shape[2]

    @pl.when(step == 0)
    def _():
        turned(place_ref, h_ffn_ref, h_plain, h_turned, rows)
        turned(place_ref, grad_out_ref, out_plain, out_turned, rows)

    def fill(target):
        shape = (2, count, rows, -1)
        grad = dot_nn(h_turned[...], grad_pre_ref[0]).astype(BF16)
        target[0, :, :, :, :wide] = grad.reshape(shape)
        grad = dot_nn(out_turned[...], a_ref[0]).astype(BF16)
        target[0, :, :, :, wide:] = grad.reshape(shape)

    @pl.when(step < parts // 2)
    def _():
        fill(keep_ref)

    @pl.when(step >= parts // 2)
    def _():
        fill(send_ref)


def down_grads_kernel(parts, place_ref, *refs):
    grad_ref, h_mid_ref, keep_ref, send_ref, low_turned, low_plain = refs
    step = pl.program_id(0)
    count, rows = keep_ref.shape[2:4]

    @pl.when(step == 0)
    def _():
        turned(place_ref, grad_ref, low_plain, low_turned, rows)

    def fill(target):
        grad = dot_nn(low_turned[...], h_mid_ref[0]).astype(BF16)
        target[:, 0] = grad.reshape(2, count, rows, -1)

    @pl.when(step < parts // 2)
    def _():
        fill(keep_ref)

    @pl.when(step >= parts // 2)
    def _():
        fill(send_ref)


def split_grads(kernel, name, places, turns, sides, block, outside, at_part):
    parts, rows, _ = sides[0].shape
    depth = turns[0].shape[1]
    half = parts // 2
    columns = sum(side.shape[2] for side in sides)
    whole = pl.BlockSpec((rows, depth), lambda i, place: (0, 0))
    return pl.pallas_call(
        functools.partial(kernel, parts),
        grid_spec=pltpu.PrefetchScalarGridSpec(
            num_scalar_prefetch=1,
            grid=(parts,),
            in_specs=[whole] * len(turns)
            + [pl.BlockSpec((1,) + side.shape[1:], lambda i, place: (i, 0, 0)) for side in sides],
            out_specs=[
                pl.BlockSpec(block, lambda i, place: at_part(jnp.minimum(i, half - 1))),
                pl.BlockSpec(block, lambda i, place: at_part(jnp.maximum(i - half, 0))),
            ],
            scratch_shapes=[pltpu.VMEM((depth, rows), BF16)] * (2 * len(turns)),
        ),
        out_shape=[jax.ShapeDtypeStruct(outside, BF16)] * 2,
        compiler_params=pltpu.CompilerParams(vmem_limit_bytes=VMEM_LIMIT),
        cost_estimate=pl.CostEstimate(
            flops=2 * rows * depth * parts * columns,
            bytes_accessed=16 << 20,
            transcendentals=0,
        ),
        name=name,
    )(places.dp_places, *turns, *sides)


def up_grads(places, h_ffn, grad_out, grad_pre, a_parts):
    a_all = jnp.stack(a_parts)
    half = len(a_parts) // 2
    count = places.dp_size // 2
    tail = (count, h_ffn.shape[1] // places.dp_size, grad_pre.shape[2] + a_all.shape[2])
    return split_grads(
        up_grads_kernel, "up_grads", places, [h_ffn, grad_out], [grad_pre, a_all],
        (1, 2) + tail, (half, 2) + tail, lambda part: (part, 0, 0, 0, 0),
    )


def down_grads(places, grad, h_mid):
    half = h_mid.shape[0] // 2
    count = places.dp_size // 2
    tail = (count, grad.shape[1] // places.dp_size, h_mid.shape[2])
    return split_grads(
        down_grads_kernel, "down_grads", places, [grad], [h_mid],
        (2, 1) + tail, (2, half) + tail, lambda part: (0, part, 0, 0, 0),
    )


def whole_grads_kernel(parts, place_ref, *refs):
    del place_ref
    low_ref, h_ffn_ref, grad_out_ref, grad_pre_ref, h_mid_ref, a_ref, matrix_ref = refs[:7]
    low_turned, h_turned, out_turned = refs[7:]
    wide = h_mid_ref.shape[2]
    shape = matrix_ref.shape[:3] + (-1,)

    @pl.when(pl.program_id(0) == 0)
    def _():
        for source, target in (
            (low_ref, low_turned), (h_ffn_ref, h_turned), (grad_out_ref, out_turned)
        ):
            target[...] = source[...].astype(F32).T.astype(BF16)

    grad = dot_nn(h_turned[...], grad_pre_ref[0]).astype(BF16)
    matrix_ref[:, :, :, :wide] = grad.reshape(shape)
    grad = dot_nn(low_turned[...], h_mid_ref[0]).astype(BF16)
    matrix_ref[:, :, :, wide : 2 * wide] = grad.reshape(shape)
    grad = dot_nn(out_turned[...], a_ref[0]).astype(BF16)
    matrix_ref[:, :, :, 2 * wide :] = grad.reshape(shape)


def whole_grads(places, low, h_ffn, grad_out, grad_pre, h_mid, a_parts):
    rows, depth = low.shape
    parts, _, wide = h_mid.shape
    narrow = a_parts[0].shape[1]
    block = depth // places.dp_size
    columns = 2 * wide + narrow
    whole = pl.BlockSpec((rows, depth), lambda i, place: (0, 0))
    each = pl.BlockSpec((1, rows, wide), lambda i, place: (i, 0, 0))
    return pl.pallas_call(
        functools.partial(whole_grads_kernel, parts),
        grid_spec=pltpu.PrefetchScalarGridSpec(
            num_scalar_prefetch=1,
            grid=(parts,),
            in_specs=[whole] * 3
            + [each] * 2
            + [pl.BlockSpec((1, rows, narrow), lambda i, place: (i, 0, 0))],
            out_specs=pl.BlockSpec(
                (places.dp_size, 1, block, columns), lambda i, place: (0, place[i], 0, 0)
            ),
            scratch_shapes=[pltpu.VMEM((depth, rows), BF16)] * 3,
        ),
        out_shape=jax.ShapeDtypeStruct((places.dp_size, parts, block, columns), BF16),
        compiler_params=pltpu.CompilerParams(vmem_limit_bytes=VMEM_LIMIT),
        cost_estimate=pl.CostEstimate(
            flops=2 * rows * depth * parts * columns,
            bytes_accessed=30 << 20,
            transcendentals=0,
        ),
        name="whole_grads",
    )(places.tensor_places, low, h_ffn, grad_out, grad_pre, h_mid, jnp.stack(a_parts))


def attn_grads_kernel(parts, place_ref, *refs):
    h_refs = refs[:parts]
    packed_ref, keep_ref, send_ref, total = refs[parts:]
    count, rows, _ = keep_ref.shape
    tokens = packed_ref.shape[0] // parts
    for part in range(parts):
        flipped = h_refs[part][...].astype(F32).T.astype(BF16)
        grad = dot_nn(flipped, packed_ref[part * tokens : (part + 1) * tokens, :])
        if part == 0:
            total[...] = grad
        else:
            total[...] += grad
    for at in range(count):
        keep_ref[at] = total[block_rows(place_ref, at, rows), :].astype(BF16)
        send_ref[at] = total[block_rows(place_ref, count + at, rows), :].astype(BF16)


def attn_grads(places, h_parts, packed):
    parts = len(h_parts)
    tokens, depth = h_parts[0].shape
    columns = packed.shape[1]
    count = places.dp_size // 2
    block = depth // places.dp_size
    vmem = pl.BlockSpec(memory_space=pltpu.VMEM)
    return pl.pallas_call(
        functools.partial(attn_grads_kernel, parts),
        in_specs=[pl.BlockSpec(memory_space=pltpu.SMEM)] + [vmem] * (parts + 1),
        out_specs=[vmem] * 2,
        out_shape=[jax.ShapeDtypeStruct((count, block, columns), BF16)] * 2,
        scratch_shapes=[
            pltpu.VMEM((depth, columns), F32),
        ],
        compiler_params=pltpu.CompilerParams(vmem_limit_bytes=VMEM_LIMIT),
        cost_estimate=pl.CostEstimate(
            flops=2 * tokens * parts * depth * columns,
            bytes_accessed=8 << 20,
            transcendentals=0,
        ),
        name="attn_grads",
    )(places.dp_places, *h_parts, packed)


def half_mask(shape, head):
    lane = lax.broadcasted_iota(jnp.int32, shape, len(shape) - 1)
    return (lane // HD) == (head % 2)


def place_rows(place_ref, pieces, target):
    for half, piece in enumerate(pieces):
        count, rows, _ = piece.shape
        for at in range(count):
            target[block_rows(place_ref, half * count + at, rows), :] = piece[at]


def forward_kernel(block_ref, place_ref, *refs):
    parts = block_ref.shape[0]
    rows_refs = refs[:parts]
    pieces = refs[parts : parts + 2]
    column_ref, row_ref, scale_ref = refs[parts + 2 : parts + 5]
    query_ref, key_ref, value_ref, mixture_ref, logsum_ref = refs[parts + 5 : parts + 10]
    scaled_refs = refs[parts + 10 : -2]
    score_ref, weight_ref = refs[-2:]
    width = query_ref.shape[1]
    length = query_ref.shape[0]
    rows = length // parts

    place_rows(place_ref, pieces, weight_ref)
    for part in range(parts):
        at = pl.ds(pl.multiple_of(block_ref[part] * rows, rows), rows)
        packed = dot_nn(rows_refs[part][...], weight_ref[...])
        query_ref[at, :] = packed[:, :width].astype(BF16) * jnp.asarray(0.125, BF16)
        key_ref[at, :] = packed[:, width : 2 * width].astype(BF16)
        value_ref[at, :] = packed[:, 2 * width :].astype(BF16)

    for query_block in range(length // BLOCK):
        here = pl.ds(query_block * BLOCK, BLOCK)

        def one_head(head, logsums, query_block=query_block, here=here):
            lanes = pl.ds(pl.multiple_of((head // 2) * 128, 128), 128)
            own = half_mask((BLOCK, 128), head)
            query = jnp.where(own, query_ref[here, lanes], jnp.asarray(0, BF16))
            highest = jnp.full((BLOCK, 128), MASKED_SCORE, F32)
            for key_block in range(query_block + 1):
                there = pl.ds(key_block * BLOCK, BLOCK)
                scores = dot_nt(query, key_ref[there, lanes])
                if key_block == query_block or key_block * BLOCK >= PROMPT:
                    first = lax.broadcasted_iota(jnp.int32, (BLOCK, BLOCK), 0)
                    second = lax.broadcasted_iota(jnp.int32, (BLOCK, BLOCK), 1)
                    seen = None
                    if key_block == query_block:
                        seen = second <= first
                    if key_block * BLOCK >= PROMPT:
                        query_at = pl.ds(query_block * BLOCK - PROMPT, BLOCK)
                        key_at = pl.ds(key_block * BLOCK - PROMPT, BLOCK)
                        same = column_ref[query_at, :] == row_ref[:, key_at]
                        seen = same if seen is None else seen & same
                    scores = jnp.where(seen, scores, MASKED_SCORE)
                score_ref[:, there] = scores
                for lane in range(0, BLOCK, 128):
                    highest = jnp.maximum(highest, scores[:, lane : lane + 128])
            top = jnp.max(highest, axis=1, keepdims=True)
            total = jnp.zeros((BLOCK, 128), F32)
            mixed = jnp.zeros((BLOCK, 128), F32)
            for key_block in range(query_block + 1):
                there = pl.ds(key_block * BLOCK, BLOCK)
                weights = jnp.exp(score_ref[:, there] - top)
                for lane in range(0, BLOCK, 128):
                    total = total + weights[:, lane : lane + 128]
                mixed = mixed + dot_nn(weights.astype(BF16), value_ref[there, lanes])
            denominator = jnp.sum(total, axis=1, keepdims=True)
            mixed = mixed / denominator
            mixture_ref[here, lanes] = jnp.where(own, mixed, mixture_ref[here, lanes])
            lane = lax.broadcasted_iota(jnp.int32, (BLOCK, 128), 1)
            return jnp.where(lane == head, top + jnp.log(denominator), logsums)

        logsums = lax.fori_loop(0, width // HD, one_head, jnp.zeros((BLOCK, 128), F32))
        logsum_ref[:, here] = logsums.T[: logsum_ref.shape[0], :]

    for part in range(parts):
        at = pl.ds(pl.multiple_of(block_ref[part] * rows, rows), rows)
        scaled_refs[part][...] = (mixture_ref[at, :] * scale_ref[...]).astype(BF16)


def attend_forward(places, rows, pieces, seg_column, seg_row, scale):
    parts = len(rows)
    length = parts * rows[0].shape[0]
    width = pieces[0].shape[2] // 3
    depth = rows[0].shape[1]
    heads = width // HD
    pairs = length * length * 5 // 8
    whole = pl.BlockSpec(memory_space=pltpu.VMEM)
    return pl.pallas_call(
        forward_kernel,
        in_specs=[pl.BlockSpec(memory_space=pltpu.SMEM)] * 2 + [whole] * (parts + 5),
        out_specs=[whole] * (5 + parts),
        out_shape=[jax.ShapeDtypeStruct((length, width), BF16)] * 3
        + [
            jax.ShapeDtypeStruct((length, width), F32),
            jax.ShapeDtypeStruct((8, length), F32),
        ]
        + [jax.ShapeDtypeStruct((length // parts, width), BF16)] * parts,
        scratch_shapes=[
            pltpu.VMEM((BLOCK, length), F32),
            pltpu.VMEM((depth, 3 * width), BF16),
        ],
        compiler_params=pltpu.CompilerParams(vmem_limit_bytes=VMEM_LIMIT),
        cost_estimate=pl.CostEstimate(
            flops=2 * length * depth * 3 * width + heads * pairs * 4 * 256,
            bytes_accessed=20 << 20,
            transcendentals=heads * pairs,
        ),
        name="attend_forward",
    )(places.tensor_places, places.dp_places, *rows, *pieces, seg_column, seg_row, scale)


def backward_kernel(block_ref, place_ref, open_ref, edge_ref, *refs):
    parts = block_ref.shape[0]
    grad_refs = refs[:parts]
    query_ref, key_ref, value_ref, mixture_ref, logsum_ref = refs[parts : parts + 5]
    column_ref, row_ref = refs[parts + 5 : parts + 7]
    pieces = refs[parts + 7 : parts + 9]
    packed_ref, inner_sum_ref, keep_ref, send_ref = refs[parts + 9 : parts + 13]
    dout_ref, inner_ref, dq_ref, dk_ref, dv_ref, weight_ref = refs[parts + 13 :]
    length, width = query_ref.shape
    rows = length // parts

    for part in range(parts):
        at = pl.ds(pl.multiple_of(block_ref[part] * rows, rows), rows)
        dout_ref[at, :] = grad_refs[part][...]
    picks = lax.broadcasted_iota(jnp.int32, (8, width), 1) // HD == lax.broadcasted_iota(
        jnp.int32, (8, width), 0
    )
    picks = jnp.where(picks, 1.0, 0.0)
    inner_sum = jnp.zeros((8, 128), F32)
    for part in range(length // BLOCK):
        at = pl.ds(part * BLOCK, BLOCK)
        product = dout_ref[at, :].astype(F32) * mixture_ref[at, :]
        inner = lax.dot_general(
            picks,
            product,
            (((1,), (1,)), ((), ())),
            precision=lax.Precision.HIGHEST,
            preferred_element_type=F32,
        )
        inner_ref[:, at] = inner
        for lane in range(0, BLOCK, 128):
            inner_sum = inner_sum + inner[:, lane : lane + 128]
    inner_sum_ref[...] = inner_sum
    dq_ref[...] = jnp.zeros_like(dq_ref)
    dk_ref[...] = jnp.zeros_like(dk_ref)
    dv_ref[...] = jnp.zeros_like(dv_ref)

    def one_pair(head, key_block, query_block, edge):
        lanes = pl.ds(pl.multiple_of((head // 2) * 128, 128), 128)
        there = pl.ds(pl.multiple_of(key_block * BLOCK, BLOCK), BLOCK)
        here = pl.ds(pl.multiple_of(query_block * BLOCK, BLOCK), BLOCK)
        own = half_mask((BLOCK, 128), head)
        none = jnp.asarray(0, BF16)
        query = jnp.where(own, query_ref[here, lanes], none)
        dout = jnp.where(own, dout_ref[here, lanes], none)
        key = key_ref[there, lanes]
        scores = dot_nt(key, query)
        weights = jnp.exp(scores - logsum_ref[pl.ds(head, 1), here])
        if edge:
            key_at = key_block * BLOCK + lax.broadcasted_iota(jnp.int32, (BLOCK, BLOCK), 0)
            query_at = query_block * BLOCK + lax.broadcasted_iota(jnp.int32, (BLOCK, BLOCK), 1)
            same = column_ref[there, :] == row_ref[:, here]
            weights = jnp.where((key_at <= query_at) & same, weights, 0.0)
        dv_ref[there, lanes] += dot_nn(weights.astype(BF16), dout)
        grad = dot_nt(value_ref[there, lanes], dout)
        grad = (weights * (grad - inner_ref[pl.ds(head, 1), here])).astype(BF16)
        dk_ref[there, lanes] += dot_nn(grad, query)
        dq_ref[here, lanes] += dot_tn(grad, jnp.where(own, key, none))

    def one_head(head, carry):
        def open_pair(at, inside):
            one_pair(head, open_ref[2 * at], open_ref[2 * at + 1], False)
            return inside

        def edge_pair(at, inside):
            one_pair(head, edge_ref[2 * at], edge_ref[2 * at + 1], True)
            return inside

        lax.fori_loop(0, open_ref.shape[0] // 2, open_pair, 0)
        lax.fori_loop(0, edge_ref.shape[0] // 2, edge_pair, 0)
        return carry

    lax.fori_loop(0, width // HD, one_head, 0)
    for part in range(parts):
        at = pl.ds(pl.multiple_of(block_ref[part] * rows, rows), rows)
        to = pl.ds(part * rows, rows)
        packed_ref[to, :width] = (dq_ref[at, :] * 0.125).astype(BF16)
        packed_ref[to, width : 2 * width] = dk_ref[at, :].astype(BF16)
        packed_ref[to, 2 * width :] = dv_ref[at, :].astype(BF16)
    place_rows(place_ref, pieces, weight_ref)
    for part in range(parts):
        grad = dot_nt(packed_ref[part * rows : (part + 1) * rows, :], weight_ref[...])
        half = parts // 2
        target = keep_ref if part < half else send_ref
        target[part % half] = grad.astype(BF16)


def attend_backward(
    places, grads, queries, keys, values, mixture, logsum, seg_column, seg_row, pieces
):
    parts = len(grads)
    length, width = queries.shape
    heads = width // HD
    depth = pieces[0].shape[0] * pieces[0].shape[1] * 2
    opened, edges = [], []
    for query_block in range(length // BLOCK):
        for key_block in range(query_block + 1):
            if key_block == query_block or key_block * BLOCK >= PROMPT:
                edges += [key_block, query_block]
            else:
                opened += [key_block, query_block]
    whole = pl.BlockSpec(memory_space=pltpu.VMEM)
    scalars = pl.BlockSpec(memory_space=pltpu.SMEM)
    pairs = length * length * 5 // 8
    return pl.pallas_call(
        backward_kernel,
        in_specs=[scalars] * 4 + [whole] * (parts + 9),
        out_specs=[whole] * 4,
        out_shape=[
            jax.ShapeDtypeStruct((length, 3 * width), BF16),
            jax.ShapeDtypeStruct((8, 128), F32),
            jax.ShapeDtypeStruct((parts // 2, length // parts, depth), BF16),
            jax.ShapeDtypeStruct((parts // 2, length // parts, depth), BF16),
        ],
        scratch_shapes=[
            pltpu.VMEM((length, width), BF16),
            pltpu.VMEM((8, length), F32),
            pltpu.VMEM((length, width), F32),
            pltpu.VMEM((length, width), F32),
            pltpu.VMEM((length, width), F32),
            pltpu.VMEM((depth, 3 * width), BF16),
        ],
        compiler_params=pltpu.CompilerParams(vmem_limit_bytes=VMEM_LIMIT),
        cost_estimate=pl.CostEstimate(
            flops=heads * pairs * 10 * 256 + 2 * length * depth * 3 * width,
            bytes_accessed=16 << 20,
            transcendentals=heads * pairs,
        ),
        name="attend_backward",
    )(
        places.tensor_places,
        places.dp_places,
        jnp.array(opened, jnp.int32),
        jnp.array(edges, jnp.int32),
        *grads,
        queries,
        keys,
        values,
        mixture,
        logsum,
        seg_column,
        seg_row,
        *pieces,
    )


def local(
    layer_input,
    segment_ids,
    ln_attn_gain,
    w_query,
    w_key,
    w_value,
    head_scale,
    w_out,
    ln_post_gain,
    ln_ffn_gain,
    w_up,
    ln_mid_gain,
    w_down,
    out_cotangent,
):
    places = Places()
    tensor_size = places.tensor_size
    tensor_order = places.tensor_order
    tensor_masks = places.tensor_masks
    local_heads = H // tensor_size
    width = local_heads * HD
    parts = range(tensor_size)

    seg_row = segment_ids[0][None, :]
    seg_column = segment_ids[0][:, None]
    prompt = jnp.zeros((PROMPT,), jnp.int32)
    long_row = jnp.concatenate([prompt, segment_ids[0]])[None, :]
    long_column = jnp.concatenate([prompt, segment_ids[0]])[:, None]

    attn_shards, matrix_set = [], []
    for layer in range(LAYERS):
        packed = jnp.concatenate([w_query[layer], w_key[layer], w_value[layer]], axis=1)
        attn_shards.append(packed.astype(BF16))
        packed = jnp.concatenate([w_up[layer], w_down[layer].T, w_out[layer].T], axis=1)
        packed = packed.astype(BF16)
        whole = lax.all_gather(packed, ("dp", "tensor"), axis=0, tiled=False)
        matrix_set.append(whole.reshape(places.dp_size, tensor_size, *packed.shape))
    attn_set = [gather_near(gather_far(attn_shards[0], places), places)]

    def exchange(blocks):
        return [
            block if at == 0 else swap(block, "tensor", tensor_order[at])
            for at, block in enumerate(blocks)
        ]

    stream = layer_input
    normed_one, _ = normalize(stream)
    h_attn = (normed_one * ln_attn_gain[0]).astype(BF16)
    saved = []
    for layer in range(LAYERS):
        last = layer == LAYERS - 1
        if layer > 0:
            shard, _ = lax.optimization_barrier((attn_shards[layer], logsum))
            attn_set.append(gather_near(gather_far(shard, places), places))
        h_parts = gather_tensor([h_attn], tensor_masks)
        scale_all = head_scale[layer].reshape(tensor_size, local_heads)
        scale_rel = jnp.repeat(scale_all[places.tensor_places], HD, axis=1)
        queries, keys, values, mixture, logsum, *a_parts = attend_forward(
            places, h_parts, attn_set[layer], seg_column, seg_row, scale_rel[:1]
        )
        a_parts = exchange(a_parts)
        gain_mid = ln_mid_gain[layer].reshape(tensor_size, -1)[places.tensor_places]
        stream_in = stream
        attn_out, middle, stream, h_ffn, mean, factor, pre, h_mid, *h_next = ffn_forward(
            places, stream, a_parts, matrix_set[layer], ln_post_gain[layer], ln_ffn_gain[layer],
            gain_mid, ln_attn_gain[(layer + 1) % LAYERS], last,
        )
        if not last:
            h_attn = h_next[0]
        saved.append(
            (
                stream_in, h_parts, queries, keys, values, mixture, logsum, scale_rel, a_parts,
                attn_out, middle, h_ffn, mean, factor, gain_mid, pre, h_mid,
            )
        )

    grad_stream = out_cotangent
    matrix_grads = [None] * LAYERS
    small_grads = [None] * LAYERS
    core_hop = ("tensor", tensor_masks[-1])
    side_hops = [("tensor", mask) for mask in reversed(tensor_masks[:-1])]
    near_hop = ("dp", places.near_mask)
    for layer in reversed(range(LAYERS)):
        (
            stream_in, h_parts, queries, keys, values, mixture, logsum, scale_rel, a_parts,
            attn_out, middle, h_ffn, mean, factor, gain_mid, pre, h_mid,
        ) = saved[layer]
        if layer == 0:
            down_keep, down_send = down_grads(places, grad_stream, h_mid)
            grad_stream, down_keep, down_send = lax.optimization_barrier(
                (grad_stream, down_keep, down_send)
            )
            down_arrived = swap(down_send, *core_hop)
        grad_low, grad_middle, grad_out, *rest = ffn_backward(
            places, grad_stream, attn_out, middle, mean, factor, pre, matrix_set[layer],
            ln_post_gain[layer], ln_ffn_gain[layer], gain_mid, scale_rel,
        )
        dout_parts = exchange(rest[:tensor_size])
        grad_pre, mid_sum, ffn_sum, post_sum = rest[tensor_size:]
        wide = h_mid.shape[2]
        if layer > 0:
            whole = whole_grads(places, grad_low, h_ffn, grad_out, grad_pre, h_mid, a_parts)
            dout_parts, whole = lax.optimization_barrier((dout_parts, whole))
            whole = whole.reshape(-1, *whole.shape[2:])
            rows = lax.psum_scatter(whole, ("dp", "tensor"), scatter_dimension=0, tiled=False)
            rows = rows.astype(F32)
            up_rows, down_rows, out_rows = (
                rows[:, :wide], rows[:, wide : 2 * wide], rows[:, 2 * wide :]
            )
        else:
            up_keep, up_send = up_grads(places, h_ffn, grad_out, grad_pre, a_parts)
            ups = add_halves(up_keep, swap(up_send, *core_hop))
            downs = add_halves(down_keep, down_arrived)
            dout_parts, ups, downs, above = lax.optimization_barrier(
                (dout_parts, ups, downs, matrix_grads[1][:3])
            )
            matrix_grads[1] = above + matrix_grads[1][3:]
            side_arrived = swap(ups[1], *side_hops[0])
            near_arrived = swap(downs[1], *near_hop)
        packed, inner_sum, keep, send = attend_backward(
            places, dout_parts, queries, keys, values, mixture, logsum, long_column, long_row,
            attn_set[layer],
        )
        if layer == 0:
            packed, send, side_arrived, near_arrived = lax.optimization_barrier(
                (packed, send, side_arrived, near_arrived)
            )
        grad_head = jnp.sum(inner_sum[:local_heads], 1) / scale_rel[0, ::HD]
        arrived = swap(send, *core_hop)
        for hop in side_hops:
            keep, send = add_halves(keep, arrived)
            arrived = swap(send, *hop)
        attn_keep, attn_send = attn_grads(places, h_parts, packed)
        attn_arrived = swap(attn_send, *near_hop)
        if layer > 0:
            arrived, attn_arrived = lax.optimization_barrier((arrived, attn_arrived))
        grad_h = (keep.astype(F32) + arrived.astype(F32)).reshape(stream_in.shape)
        normed_one, factor_one = normalize(stream_in)
        grad_attn_gain = jnp.sum(grad_h * normed_one, 0)
        grad_stream = grad_middle + norm_back(
            grad_h * ln_attn_gain[layer], normed_one, factor_one
        )
        attn_rows = scatter_rest(attn_keep, attn_arrived, places.far_hops)
        if layer == 0:
            hops = side_hops[1:] + [near_hop] + places.far_hops
            upper_rows = scatter_rest(ups[0], side_arrived, hops)
            up_rows, out_rows = upper_rows[:, :wide], upper_rows[:, wide:]
            down_rows = scatter_rest(downs[0], near_arrived, side_hops + places.far_hops)
        matrix_grads[layer] = (
            attn_rows[:, :width],
            attn_rows[:, width : 2 * width],
            attn_rows[:, 2 * width :],
            out_rows.T,
            up_rows,
            down_rows.T,
        )
        grad_head_all = lax.dynamic_update_slice_in_dim(
            jnp.zeros((H,), F32), grad_head, places.tensor_index * local_heads, 0
        )
        grad_mid_all = jnp.sum(mid_sum, 1)[places.tensor_sources].reshape(-1)
        small_grads[layer] = (
            grad_attn_gain, grad_head_all, jnp.sum(post_sum, 0), jnp.sum(ffn_sum, 0),
            grad_mid_all,
        )
    sizes = [part.shape[0] for part in small_grads[0]]
    vector = jnp.concatenate([part for layer in range(LAYERS) for part in small_grads[layer]])
    count = vector.shape[0]
    vector = jnp.pad(vector, (0, -count % 1024)).reshape(-1, 128)
    vector = sum_everywhere(vector).reshape(-1)
    smalls, start = [], 0
    for layer in range(LAYERS):
        found = []
        for size in sizes:
            found.append(lax.slice_in_dim(vector, start, start + size))
            start += size
        smalls.append(found)
    small = [jnp.stack([smalls[layer][at] for layer in range(LAYERS)]) for at in range(5)]
    stacked = [
        jnp.stack([matrix_grads[layer][at] for layer in range(LAYERS)]) for at in range(6)
    ]
    return (
        stream, grad_stream, small[0], stacked[0], stacked[1], stacked[2], small[1], stacked[3],
        small[2], small[3], stacked[4], small[4], stacked[5],
    )


def solution(mesh):
    rows = P(("dp", "tensor"), None)
    first = P(None, "dp", "tensor")
    second = P(None, "tensor", "dp")
    in_specs = (
        rows, P("dp", None), P(), first, first, first, P(), second, P(), P(), first, P(), second,
        rows,
    )
    out_specs = (
        rows, rows, P(), first, first, first, P(), second, P(), P(), first, P(), second,
    )
    return jax.shard_map(local, mesh=mesh, in_specs=in_specs, out_specs=out_specs, check_vma=False)
```

```python
import functools

import jax
import jax.numpy as jnp
from jax import lax
from jax.experimental import pallas as pl
from jax.experimental.pallas import tpu as pltpu
from jax.sharding import PartitionSpec as P

H = 16
HD = 64
LAYERS = 2
PROMPT = 1024
BLOCK = 512

NORM_EPSILON = 1e-05
MASKED_SCORE = -1e30
F32 = jnp.float32
BF16 = jnp.bfloat16
VMEM_LIMIT = 67_000_000


def tanh_gelu(inputs):
    return (
        0.5
        * inputs
        * (1.0 + jnp.tanh(0.7978845608028654 * (inputs + 0.044715 * inputs * inputs * inputs)))
    )


def normalize(values):
    center = values - jnp.mean(values, -1, keepdims=True)
    factor = lax.rsqrt(jnp.mean(center * center, -1, keepdims=True) + NORM_EPSILON)
    return (center * factor, factor)


def norm_back(grad_norm, normed, factor):
    return factor * (
        grad_norm
        - jnp.mean(grad_norm, -1, keepdims=True)
        - normed * jnp.mean(grad_norm * normed, -1, keepdims=True)
    )


def dot_nn(left, right):
    return lax.dot_general(left, right, (((1,), (0,)), ((), ())), preferred_element_type=F32)


def dot_tn(left, right):
    return lax.dot_general(left, right, (((0,), (0,)), ((), ())), preferred_element_type=F32)


def dot_nt(left, right):
    return lax.dot_general(left, right, (((1,), (1,)), ((), ())), preferred_element_type=F32)


def bit_masks(size):
    masks = []
    while size > 1:
        size //= 2
        masks.append(size)
    return masks


def relative_order(masks):
    order = [0]
    for mask in masks:
        order = order + [mask | other for other in order]
    return order


def swap(array, axis, mask):
    size = lax.axis_size(axis)
    return lax.ppermute(array, axis, [(i, i ^ mask) for i in range(size)])


class Places:
    def __init__(self):
        self.dp_size = lax.axis_size("dp")
        self.tensor_size = lax.axis_size("tensor")
        dp_index = lax.axis_index("dp").astype(jnp.int32)
        self.tensor_index = lax.axis_index("tensor").astype(jnp.int32)
        self.tensor_masks = bit_masks(self.tensor_size)
        masks = bit_masks(self.dp_size)
        self.far_masks = relative_order(masks[:-1])
        self.near_mask = masks[-1]
        self.far_hops = [("dp", mask) for mask in reversed(masks[:-1])]
        dp_order = self.far_masks + [mask | self.near_mask for mask in self.far_masks]
        self.tensor_order = relative_order(self.tensor_masks)
        tensor_inverse = [self.tensor_order.index(i) for i in range(self.tensor_size)]
        self.dp_places = jnp.array(dp_order, jnp.int32) ^ dp_index
        self.tensor_places = jnp.array(self.tensor_order, jnp.int32) ^ self.tensor_index
        spots = jnp.arange(self.tensor_size, dtype=jnp.int32) ^ self.tensor_index
        self.tensor_sources = jnp.array(tensor_inverse, jnp.int32)[spots]


def gather_far(shard, places):
    others = [swap(shard, "dp", mask) for mask in places.far_masks[1:]]
    return jnp.stack([shard] + others)


def gather_near(part, places):
    return [part, swap(part, "dp", places.near_mask)]


def gather_tensor(parts, masks):
    for mask in masks:
        parts = parts + [jax.tree.map(lambda x, m=mask: swap(x, "tensor", m), p) for p in parts]
    return parts


def gather_late_tensor(shard, places):
    pieces = gather_near(gather_far(shard, places), places)
    return gather_tensor([pieces], places.tensor_masks)


def gather_late_near(shard, places):
    parts = gather_tensor([gather_far(shard, places)], places.tensor_masks[:-1])
    pieces = [gather_near(part, places) for part in parts]
    return gather_tensor(pieces, places.tensor_masks[-1:])


def add_low(kept, arrived):
    return (kept.astype(F32) + arrived.astype(F32)).astype(BF16)


def add_halves(kept, arrived):
    half = kept.shape[0] // 2
    return add_low(kept[:half], arrived[:half]), add_low(kept[half:], arrived[half:])


def split_add(kept, arrived):
    while kept.shape[0] == 1:
        kept, arrived = kept[0], arrived[0]
    return add_halves(kept, arrived)


def scatter_rest(kept, arrived, hops):
    for hop in hops:
        kept, sent = split_add(kept, arrived)
        arrived = swap(sent, *hop)
    total = kept.astype(F32) + arrived.astype(F32)
    return total.reshape(total.shape[-2:])


def sum_everywhere(vector):
    for axis in ("tensor", "dp"):
        for mask in reversed(bit_masks(lax.axis_size(axis))):
            vector = vector + swap(vector, axis, mask)
    return vector


def block_rows(place_ref, at, rows):
    return pl.ds(pl.multiple_of(place_ref[at] * rows, rows), rows)


def start_rows(spot, blocks, columns, target, semaphore):
    count, _, rows, _ = blocks.shape
    for at in range(count):
        pltpu.make_async_copy(
            blocks.at[at, spot, :, columns], target.at[at * rows : (at + 1) * rows, :], semaphore
        ).start()


def wait_whole(target, semaphore):
    pltpu.make_async_copy(target, target, semaphore).wait()


def each_rows(total, chunk, body):
    for start in range(0, total, chunk):
        body(pl.ds(start, chunk))


def lanes(values, width):
    return jnp.concatenate([values] * (width // 128), axis=1)


def fold_lanes(values):
    total = values[:, :128]
    for lane in range(128, values.shape[1], 128):
        total = total + values[:, lane : lane + 128]
    return total


def fold_rows(values):
    return jnp.sum(values.reshape(values.shape[0] // 8, 8, values.shape[1]), axis=0)


CHUNK = 16


def ffn_forward_kernel(parts, last, place_ref, *refs):
    refs = list(refs)

    def take(count):
        taken = refs[:count]
        del refs[:count]
        return taken

    (stream_ref,) = take(1)
    a_refs = take(parts)
    (matrix_ref,) = take(1)
    post_ref, ffn_ref, mid_ref, next_ref = take(4)
    out_ref, middle_ref, next_stream_ref, h_ffn_ref, mean_ref, factor_ref = take(6)
    pre_ref, h_mid_ref = take(2)
    h_next_ref = None if last else take(1)[0]
    w_up, w_out, w_down, active, pre_buf, mid_buf, sums, squares = take(8)
    up_sem, out_sem, down_sem, pre_sem, mid_sem = take(5)
    rows, depth = stream_ref.shape
    wide = w_up.shape[2]
    narrow = w_out.shape[2]
    hidden = parts * wide

    up_columns, down_columns = pl.ds(0, wide), pl.ds(wide, wide)
    out_columns = pl.ds(2 * wide, narrow)
    for at in range(parts):
        start_rows(place_ref[at], matrix_ref, out_columns, w_out.at[at], out_sem)
    for at in range(parts):
        start_rows(place_ref[at], matrix_ref, up_columns, w_up.at[at], up_sem.at[at])
    for at in range(parts):
        start_rows(place_ref[at], matrix_ref, down_columns, w_down.at[at], down_sem.at[at])
    wait_whole(w_out, out_sem)
    out_ref[...] = sum(dot_nt(a_refs[at][...], w_out[at]) for at in range(parts))

    def middle_rows(here):
        normed, _ = normalize(out_ref[here, :])
        middle = stream_ref[here, :] + normed * post_ref[...]
        middle_ref[here, :] = middle
        normed, _ = normalize(middle)
        h_ffn_ref[here, :] = (normed * ffn_ref[...]).astype(BF16)

    each_rows(rows, CHUNK, middle_rows)
    sums[...] = jnp.zeros_like(sums)
    squares[...] = jnp.zeros_like(squares)

    def write_pre(at):
        return pltpu.make_async_copy(pre_buf.at[at % 2], pre_ref.at[at], pre_sem.at[at % 2])

    def write_mid(at):
        return pltpu.make_async_copy(mid_buf.at[at % 2], h_mid_ref.at[at], mid_sem.at[at % 2])

    wait_whole(w_up.at[0], up_sem.at[0])
    pre_buf[0] = dot_nn(h_ffn_ref[...], w_up[0])
    for at in range(parts):
        write_pre(at).start()
        if at + 1 < parts:
            wait_whole(w_up.at[at + 1], up_sem.at[at + 1])
            if at >= 1:
                write_pre(at - 1).wait()
            pre_buf[(at + 1) % 2] = dot_nn(h_ffn_ref[...], w_up[at + 1])

        def active_rows(here, at=at):
            value = tanh_gelu(pre_buf[at % 2, here, :])
            active[at, here, :] = value
            sums[here, :] += fold_lanes(value)
            squares[here, :] += fold_lanes(value * value)

        each_rows(rows, CHUNK, active_rows)
    mean = jnp.sum(sums[...], axis=1, keepdims=True) / hidden
    spread = jnp.sum(squares[...], axis=1, keepdims=True) / hidden - mean * mean
    mean_ref[...] = jnp.broadcast_to(mean, mean_ref.shape)
    factor_ref[...] = jnp.broadcast_to(lax.rsqrt(spread + NORM_EPSILON), factor_ref.shape)

    def mid_part(at):
        def mid_rows(here):
            normed = active[at, here, :] - lanes(mean_ref[here, :], wide)
            normed = normed * lanes(factor_ref[here, :], wide)
            mid_buf[at % 2, here, :] = (normed * mid_ref[at : at + 1, :]).astype(BF16)

        each_rows(rows, CHUNK, mid_rows)

    mid_part(0)
    for at in range(parts):
        write_mid(at).start()
        wait_whole(w_down.at[at], down_sem.at[at])
        if 1 <= at < parts - 1:
            write_mid(at - 1).wait()
        product = dot_nt(mid_buf[at % 2], w_down[at])
        if at == 0:
            next_stream_ref[...] = middle_ref[...] + product
        else:
            next_stream_ref[...] += product
        if at + 1 < parts:
            mid_part(at + 1)
    if not last:

        def next_rows(here):
            normed, _ = normalize(next_stream_ref[here, :])
            h_next_ref[here, :] = (normed * next_ref[...]).astype(BF16)

        each_rows(rows, CHUNK, next_rows)
    for at in range(max(parts - 2, 0), parts):
        write_pre(at).wait()
        write_mid(at).wait()


def ffn_forward(places, stream, a_parts, matrices, post, ffn, mid, following, last):
    rows, depth = stream.shape
    parts, wide = mid.shape
    narrow = a_parts[0].shape[1]
    vmem = pl.BlockSpec(memory_space=pltpu.VMEM)
    hbm = pl.BlockSpec(memory_space=pl.ANY)
    full = jax.ShapeDtypeStruct((rows, depth), F32)
    low = jax.ShapeDtypeStruct((rows, depth), BF16)
    stat = jax.ShapeDtypeStruct((rows, 128), F32)
    outs = [full, full, full, low, stat, stat] + [
        jax.ShapeDtypeStruct((parts, rows, wide), F32),
        jax.ShapeDtypeStruct((parts, rows, wide), BF16),
    ]
    out_specs = [vmem] * 6 + [hbm] * 2
    if not last:
        outs, out_specs = outs + [low], out_specs + [vmem]
    dma = pltpu.SemaphoreType.DMA
    return pl.pallas_call(
        functools.partial(ffn_forward_kernel, parts, last),
        in_specs=[pl.BlockSpec(memory_space=pltpu.SMEM)]
        + [vmem] * (1 + parts)
        + [hbm]
        + [vmem] * 4,
        out_specs=out_specs,
        out_shape=outs,
        scratch_shapes=[
            pltpu.VMEM((parts, depth, wide), BF16),
            pltpu.VMEM((parts, depth, narrow), BF16),
            pltpu.VMEM((parts, depth, wide), BF16),
            pltpu.VMEM((parts, rows, wide), F32),
            pltpu.VMEM((2, rows, wide), F32),
            pltpu.VMEM((2, rows, wide), BF16),
            pltpu.VMEM((rows, 128), F32),
            pltpu.VMEM((rows, 128), F32),
            dma((parts,)),
            dma,
            dma((parts,)),
            dma((2,)),
            dma((2,)),
        ],
        compiler_params=pltpu.CompilerParams(vmem_limit_bytes=VMEM_LIMIT),
        cost_estimate=pl.CostEstimate(
            flops=2 * rows * depth * parts * (2 * wide + narrow),
            bytes_accessed=40 << 20,
            transcendentals=rows * parts * wide,
        ),
        name="ffn_forward",
    )(
        places.tensor_places,
        stream,
        *a_parts,
        matrices,
        post[None],
        ffn[None],
        mid,
        following[None],
    )


def ffn_backward_kernel(parts, place_ref, *refs):
    refs = list(refs)

    def take(count):
        taken = refs[:count]
        del refs[:count]
        return taken

    grad_ref, out_ref, middle_ref, mean_ref, factor_ref, pre_ref = take(6)
    (matrix_ref,) = take(1)
    post_ref, ffn_ref, mid_ref, scale_ref = take(4)
    low_ref, grad_middle_ref, grad_out_ref = take(3)
    dout_refs = take(parts)
    grad_pre_ref, mid_sum_ref, ffn_sum_ref, post_sum_ref = take(4)
    weights, w_out, grad_normed, normed_four, slope, pre_buf, product, low_buf = take(8)
    first, second = take(2)
    weight_sem, out_sem, pre_sem, low_sem = take(4)
    rows, depth = grad_ref.shape
    wide = weights.shape[2]
    narrow = w_out.shape[2]
    hidden = parts * wide

    def read_pre(at):
        return pltpu.make_async_copy(pre_ref.at[at], pre_buf.at[at % 2], pre_sem.at[at % 2])

    up_columns, down_columns = pl.ds(0, wide), pl.ds(wide, wide)
    out_columns = pl.ds(2 * wide, narrow)
    for at in range(parts):
        start_rows(place_ref[at], matrix_ref, down_columns, weights.at[at], weight_sem.at[at])
        if at < 2:
            read_pre(at).start()
    for at in range(parts):
        start_rows(place_ref[at], matrix_ref, out_columns, w_out.at[at], out_sem)
    low_ref[...] = grad_ref[...].astype(BF16)
    first[...] = jnp.zeros_like(first)
    second[...] = jnp.zeros_like(second)
    mid_sum_ref[...] = jnp.zeros_like(mid_sum_ref)
    ffn_sum_ref[...] = jnp.zeros_like(ffn_sum_ref)
    post_sum_ref[...] = jnp.zeros_like(post_sum_ref)
    wait_whole(weights.at[0], weight_sem.at[0])
    product[0] = dot_nn(low_ref[...], weights[0])
    for at in range(parts):
        start_rows(place_ref[at], matrix_ref, up_columns, weights.at[at], weight_sem.at[at])
        read_pre(at).wait()
        if at + 1 < parts:
            wait_whole(weights.at[at + 1], weight_sem.at[at + 1])
            product[(at + 1) % 2] = dot_nn(low_ref[...], weights[at + 1])

        def hidden_rows(here, at=at):
            value = pre_buf[at % 2, here, :]
            squared = value * value
            bend = jnp.tanh(value * (0.7978845608028654 + 0.035677408136300125 * squared))
            raised = 0.5 + 0.5 * bend
            normed = value * raised - lanes(mean_ref[here, :], wide)
            normed = normed * lanes(factor_ref[here, :], wide)
            steep = value * (0.7978845608028654 + 0.10703222440890037 * squared)
            slope[at, here, :] = raised + 0.5 * steep * (1.0 - bend * bend)
            normed_four[at, here, :] = normed.astype(BF16)
            grad = product[at % 2, here, :]
            mid_sum_ref[at] += fold_rows(grad * normed)
            grad = grad * mid_ref[at : at + 1, :]
            grad_normed[at, here, :] = grad
            first[here, :] += fold_lanes(grad)
            second[here, :] += fold_lanes(grad * normed)

        each_rows(rows, CHUNK, hidden_rows)
        if at + 2 < parts:
            read_pre(at + 2).start()
    first[...] = jnp.broadcast_to(
        jnp.sum(first[...], axis=1, keepdims=True) / hidden, first.shape
    )
    second[...] = jnp.broadcast_to(
        jnp.sum(second[...], axis=1, keepdims=True) / hidden, second.shape
    )

    def write_low(at):
        return pltpu.make_async_copy(low_buf.at[at % 2], grad_pre_ref.at[at], low_sem.at[at % 2])

    def low_part(at):
        def pre_rows(here):
            normed = normed_four[at, here, :].astype(F32)
            grad = grad_normed[at, here, :] - lanes(first[here, :], wide)
            grad = grad - normed * lanes(second[here, :], wide)
            grad = grad * slope[at, here, :] * lanes(factor_ref[here, :], wide)
            low_buf[at % 2, here, :] = grad.astype(BF16)

        each_rows(rows, CHUNK, pre_rows)

    low_part(0)
    for at in range(parts):
        write_low(at).start()
        wait_whole(weights.at[at], weight_sem.at[at])
        if 1 <= at < parts - 1:
            write_low(at - 1).wait()
        part = dot_nt(low_buf[at % 2], weights[at])
        if at == 0:
            product[0] = part
        else:
            product[0] += part
        if at + 1 < parts:
            low_part(at + 1)

    def middle_rows(here):
        grad = product[0, here, :]
        normed, factor = normalize(middle_ref[here, :])
        ffn_sum_ref[...] += fold_rows(grad * normed)
        grad = grad_ref[here, :] + norm_back(grad * ffn_ref[...], normed, factor)
        grad_middle_ref[here, :] = grad
        normed, factor = normalize(out_ref[here, :])
        post_sum_ref[...] += fold_rows(grad * normed)
        grad_out_ref[here, :] = norm_back(grad * post_ref[...], normed, factor).astype(BF16)

    each_rows(rows, CHUNK, middle_rows)
    wait_whole(w_out, out_sem)
    for at in range(parts):
        grad = dot_nn(grad_out_ref[...], w_out[at])
        dout_refs[at][...] = (grad * scale_ref[at : at + 1, :]).astype(BF16)
    for at in range(max(parts - 2, 0), parts):
        write_low(at).wait()


def ffn_backward(places, grad, out, middle, mean, factor, pre, matrices, post, ffn, mid, scale):
    rows, depth = grad.shape
    parts, wide = mid.shape
    narrow = scale.shape[1]
    vmem = pl.BlockSpec(memory_space=pltpu.VMEM)
    hbm = pl.BlockSpec(memory_space=pl.ANY)
    low = jax.ShapeDtypeStruct((rows, depth), BF16)
    sums = jax.ShapeDtypeStruct((8, depth), F32)
    dma = pltpu.SemaphoreType.DMA
    return pl.pallas_call(
        functools.partial(ffn_backward_kernel, parts),
        in_specs=[pl.BlockSpec(memory_space=pltpu.SMEM)]
        + [vmem] * 5
        + [hbm] * 2
        + [vmem] * 4,
        out_specs=[vmem] * (3 + parts) + [hbm] + [vmem] * 3,
        out_shape=[low, jax.ShapeDtypeStruct((rows, depth), F32), low]
        + [jax.ShapeDtypeStruct((rows, narrow), BF16)] * parts
        + [
            jax.ShapeDtypeStruct((parts, rows, wide), BF16),
            jax.ShapeDtypeStruct((parts, 8, wide), F32),
            sums,
            sums,
        ],
        scratch_shapes=[
            pltpu.VMEM((parts, depth, wide), BF16),
            pltpu.VMEM((parts, depth, narrow), BF16),
            pltpu.VMEM((parts, rows, wide), F32),
            pltpu.VMEM((parts, rows, wide), BF16),
            pltpu.VMEM((parts, rows, wide), F32),
            pltpu.VMEM((2, rows, wide), F32),
            pltpu.VMEM((2, rows, depth), F32),
            pltpu.VMEM((2, rows, wide), BF16),
            pltpu.VMEM((rows, 128), F32),
            pltpu.VMEM((rows, 128), F32),
            dma((parts,)),
            dma,
            dma((2,)),
            dma((2,)),
        ],
        compiler_params=pltpu.CompilerParams(vmem_limit_bytes=VMEM_LIMIT),
        cost_estimate=pl.CostEstimate(
            flops=2 * rows * depth * parts * (2 * wide + narrow),
            bytes_accessed=44 << 20,
            transcendentals=rows * parts * wide,
        ),
        name="ffn_backward",
    )(
        places.tensor_places,
        grad,
        out,
        middle,
        mean,
        factor,
        pre,
        matrices,
        post[None],
        ffn[None],
        mid,
        scale,
    )


def turned(place_ref, source, plain, target, rows):
    plain[...] = source[...].astype(BF16).astype(F32).T.astype(BF16)
    for at in range(target.shape[0] // rows):
        target[at * rows : (at + 1) * rows, :] = plain[block_rows(place_ref, at, rows), :]


def up_grads_kernel(parts, place_ref, *refs):
    h_ffn_ref, grad_out_ref, grad_pre_ref, a_ref, keep_ref, send_ref = refs[:6]
    h_turned, out_turned, h_plain, out_plain = refs[6:]
    step = pl.program_id(0)
    count, rows = keep_ref.shape[2:4]
    wide = grad_pre_ref.shape[2]

    @pl.when(step == 0)
    def _():
        turned(place_ref, h_ffn_ref, h_plain, h_turned, rows)
        turned(place_ref, grad_out_ref, out_plain, out_turned, rows)

    def fill(target):
        shape = (2, count, rows, -1)
        grad = dot_nn(h_turned[...], grad_pre_ref[0]).astype(BF16)
        target[0, :, :, :, :wide] = grad.reshape(shape)
        grad = dot_nn(out_turned[...], a_ref[0]).astype(BF16)
        target[0, :, :, :, wide:] = grad.reshape(shape)

    @pl.when(step < parts // 2)
    def _():
        fill(keep_ref)

    @pl.when(step >= parts // 2)
    def _():
        fill(send_ref)


def down_grads_kernel(parts, place_ref, *refs):
    grad_ref, h_mid_ref, keep_ref, send_ref, low_turned, low_plain = refs
    step = pl.program_id(0)
    count, rows = keep_ref.shape[2:4]

    @pl.when(step == 0)
    def _():
        turned(place_ref, grad_ref, low_plain, low_turned, rows)

    def fill(target):
        grad = dot_nn(low_turned[...], h_mid_ref[0]).astype(BF16)
        target[:, 0] = grad.reshape(2, count, rows, -1)

    @pl.when(step < parts // 2)
    def _():
        fill(keep_ref)

    @pl.when(step >= parts // 2)
    def _():
        fill(send_ref)


def split_grads(kernel, name, places, turns, sides, block, outside, at_part):
    parts, rows, _ = sides[0].shape
    depth = turns[0].shape[1]
    half = parts // 2
    columns = sum(side.shape[2] for side in sides)
    whole = pl.BlockSpec((rows, depth), lambda i, place: (0, 0))
    return pl.pallas_call(
        functools.partial(kernel, parts),
        grid_spec=pltpu.PrefetchScalarGridSpec(
            num_scalar_prefetch=1,
            grid=(parts,),
            in_specs=[whole] * len(turns)
            + [pl.BlockSpec((1,) + side.shape[1:], lambda i, place: (i, 0, 0)) for side in sides],
            out_specs=[
                pl.BlockSpec(block, lambda i, place: at_part(jnp.minimum(i, half - 1))),
                pl.BlockSpec(block, lambda i, place: at_part(jnp.maximum(i - half, 0))),
            ],
            scratch_shapes=[pltpu.VMEM((depth, rows), BF16)] * (2 * len(turns)),
        ),
        out_shape=[jax.ShapeDtypeStruct(outside, BF16)] * 2,
        compiler_params=pltpu.CompilerParams(vmem_limit_bytes=VMEM_LIMIT),
        cost_estimate=pl.CostEstimate(
            flops=2 * rows * depth * parts * columns,
            bytes_accessed=16 << 20,
            transcendentals=0,
        ),
        name=name,
    )(places.dp_places, *turns, *sides)


def up_grads(places, h_ffn, grad_out, grad_pre, a_parts):
    a_all = jnp.stack(a_parts)
    half = len(a_parts) // 2
    count = places.dp_size // 2
    tail = (count, h_ffn.shape[1] // places.dp_size, grad_pre.shape[2] + a_all.shape[2])
    return split_grads(
        up_grads_kernel, "up_grads", places, [h_ffn, grad_out], [grad_pre, a_all],
        (1, 2) + tail, (half, 2) + tail, lambda part: (part, 0, 0, 0, 0),
    )


def down_grads(places, grad, h_mid):
    half = h_mid.shape[0] // 2
    count = places.dp_size // 2
    tail = (count, grad.shape[1] // places.dp_size, h_mid.shape[2])
    return split_grads(
        down_grads_kernel, "down_grads", places, [grad], [h_mid],
        (2, 1) + tail, (2, half) + tail, lambda part: (0, part, 0, 0, 0),
    )


def whole_grads_kernel(parts, place_ref, *refs):
    del place_ref
    low_ref, h_ffn_ref, grad_out_ref, grad_pre_ref, h_mid_ref, a_ref, matrix_ref = refs[:7]
    low_turned, h_turned, out_turned = refs[7:]
    wide = h_mid_ref.shape[2]
    shape = matrix_ref.shape[:3] + (-1,)

    @pl.when(pl.program_id(0) == 0)
    def _():
        for source, target in (
            (low_ref, low_turned), (h_ffn_ref, h_turned), (grad_out_ref, out_turned)
        ):
            target[...] = source[...].astype(F32).T.astype(BF16)

    grad = dot_nn(h_turned[...], grad_pre_ref[0]).astype(BF16)
    matrix_ref[:, :, :, :wide] = grad.reshape(shape)
    grad = dot_nn(low_turned[...], h_mid_ref[0]).astype(BF16)
    matrix_ref[:, :, :, wide : 2 * wide] = grad.reshape(shape)
    grad = dot_nn(out_turned[...], a_ref[0]).astype(BF16)
    matrix_ref[:, :, :, 2 * wide :] = grad.reshape(shape)


def whole_grads(places, low, h_ffn, grad_out, grad_pre, h_mid, a_parts):
    rows, depth = low.shape
    parts, _, wide = h_mid.shape
    narrow = a_parts[0].shape[1]
    block = depth // places.dp_size
    columns = 2 * wide + narrow
    whole = pl.BlockSpec((rows, depth), lambda i, place: (0, 0))
    each = pl.BlockSpec((1, rows, wide), lambda i, place: (i, 0, 0))
    return pl.pallas_call(
        functools.partial(whole_grads_kernel, parts),
        grid_spec=pltpu.PrefetchScalarGridSpec(
            num_scalar_prefetch=1,
            grid=(parts,),
            in_specs=[whole] * 3
            + [each] * 2
            + [pl.BlockSpec((1, rows, narrow), lambda i, place: (i, 0, 0))],
            out_specs=pl.BlockSpec(
                (places.dp_size, 1, block, columns), lambda i, place: (0, place[i], 0, 0)
            ),
            scratch_shapes=[pltpu.VMEM((depth, rows), BF16)] * 3,
        ),
        out_shape=jax.ShapeDtypeStruct((places.dp_size, parts, block, columns), BF16),
        compiler_params=pltpu.CompilerParams(vmem_limit_bytes=VMEM_LIMIT),
        cost_estimate=pl.CostEstimate(
            flops=2 * rows * depth * parts * columns,
            bytes_accessed=30 << 20,
            transcendentals=0,
        ),
        name="whole_grads",
    )(places.tensor_places, low, h_ffn, grad_out, grad_pre, h_mid, jnp.stack(a_parts))


def attn_grads_kernel(parts, place_ref, *refs):
    h_refs = refs[:parts]
    packed_ref, keep_ref, send_ref, total = refs[parts:]
    count, rows, _ = keep_ref.shape
    tokens = packed_ref.shape[0] // parts
    for part in range(parts):
        flipped = h_refs[part][...].astype(F32).T.astype(BF16)
        grad = dot_nn(flipped, packed_ref[part * tokens : (part + 1) * tokens, :])
        if part == 0:
            total[...] = grad
        else:
            total[...] += grad
    for at in range(count):
        keep_ref[at] = total[block_rows(place_ref, at, rows), :].astype(BF16)
        send_ref[at] = total[block_rows(place_ref, count + at, rows), :].astype(BF16)


def attn_grads(places, h_parts, packed):
    parts = len(h_parts)
    tokens, depth = h_parts[0].shape
    columns = packed.shape[1]
    count = places.dp_size // 2
    block = depth // places.dp_size
    vmem = pl.BlockSpec(memory_space=pltpu.VMEM)
    return pl.pallas_call(
        functools.partial(attn_grads_kernel, parts),
        in_specs=[pl.BlockSpec(memory_space=pltpu.SMEM)] + [vmem] * (parts + 1),
        out_specs=[vmem] * 2,
        out_shape=[jax.ShapeDtypeStruct((count, block, columns), BF16)] * 2,
        scratch_shapes=[
            pltpu.VMEM((depth, columns), F32),
        ],
        compiler_params=pltpu.CompilerParams(vmem_limit_bytes=VMEM_LIMIT),
        cost_estimate=pl.CostEstimate(
            flops=2 * tokens * parts * depth * columns,
            bytes_accessed=8 << 20,
            transcendentals=0,
        ),
        name="attn_grads",
    )(places.dp_places, *h_parts, packed)


def half_mask(shape, head):
    lane = lax.broadcasted_iota(jnp.int32, shape, len(shape) - 1)
    return (lane // HD) == (head % 2)


def place_rows(place_ref, pieces, target):
    for half, piece in enumerate(pieces):
        count, rows, _ = piece.shape
        for at in range(count):
            target[block_rows(place_ref, half * count + at, rows), :] = piece[at]


def forward_kernel(block_ref, place_ref, *refs):
    parts = block_ref.shape[0]
    rows_refs = refs[:parts]
    pieces = refs[parts : parts + 2]
    column_ref, row_ref, scale_ref = refs[parts + 2 : parts + 5]
    query_ref, key_ref, value_ref, mixture_ref, logsum_ref = refs[parts + 5 : parts + 10]
    scaled_refs = refs[parts + 10 : -2]
    score_ref, weight_ref = refs[-2:]
    width = query_ref.shape[1]
    length = query_ref.shape[0]
    rows = length // parts

    place_rows(place_ref, pieces, weight_ref)
    for part in range(parts):
        at = pl.ds(pl.multiple_of(block_ref[part] * rows, rows), rows)
        packed = dot_nn(rows_refs[part][...], weight_ref[...])
        query_ref[at, :] = packed[:, :width].astype(BF16) * jnp.asarray(0.125, BF16)
        key_ref[at, :] = packed[:, width : 2 * width].astype(BF16)
        value_ref[at, :] = packed[:, 2 * width :].astype(BF16)

    for query_block in range(length // BLOCK):
        here = pl.ds(query_block * BLOCK, BLOCK)

        def one_head(head, logsums, query_block=query_block, here=here):
            lanes = pl.ds(pl.multiple_of((head // 2) * 128, 128), 128)
            own = half_mask((BLOCK, 128), head)
            query = jnp.where(own, query_ref[here, lanes], jnp.asarray(0, BF16))
            highest = jnp.full((BLOCK, 128), MASKED_SCORE, F32)
            for key_block in range(query_block + 1):
                there = pl.ds(key_block * BLOCK, BLOCK)
                scores = dot_nt(query, key_ref[there, lanes])
                if key_block == query_block or key_block * BLOCK >= PROMPT:
                    first = lax.broadcasted_iota(jnp.int32, (BLOCK, BLOCK), 0)
                    second = lax.broadcasted_iota(jnp.int32, (BLOCK, BLOCK), 1)
                    seen = None
                    if key_block == query_block:
                        seen = second <= first
                    if key_block * BLOCK >= PROMPT:
                        query_at = pl.ds(query_block * BLOCK - PROMPT, BLOCK)
                        key_at = pl.ds(key_block * BLOCK - PROMPT, BLOCK)
                        same = column_ref[query_at, :] == row_ref[:, key_at]
                        seen = same if seen is None else seen & same
                    scores = jnp.where(seen, scores, MASKED_SCORE)
                score_ref[:, there] = scores
                for lane in range(0, BLOCK, 128):
                    highest = jnp.maximum(highest, scores[:, lane : lane + 128])
            top = jnp.max(highest, axis=1, keepdims=True)
            total = jnp.zeros((BLOCK, 128), F32)
            mixed = jnp.zeros((BLOCK, 128), F32)
            for key_block in range(query_block + 1):
                there = pl.ds(key_block * BLOCK, BLOCK)
                weights = jnp.exp(score_ref[:, there] - top)
                for lane in range(0, BLOCK, 128):
                    total = total + weights[:, lane : lane + 128]
                mixed = mixed + dot_nn(weights.astype(BF16), value_ref[there, lanes])
            denominator = jnp.sum(total, axis=1, keepdims=True)
            mixed = mixed / denominator
            mixture_ref[here, lanes] = jnp.where(own, mixed, mixture_ref[here, lanes])
            lane = lax.broadcasted_iota(jnp.int32, (BLOCK, 128), 1)
            return jnp.where(lane == head, top + jnp.log(denominator), logsums)

        logsums = lax.fori_loop(0, width // HD, one_head, jnp.zeros((BLOCK, 128), F32))
        logsum_ref[:, here] = logsums.T[: logsum_ref.shape[0], :]

    for part in range(parts):
        at = pl.ds(pl.multiple_of(block_ref[part] * rows, rows), rows)
        scaled_refs[part][...] = (mixture_ref[at, :] * scale_ref[...]).astype(BF16)


def attend_forward(places, rows, pieces, seg_column, seg_row, scale):
    parts = len(rows)
    length = parts * rows[0].shape[0]
    width = pieces[0].shape[2] // 3
    depth = rows[0].shape[1]
    heads = width // HD
    pairs = length * length * 5 // 8
    whole = pl.BlockSpec(memory_space=pltpu.VMEM)
    return pl.pallas_call(
        forward_kernel,
        in_specs=[pl.BlockSpec(memory_space=pltpu.SMEM)] * 2 + [whole] * (parts + 5),
        out_specs=[whole] * (5 + parts),
        out_shape=[jax.ShapeDtypeStruct((length, width), BF16)] * 3
        + [
            jax.ShapeDtypeStruct((length, width), F32),
            jax.ShapeDtypeStruct((8, length), F32),
        ]
        + [jax.ShapeDtypeStruct((length // parts, width), BF16)] * parts,
        scratch_shapes=[
            pltpu.VMEM((BLOCK, length), F32),
            pltpu.VMEM((depth, 3 * width), BF16),
        ],
        compiler_params=pltpu.CompilerParams(vmem_limit_bytes=VMEM_LIMIT),
        cost_estimate=pl.CostEstimate(
            flops=2 * length * depth * 3 * width + heads * pairs * 4 * 256,
            bytes_accessed=20 << 20,
            transcendentals=heads * pairs,
        ),
        name="attend_forward",
    )(places.tensor_places, places.dp_places, *rows, *pieces, seg_column, seg_row, scale)


def backward_kernel(block_ref, place_ref, open_ref, edge_ref, *refs):
    parts = block_ref.shape[0]
    grad_refs = refs[:parts]
    query_ref, key_ref, value_ref, mixture_ref, logsum_ref = refs[parts : parts + 5]
    column_ref, row_ref = refs[parts + 5 : parts + 7]
    pieces = refs[parts + 7 : parts + 9]
    packed_ref, inner_sum_ref, keep_ref, send_ref = refs[parts + 9 : parts + 13]
    dout_ref, inner_ref, dq_ref, dk_ref, dv_ref, weight_ref = refs[parts + 13 :]
    length, width = query_ref.shape
    rows = length // parts

    for part in range(parts):
        at = pl.ds(pl.multiple_of(block_ref[part] * rows, rows), rows)
        dout_ref[at, :] = grad_refs[part][...]
    picks = lax.broadcasted_iota(jnp.int32, (8, width), 1) // HD == lax.broadcasted_iota(
        jnp.int32, (8, width), 0
    )
    picks = jnp.where(picks, 1.0, 0.0)
    inner_sum = jnp.zeros((8, 128), F32)
    for part in range(length // BLOCK):
        at = pl.ds(part * BLOCK, BLOCK)
        product = dout_ref[at, :].astype(F32) * mixture_ref[at, :]
        inner = lax.dot_general(
            picks,
            product,
            (((1,), (1,)), ((), ())),
            precision=lax.Precision.HIGHEST,
            preferred_element_type=F32,
        )
        inner_ref[:, at] = inner
        for lane in range(0, BLOCK, 128):
            inner_sum = inner_sum + inner[:, lane : lane + 128]
    inner_sum_ref[...] = inner_sum
    dq_ref[...] = jnp.zeros_like(dq_ref)
    dk_ref[...] = jnp.zeros_like(dk_ref)
    dv_ref[...] = jnp.zeros_like(dv_ref)

    def one_pair(head, key_block, query_block, edge):
        lanes = pl.ds(pl.multiple_of((head // 2) * 128, 128), 128)
        there = pl.ds(pl.multiple_of(key_block * BLOCK, BLOCK), BLOCK)
        here = pl.ds(pl.multiple_of(query_block * BLOCK, BLOCK), BLOCK)
        own = half_mask((BLOCK, 128), head)
        none = jnp.asarray(0, BF16)
        query = jnp.where(own, query_ref[here, lanes], none)
        dout = jnp.where(own, dout_ref[here, lanes], none)
        key = key_ref[there, lanes]
        scores = dot_nt(key, query)
        weights = jnp.exp(scores - logsum_ref[pl.ds(head, 1), here])
        if edge:
            key_at = key_block * BLOCK + lax.broadcasted_iota(jnp.int32, (BLOCK, BLOCK), 0)
            query_at = query_block * BLOCK + lax.broadcasted_iota(jnp.int32, (BLOCK, BLOCK), 1)
            same = column_ref[there, :] == row_ref[:, here]
            weights = jnp.where((key_at <= query_at) & same, weights, 0.0)
        dv_ref[there, lanes] += dot_nn(weights.astype(BF16), dout)
        grad = dot_nt(value_ref[there, lanes], dout)
        grad = (weights * (grad - inner_ref[pl.ds(head, 1), here])).astype(BF16)
        dk_ref[there, lanes] += dot_nn(grad, query)
        dq_ref[here, lanes] += dot_tn(grad, jnp.where(own, key, none))

    def one_head(head, carry):
        def open_pair(at, inside):
            one_pair(head, open_ref[2 * at], open_ref[2 * at + 1], False)
            return inside

        def edge_pair(at, inside):
            one_pair(head, edge_ref[2 * at], edge_ref[2 * at + 1], True)
            return inside

        lax.fori_loop(0, open_ref.shape[0] // 2, open_pair, 0)
        lax.fori_loop(0, edge_ref.shape[0] // 2, edge_pair, 0)
        return carry

    lax.fori_loop(0, width // HD, one_head, 0)
    for part in range(parts):
        at = pl.ds(pl.multiple_of(block_ref[part] * rows, rows), rows)
        to = pl.ds(part * rows, rows)
        packed_ref[to, :width] = (dq_ref[at, :] * 0.125).astype(BF16)
        packed_ref[to, width : 2 * width] = dk_ref[at, :].astype(BF16)
        packed_ref[to, 2 * width :] = dv_ref[at, :].astype(BF16)
    place_rows(place_ref, pieces, weight_ref)
    for part in range(parts):
        grad = dot_nt(packed_ref[part * rows : (part + 1) * rows, :], weight_ref[...])
        half = parts // 2
        target = keep_ref if part < half else send_ref
        target[part % half] = grad.astype(BF16)


def attend_backward(
    places, grads, queries, keys, values, mixture, logsum, seg_column, seg_row, pieces
):
    parts = len(grads)
    length, width = queries.shape
    heads = width // HD
    depth = pieces[0].shape[0] * pieces[0].shape[1] * 2
    opened, edges = [], []
    for query_block in range(length // BLOCK):
        for key_block in range(query_block + 1):
            if key_block == query_block or key_block * BLOCK >= PROMPT:
                edges += [key_block, query_block]
            else:
                opened += [key_block, query_block]
    whole = pl.BlockSpec(memory_space=pltpu.VMEM)
    scalars = pl.BlockSpec(memory_space=pltpu.SMEM)
    pairs = length * length * 5 // 8
    return pl.pallas_call(
        backward_kernel,
        in_specs=[scalars] * 4 + [whole] * (parts + 9),
        out_specs=[whole] * 4,
        out_shape=[
            jax.ShapeDtypeStruct((length, 3 * width), BF16),
            jax.ShapeDtypeStruct((8, 128), F32),
            jax.ShapeDtypeStruct((parts // 2, length // parts, depth), BF16),
            jax.ShapeDtypeStruct((parts // 2, length // parts, depth), BF16),
        ],
        scratch_shapes=[
            pltpu.VMEM((length, width), BF16),
            pltpu.VMEM((8, length), F32),
            pltpu.VMEM((length, width), F32),
            pltpu.VMEM((length, width), F32),
            pltpu.VMEM((length, width), F32),
            pltpu.VMEM((depth, 3 * width), BF16),
        ],
        compiler_params=pltpu.CompilerParams(vmem_limit_bytes=VMEM_LIMIT),
        cost_estimate=pl.CostEstimate(
            flops=heads * pairs * 10 * 256 + 2 * length * depth * 3 * width,
            bytes_accessed=16 << 20,
            transcendentals=heads * pairs,
        ),
        name="attend_backward",
    )(
        places.tensor_places,
        places.dp_places,
        jnp.array(opened, jnp.int32),
        jnp.array(edges, jnp.int32),
        *grads,
        queries,
        keys,
        values,
        mixture,
        logsum,
        seg_column,
        seg_row,
        *pieces,
    )


def local(
    layer_input,
    segment_ids,
    ln_attn_gain,
    w_query,
    w_key,
    w_value,
    head_scale,
    w_out,
    ln_post_gain,
    ln_ffn_gain,
    w_up,
    ln_mid_gain,
    w_down,
    out_cotangent,
):
    places = Places()
    tensor_size = places.tensor_size
    tensor_order = places.tensor_order
    tensor_masks = places.tensor_masks
    local_heads = H // tensor_size
    width = local_heads * HD
    parts = range(tensor_size)

    seg_row = segment_ids[0][None, :]
    seg_column = segment_ids[0][:, None]
    prompt = jnp.zeros((PROMPT,), jnp.int32)
    long_row = jnp.concatenate([prompt, segment_ids[0]])[None, :]
    long_column = jnp.concatenate([prompt, segment_ids[0]])[:, None]

    attn_shards, matrix_set = [], []
    for layer in range(LAYERS):
        packed = jnp.concatenate([w_query[layer], w_key[layer], w_value[layer]], axis=1)
        attn_shards.append(packed.astype(BF16))
        packed = jnp.concatenate([w_up[layer], w_down[layer].T, w_out[layer].T], axis=1)
        packed = packed.astype(BF16)
        whole = lax.all_gather(packed, ("dp", "tensor"), axis=0, tiled=False)
        matrix_set.append(whole.reshape(places.dp_size, tensor_size, *packed.shape))
    attn_set = [gather_near(gather_far(attn_shards[0], places), places)]

    def exchange(blocks):
        return [
            block if at == 0 else swap(block, "tensor", tensor_order[at])
            for at, block in enumerate(blocks)
        ]

    stream = layer_input
    normed_one, _ = normalize(stream)
    h_attn = (normed_one * ln_attn_gain[0]).astype(BF16)
    saved = []
    for layer in range(LAYERS):
        last = layer == LAYERS - 1
        h_parts = gather_tensor([h_attn], tensor_masks)
        scale_all = head_scale[layer].reshape(tensor_size, local_heads)
        scale_rel = jnp.repeat(scale_all[places.tensor_places], HD, axis=1)
        queries, keys, values, mixture, logsum, *a_parts = attend_forward(
            places, h_parts, attn_set[layer], seg_column, seg_row, scale_rel[:1]
        )
        a_parts = exchange(a_parts)
        if not last:
            shard, _ = lax.optimization_barrier((attn_shards[layer + 1], h_parts))
            pieces = gather_near(gather_far(shard, places), places)
            a_parts, pieces = lax.optimization_barrier((a_parts, pieces))
            attn_set.append(pieces)
        gain_mid = ln_mid_gain[layer].reshape(tensor_size, -1)[places.tensor_places]
        stream_in = stream
        attn_out, middle, stream, h_ffn, mean, factor, pre, h_mid, *h_next = ffn_forward(
            places, stream, a_parts, matrix_set[layer], ln_post_gain[layer], ln_ffn_gain[layer],
            gain_mid, ln_attn_gain[(layer + 1) % LAYERS], last,
        )
        if not last:
            h_attn = h_next[0]
        saved.append(
            (
                stream_in, h_parts, queries, keys, values, mixture, logsum, scale_rel, a_parts,
                attn_out, middle, h_ffn, mean, factor, gain_mid, pre, h_mid,
            )
        )

    grad_stream = out_cotangent
    matrix_grads = [None] * LAYERS
    small_grads = [None] * LAYERS
    core_hop = ("tensor", tensor_masks[-1])
    side_hops = [("tensor", mask) for mask in reversed(tensor_masks[:-1])]
    near_hop = ("dp", places.near_mask)
    for layer in reversed(range(LAYERS)):
        (
            stream_in, h_parts, queries, keys, values, mixture, logsum, scale_rel, a_parts,
            attn_out, middle, h_ffn, mean, factor, gain_mid, pre, h_mid,
        ) = saved[layer]
        if layer == 0:
            down_keep, down_send = down_grads(places, grad_stream, h_mid)
            grad_stream, down_keep, down_send = lax.optimization_barrier(
                (grad_stream, down_keep, down_send)
            )
            down_arrived = swap(down_send, *core_hop)
        grad_low, grad_middle, grad_out, *rest = ffn_backward(
            places, grad_stream, attn_out, middle, mean, factor, pre, matrix_set[layer],
            ln_post_gain[layer], ln_ffn_gain[layer], gain_mid, scale_rel,
        )
        if layer == 0:
            rest, down_arrived, above = lax.optimization_barrier(
                (rest, down_arrived, matrix_grads[1][:3])
            )
            matrix_grads[1] = above + matrix_grads[1][3:]
        dout_parts = exchange(rest[:tensor_size])
        grad_pre, mid_sum, ffn_sum, post_sum = rest[tensor_size:]
        wide = h_mid.shape[2]
        if layer > 0:
            whole = whole_grads(places, grad_low, h_ffn, grad_out, grad_pre, h_mid, a_parts)
            dout_parts, whole = lax.optimization_barrier((dout_parts, whole))
            whole = whole.reshape(-1, *whole.shape[2:])
            rows = lax.psum_scatter(whole, ("dp", "tensor"), scatter_dimension=0, tiled=False)
            rows = rows.astype(F32)
            up_rows, down_rows, out_rows = (
                rows[:, :wide], rows[:, wide : 2 * wide], rows[:, 2 * wide :]
            )
        else:
            up_keep, up_send = up_grads(places, h_ffn, grad_out, grad_pre, a_parts)
            ups = add_halves(up_keep, swap(up_send, *core_hop))
            downs = add_halves(down_keep, down_arrived)
            dout_parts, ups, downs = lax.optimization_barrier((dout_parts, ups, downs))
            side_arrived = swap(ups[1], *side_hops[0])
            near_arrived = swap(downs[1], *near_hop)
        packed, inner_sum, keep, send = attend_backward(
            places, dout_parts, queries, keys, values, mixture, logsum, long_column, long_row,
            attn_set[layer],
        )
        if layer == 0:
            send, side_arrived, near_arrived = lax.optimization_barrier(
                (send, side_arrived, near_arrived)
            )
            ups = split_add(ups[0], side_arrived)
            downs = split_add(downs[0], near_arrived)
        grad_head = jnp.sum(inner_sum[:local_heads], 1) / scale_rel[0, ::HD]
        arrived = swap(send, *core_hop)
        if layer == 0:
            packed, arrived, ups, downs = lax.optimization_barrier((packed, arrived, ups, downs))
        for hop in side_hops:
            keep, send = add_halves(keep, arrived)
            arrived = swap(send, *hop)
        attn_keep, attn_send = attn_grads(places, h_parts, packed)
        attn_arrived = swap(attn_send, *near_hop)
        if layer > 0:
            arrived, attn_arrived = lax.optimization_barrier((arrived, attn_arrived))
        grad_h = (keep.astype(F32) + arrived.astype(F32)).reshape(stream_in.shape)
        normed_one, factor_one = normalize(stream_in)
        grad_attn_gain = jnp.sum(grad_h * normed_one, 0)
        grad_stream = grad_middle + norm_back(
            grad_h * ln_attn_gain[layer], normed_one, factor_one
        )
        attn_rows = scatter_rest(attn_keep, attn_arrived, places.far_hops)
        if layer == 0:
            hops = side_hops[1:] + [near_hop] + places.far_hops
            upper_rows = scatter_rest(ups[0], swap(ups[1], *hops[0]), hops[1:])
            up_rows, out_rows = upper_rows[:, :wide], upper_rows[:, wide:]
            hops = side_hops + places.far_hops
            down_rows = scatter_rest(downs[0], swap(downs[1], *hops[0]), hops[1:])
        matrix_grads[layer] = (
            attn_rows[:, :width],
            attn_rows[:, width : 2 * width],
            attn_rows[:, 2 * width :],
            out_rows.T,
            up_rows,
            down_rows.T,
        )
        grad_head_all = lax.dynamic_update_slice_in_dim(
            jnp.zeros((H,), F32), grad_head, places.tensor_index * local_heads, 0
        )
        grad_mid_all = jnp.sum(mid_sum, 1)[places.tensor_sources].reshape(-1)
        small_grads[layer] = (
            grad_attn_gain, grad_head_all, jnp.sum(post_sum, 0), jnp.sum(ffn_sum, 0),
            grad_mid_all,
        )
    sizes = [part.shape[0] for part in small_grads[0]]
    vector = jnp.concatenate([part for layer in range(LAYERS) for part in small_grads[layer]])
    count = vector.shape[0]
    vector = jnp.pad(vector, (0, -count % 1024)).reshape(-1, 128)
    vector = sum_everywhere(vector).reshape(-1)
    smalls, start = [], 0
    for layer in range(LAYERS):
        found = []
        for size in sizes:
            found.append(lax.slice_in_dim(vector, start, start + size))
            start += size
        smalls.append(found)
    small = [jnp.stack([smalls[layer][at] for layer in range(LAYERS)]) for at in range(5)]
    stacked = [
        jnp.stack([matrix_grads[layer][at] for layer in range(LAYERS)]) for at in range(6)
    ]
    return (
        stream, grad_stream, small[0], stacked[0], stacked[1], stacked[2], small[1], stacked[3],
        small[2], small[3], stacked[4], small[4], stacked[5],
    )


def solution(mesh):
    rows = P(("dp", "tensor"), None)
    first = P(None, "dp", "tensor")
    second = P(None, "tensor", "dp")
    in_specs = (
        rows, P("dp", None), P(), first, first, first, P(), second, P(), P(), first, P(), second,
        rows,
    )
    out_specs = (
        rows, rows, P(), first, first, first, P(), second, P(), P(), first, P(), second,
    )
    return jax.shard_map(local, mesh=mesh, in_specs=in_specs, out_specs=out_specs, check_vma=False)
```

```python
import functools

import jax
import jax.numpy as jnp
from jax import lax
from jax.experimental import pallas as pl
from jax.experimental.pallas import tpu as pltpu
from jax.sharding import PartitionSpec as P

H = 16
HD = 64
LAYERS = 2
PROMPT = 1024
BLOCK = 512

NORM_EPSILON = 1e-05
MASKED_SCORE = -1e30
F32 = jnp.float32
BF16 = jnp.bfloat16
VMEM_LIMIT = 67_000_000


def tanh_gelu(inputs):
    return (
        0.5
        * inputs
        * (1.0 + jnp.tanh(0.7978845608028654 * (inputs + 0.044715 * inputs * inputs * inputs)))
    )


def normalize(values):
    center = values - jnp.mean(values, -1, keepdims=True)
    factor = lax.rsqrt(jnp.mean(center * center, -1, keepdims=True) + NORM_EPSILON)
    return (center * factor, factor)


def norm_back(grad_norm, normed, factor):
    return factor * (
        grad_norm
        - jnp.mean(grad_norm, -1, keepdims=True)
        - normed * jnp.mean(grad_norm * normed, -1, keepdims=True)
    )


def dot_nn(left, right):
    return lax.dot_general(left, right, (((1,), (0,)), ((), ())), preferred_element_type=F32)


def dot_tn(left, right):
    return lax.dot_general(left, right, (((0,), (0,)), ((), ())), preferred_element_type=F32)


def dot_nt(left, right):
    return lax.dot_general(left, right, (((1,), (1,)), ((), ())), preferred_element_type=F32)


def bit_masks(size):
    masks = []
    while size > 1:
        size //= 2
        masks.append(size)
    return masks


def relative_order(masks):
    order = [0]
    for mask in masks:
        order = order + [mask | other for other in order]
    return order


def swap(array, axis, mask):
    size = lax.axis_size(axis)
    return lax.ppermute(array, axis, [(i, i ^ mask) for i in range(size)])


class Places:
    def __init__(self):
        self.dp_size = lax.axis_size("dp")
        self.tensor_size = lax.axis_size("tensor")
        dp_index = lax.axis_index("dp").astype(jnp.int32)
        self.tensor_index = lax.axis_index("tensor").astype(jnp.int32)
        self.tensor_masks = bit_masks(self.tensor_size)
        masks = bit_masks(self.dp_size)
        self.far_masks = relative_order(masks[:-1])
        self.near_mask = masks[-1]
        self.far_hops = [("dp", mask) for mask in reversed(masks[:-1])]
        dp_order = self.far_masks + [mask | self.near_mask for mask in self.far_masks]
        self.tensor_order = relative_order(self.tensor_masks)
        tensor_inverse = [self.tensor_order.index(i) for i in range(self.tensor_size)]
        self.dp_places = jnp.array(dp_order, jnp.int32) ^ dp_index
        self.tensor_places = jnp.array(self.tensor_order, jnp.int32) ^ self.tensor_index
        spots = jnp.arange(self.tensor_size, dtype=jnp.int32) ^ self.tensor_index
        self.tensor_sources = jnp.array(tensor_inverse, jnp.int32)[spots]


def gather_far(shard, places):
    others = [swap(shard, "dp", mask) for mask in places.far_masks[1:]]
    return jnp.stack([shard] + others)


def gather_near(part, places):
    return [part, swap(part, "dp", places.near_mask)]


def gather_tensor(parts, masks):
    for mask in masks:
        parts = parts + [jax.tree.map(lambda x, m=mask: swap(x, "tensor", m), p) for p in parts]
    return parts


def gather_late_tensor(shard, places):
    pieces = gather_near(gather_far(shard, places), places)
    return gather_tensor([pieces], places.tensor_masks)


def gather_late_near(shard, places):
    parts = gather_tensor([gather_far(shard, places)], places.tensor_masks[:-1])
    pieces = [gather_near(part, places) for part in parts]
    return gather_tensor(pieces, places.tensor_masks[-1:])


def add_low(kept, arrived):
    return (kept.astype(F32) + arrived.astype(F32)).astype(BF16)


def add_halves(kept, arrived):
    half = kept.shape[0] // 2
    return add_low(kept[:half], arrived[:half]), add_low(kept[half:], arrived[half:])


def split_add(kept, arrived):
    while kept.shape[0] == 1:
        kept, arrived = kept[0], arrived[0]
    return add_halves(kept, arrived)


def scatter_rest(kept, arrived, hops):
    for hop in hops:
        kept, sent = split_add(kept, arrived)
        arrived = swap(sent, *hop)
    total = kept.astype(F32) + arrived.astype(F32)
    return total.reshape(total.shape[-2:])


def sum_everywhere(vector):
    for axis in ("tensor", "dp"):
        for mask in reversed(bit_masks(lax.axis_size(axis))):
            vector = vector + swap(vector, axis, mask)
    return vector


def block_rows(place_ref, at, rows):
    return pl.ds(pl.multiple_of(place_ref[at] * rows, rows), rows)


def start_rows(spot, blocks, columns, target, semaphore):
    count, _, rows, _ = blocks.shape
    for at in range(count):
        pltpu.make_async_copy(
            blocks.at[at, spot, :, columns], target.at[at * rows : (at + 1) * rows, :], semaphore
        ).start()


def wait_whole(target, semaphore):
    pltpu.make_async_copy(target, target, semaphore).wait()


def each_rows(total, chunk, body):
    for start in range(0, total, chunk):
        body(pl.ds(start, chunk))


def lanes(values, width):
    return jnp.concatenate([values] * (width // 128), axis=1)


def fold_lanes(values):
    total = values[:, :128]
    for lane in range(128, values.shape[1], 128):
        total = total + values[:, lane : lane + 128]
    return total


def fold_rows(values):
    return jnp.sum(values.reshape(values.shape[0] // 8, 8, values.shape[1]), axis=0)


CHUNK = 16


def ffn_forward_kernel(parts, last, place_ref, *refs):
    refs = list(refs)

    def take(count):
        taken = refs[:count]
        del refs[:count]
        return taken

    (stream_ref,) = take(1)
    a_refs = take(parts)
    (matrix_ref,) = take(1)
    post_ref, ffn_ref, mid_ref, next_ref = take(4)
    out_ref, middle_ref, next_stream_ref, h_ffn_ref, mean_ref, factor_ref = take(6)
    pre_ref, h_mid_ref = take(2)
    h_next_ref = None if last else take(1)[0]
    w_up, w_out, w_down, active, pre_buf, mid_buf, sums, squares = take(8)
    up_sem, out_sem, down_sem, pre_sem, mid_sem = take(5)
    rows, depth = stream_ref.shape
    wide = w_up.shape[2]
    narrow = w_out.shape[2]
    hidden = parts * wide

    up_columns, down_columns = pl.ds(0, wide), pl.ds(wide, wide)
    out_columns = pl.ds(2 * wide, narrow)
    for at in range(parts):
        start_rows(place_ref[at], matrix_ref, out_columns, w_out.at[at], out_sem)
    for at in range(parts):
        start_rows(place_ref[at], matrix_ref, up_columns, w_up.at[at], up_sem.at[at])
    for at in range(parts):
        start_rows(place_ref[at], matrix_ref, down_columns, w_down.at[at], down_sem.at[at])
    wait_whole(w_out, out_sem)
    out_ref[...] = sum(dot_nt(a_refs[at][...], w_out[at]) for at in range(parts))

    def middle_rows(here):
        normed, _ = normalize(out_ref[here, :])
        middle = stream_ref[here, :] + normed * post_ref[...]
        middle_ref[here, :] = middle
        normed, _ = normalize(middle)
        h_ffn_ref[here, :] = (normed * ffn_ref[...]).astype(BF16)

    each_rows(rows, CHUNK, middle_rows)
    sums[...] = jnp.zeros_like(sums)
    squares[...] = jnp.zeros_like(squares)

    def write_pre(at):
        return pltpu.make_async_copy(pre_buf.at[at % 2], pre_ref.at[at], pre_sem.at[at % 2])

    def write_mid(at):
        return pltpu.make_async_copy(mid_buf.at[at % 2], h_mid_ref.at[at], mid_sem.at[at % 2])

    wait_whole(w_up.at[0], up_sem.at[0])
    pre_buf[0] = dot_nn(h_ffn_ref[...], w_up[0])
    for at in range(parts):
        write_pre(at).start()
        if at + 1 < parts:
            wait_whole(w_up.at[at + 1], up_sem.at[at + 1])
            if at >= 1:
                write_pre(at - 1).wait()
            pre_buf[(at + 1) % 2] = dot_nn(h_ffn_ref[...], w_up[at + 1])

        def active_rows(here, at=at):
            value = tanh_gelu(pre_buf[at % 2, here, :])
            active[at, here, :] = value
            sums[here, :] += fold_lanes(value)
            squares[here, :] += fold_lanes(value * value)

        each_rows(rows, CHUNK, active_rows)
    mean = jnp.sum(sums[...], axis=1, keepdims=True) / hidden
    spread = jnp.sum(squares[...], axis=1, keepdims=True) / hidden - mean * mean
    mean_ref[...] = jnp.broadcast_to(mean, mean_ref.shape)
    factor_ref[...] = jnp.broadcast_to(lax.rsqrt(spread + NORM_EPSILON), factor_ref.shape)

    def mid_part(at):
        def mid_rows(here):
            normed = active[at, here, :] - lanes(mean_ref[here, :], wide)
            normed = normed * lanes(factor_ref[here, :], wide)
            mid_buf[at % 2, here, :] = (normed * mid_ref[at : at + 1, :]).astype(BF16)

        each_rows(rows, CHUNK, mid_rows)

    mid_part(0)
    for at in range(parts):
        write_mid(at).start()
        wait_whole(w_down.at[at], down_sem.at[at])
        if 1 <= at < parts - 1:
            write_mid(at - 1).wait()
        product = dot_nt(mid_buf[at % 2], w_down[at])
        if at == 0:
            next_stream_ref[...] = middle_ref[...] + product
        else:
            next_stream_ref[...] += product
        if at + 1 < parts:
            mid_part(at + 1)
    if not last:

        def next_rows(here):
            normed, _ = normalize(next_stream_ref[here, :])
            h_next_ref[here, :] = (normed * next_ref[...]).astype(BF16)

        each_rows(rows, CHUNK, next_rows)
    for at in range(max(parts - 2, 0), parts):
        write_pre(at).wait()
        write_mid(at).wait()


def ffn_forward(places, stream, a_parts, matrices, post, ffn, mid, following, last):
    rows, depth = stream.shape
    parts, wide = mid.shape
    narrow = a_parts[0].shape[1]
    vmem = pl.BlockSpec(memory_space=pltpu.VMEM)
    hbm = pl.BlockSpec(memory_space=pl.ANY)
    full = jax.ShapeDtypeStruct((rows, depth), F32)
    low = jax.ShapeDtypeStruct((rows, depth), BF16)
    stat = jax.ShapeDtypeStruct((rows, 128), F32)
    outs = [full, full, full, low, stat, stat] + [
        jax.ShapeDtypeStruct((parts, rows, wide), F32),
        jax.ShapeDtypeStruct((parts, rows, wide), BF16),
    ]
    out_specs = [vmem] * 6 + [hbm] * 2
    if not last:
        outs, out_specs = outs + [low], out_specs + [vmem]
    dma = pltpu.SemaphoreType.DMA
    return pl.pallas_call(
        functools.partial(ffn_forward_kernel, parts, last),
        in_specs=[pl.BlockSpec(memory_space=pltpu.SMEM)]
        + [vmem] * (1 + parts)
        + [hbm]
        + [vmem] * 4,
        out_specs=out_specs,
        out_shape=outs,
        scratch_shapes=[
            pltpu.VMEM((parts, depth, wide), BF16),
            pltpu.VMEM((parts, depth, narrow), BF16),
            pltpu.VMEM((parts, depth, wide), BF16),
            pltpu.VMEM((parts, rows, wide), F32),
            pltpu.VMEM((2, rows, wide), F32),
            pltpu.VMEM((2, rows, wide), BF16),
            pltpu.VMEM((rows, 128), F32),
            pltpu.VMEM((rows, 128), F32),
            dma((parts,)),
            dma,
            dma((parts,)),
            dma((2,)),
            dma((2,)),
        ],
        compiler_params=pltpu.CompilerParams(vmem_limit_bytes=VMEM_LIMIT),
        cost_estimate=pl.CostEstimate(
            flops=2 * rows * depth * parts * (2 * wide + narrow),
            bytes_accessed=40 << 20,
            transcendentals=rows * parts * wide,
        ),
        name="ffn_forward",
    )(
        places.tensor_places,
        stream,
        *a_parts,
        matrices,
        post[None],
        ffn[None],
        mid,
        following[None],
    )


def ffn_backward_kernel(parts, place_ref, *refs):
    refs = list(refs)

    def take(count):
        taken = refs[:count]
        del refs[:count]
        return taken

    grad_ref, out_ref, middle_ref, mean_ref, factor_ref, pre_ref = take(6)
    (matrix_ref,) = take(1)
    post_ref, ffn_ref, mid_ref, scale_ref = take(4)
    low_ref, grad_middle_ref, grad_out_ref = take(3)
    dout_refs = take(parts)
    grad_pre_ref, mid_sum_ref, ffn_sum_ref, post_sum_ref = take(4)
    weights, w_out, grad_normed, normed_four, slope, pre_buf, product, low_buf = take(8)
    first, second = take(2)
    weight_sem, out_sem, pre_sem, low_sem = take(4)
    rows, depth = grad_ref.shape
    wide = weights.shape[2]
    narrow = w_out.shape[2]
    hidden = parts * wide

    def read_pre(at):
        return pltpu.make_async_copy(pre_ref.at[at], pre_buf.at[at % 2], pre_sem.at[at % 2])

    up_columns, down_columns = pl.ds(0, wide), pl.ds(wide, wide)
    out_columns = pl.ds(2 * wide, narrow)
    for at in range(parts):
        start_rows(place_ref[at], matrix_ref, down_columns, weights.at[at], weight_sem.at[at])
        if at < 2:
            read_pre(at).start()
    for at in range(parts):
        start_rows(place_ref[at], matrix_ref, out_columns, w_out.at[at], out_sem)
    low_ref[...] = grad_ref[...].astype(BF16)
    first[...] = jnp.zeros_like(first)
    second[...] = jnp.zeros_like(second)
    mid_sum_ref[...] = jnp.zeros_like(mid_sum_ref)
    ffn_sum_ref[...] = jnp.zeros_like(ffn_sum_ref)
    post_sum_ref[...] = jnp.zeros_like(post_sum_ref)
    wait_whole(weights.at[0], weight_sem.at[0])
    product[0] = dot_nn(low_ref[...], weights[0])
    for at in range(parts):
        start_rows(place_ref[at], matrix_ref, up_columns, weights.at[at], weight_sem.at[at])
        read_pre(at).wait()
        if at + 1 < parts:
            wait_whole(weights.at[at + 1], weight_sem.at[at + 1])
            product[(at + 1) % 2] = dot_nn(low_ref[...], weights[at + 1])

        def hidden_rows(here, at=at):
            value = pre_buf[at % 2, here, :]
            squared = value * value
            bend = jnp.tanh(value * (0.7978845608028654 + 0.035677408136300125 * squared))
            raised = 0.5 + 0.5 * bend
            normed = value * raised - lanes(mean_ref[here, :], wide)
            normed = normed * lanes(factor_ref[here, :], wide)
            steep = value * (0.7978845608028654 + 0.10703222440890037 * squared)
            slope[at, here, :] = raised + 0.5 * steep * (1.0 - bend * bend)
            normed_four[at, here, :] = normed.astype(BF16)
            grad = product[at % 2, here, :]
            mid_sum_ref[at] += fold_rows(grad * normed)
            grad = grad * mid_ref[at : at + 1, :]
            grad_normed[at, here, :] = grad
            first[here, :] += fold_lanes(grad)
            second[here, :] += fold_lanes(grad * normed)

        each_rows(rows, CHUNK, hidden_rows)
        if at + 2 < parts:
            read_pre(at + 2).start()
    first[...] = jnp.broadcast_to(
        jnp.sum(first[...], axis=1, keepdims=True) / hidden, first.shape
    )
    second[...] = jnp.broadcast_to(
        jnp.sum(second[...], axis=1, keepdims=True) / hidden, second.shape
    )

    def write_low(at):
        return pltpu.make_async_copy(low_buf.at[at % 2], grad_pre_ref.at[at], low_sem.at[at % 2])

    def low_part(at):
        def pre_rows(here):
            normed = normed_four[at, here, :].astype(F32)
            grad = grad_normed[at, here, :] - lanes(first[here, :], wide)
            grad = grad - normed * lanes(second[here, :], wide)
            grad = grad * slope[at, here, :] * lanes(factor_ref[here, :], wide)
            low_buf[at % 2, here, :] = grad.astype(BF16)

        each_rows(rows, CHUNK, pre_rows)

    low_part(0)
    for at in range(parts):
        write_low(at).start()
        wait_whole(weights.at[at], weight_sem.at[at])
        if 1 <= at < parts - 1:
            write_low(at - 1).wait()
        part = dot_nt(low_buf[at % 2], weights[at])
        if at == 0:
            product[0] = part
        else:
            product[0] += part
        if at + 1 < parts:
            low_part(at + 1)

    def middle_rows(here):
        grad = product[0, here, :]
        normed, factor = normalize(middle_ref[here, :])
        ffn_sum_ref[...] += fold_rows(grad * normed)
        grad = grad_ref[here, :] + norm_back(grad * ffn_ref[...], normed, factor)
        grad_middle_ref[here, :] = grad
        normed, factor = normalize(out_ref[here, :])
        post_sum_ref[...] += fold_rows(grad * normed)
        grad_out_ref[here, :] = norm_back(grad * post_ref[...], normed, factor).astype(BF16)

    each_rows(rows, CHUNK, middle_rows)
    wait_whole(w_out, out_sem)
    for at in range(parts):
        grad = dot_nn(grad_out_ref[...], w_out[at])
        dout_refs[at][...] = (grad * scale_ref[at : at + 1, :]).astype(BF16)
    for at in range(max(parts - 2, 0), parts):
        write_low(at).wait()


def ffn_backward(places, grad, out, middle, mean, factor, pre, matrices, post, ffn, mid, scale):
    rows, depth = grad.shape
    parts, wide = mid.shape
    narrow = scale.shape[1]
    vmem = pl.BlockSpec(memory_space=pltpu.VMEM)
    hbm = pl.BlockSpec(memory_space=pl.ANY)
    low = jax.ShapeDtypeStruct((rows, depth), BF16)
    sums = jax.ShapeDtypeStruct((8, depth), F32)
    dma = pltpu.SemaphoreType.DMA
    return pl.pallas_call(
        functools.partial(ffn_backward_kernel, parts),
        in_specs=[pl.BlockSpec(memory_space=pltpu.SMEM)]
        + [vmem] * 5
        + [hbm] * 2
        + [vmem] * 4,
        out_specs=[vmem] * (3 + parts) + [hbm] + [vmem] * 3,
        out_shape=[low, jax.ShapeDtypeStruct((rows, depth), F32), low]
        + [jax.ShapeDtypeStruct((rows, narrow), BF16)] * parts
        + [
            jax.ShapeDtypeStruct((parts, rows, wide), BF16),
            jax.ShapeDtypeStruct((parts, 8, wide), F32),
            sums,
            sums,
        ],
        scratch_shapes=[
            pltpu.VMEM((parts, depth, wide), BF16),
            pltpu.VMEM((parts, depth, narrow), BF16),
            pltpu.VMEM((parts, rows, wide), F32),
            pltpu.VMEM((parts, rows, wide), BF16),
            pltpu.VMEM((parts, rows, wide), F32),
            pltpu.VMEM((2, rows, wide), F32),
            pltpu.VMEM((2, rows, depth), F32),
            pltpu.VMEM((2, rows, wide), BF16),
            pltpu.VMEM((rows, 128), F32),
            pltpu.VMEM((rows, 128), F32),
            dma((parts,)),
            dma,
            dma((2,)),
            dma((2,)),
        ],
        compiler_params=pltpu.CompilerParams(vmem_limit_bytes=VMEM_LIMIT),
        cost_estimate=pl.CostEstimate(
            flops=2 * rows * depth * parts * (2 * wide + narrow),
            bytes_accessed=44 << 20,
            transcendentals=rows * parts * wide,
        ),
        name="ffn_backward",
    )(
        places.tensor_places,
        grad,
        out,
        middle,
        mean,
        factor,
        pre,
        matrices,
        post[None],
        ffn[None],
        mid,
        scale,
    )


def turned(place_ref, source, plain, target, rows):
    plain[...] = source[...].astype(BF16).astype(F32).T.astype(BF16)
    for at in range(target.shape[0] // rows):
        target[at * rows : (at + 1) * rows, :] = plain[block_rows(place_ref, at, rows), :]


def up_grads_kernel(parts, place_ref, *refs):
    h_ffn_ref, grad_out_ref, grad_pre_ref, a_ref, keep_ref, send_ref = refs[:6]
    h_turned, out_turned, h_plain, out_plain = refs[6:]
    step = pl.program_id(0)
    count, rows = keep_ref.shape[2:4]
    wide = grad_pre_ref.shape[2]

    @pl.when(step == 0)
    def _():
        turned(place_ref, h_ffn_ref, h_plain, h_turned, rows)
        turned(place_ref, grad_out_ref, out_plain, out_turned, rows)

    def fill(target):
        shape = (2, count, rows, -1)
        grad = dot_nn(h_turned[...], grad_pre_ref[0]).astype(BF16)
        target[0, :, :, :, :wide] = grad.reshape(shape)
        grad = dot_nn(out_turned[...], a_ref[0]).astype(BF16)
        target[0, :, :, :, wide:] = grad.reshape(shape)

    @pl.when(step < parts // 2)
    def _():
        fill(keep_ref)

    @pl.when(step >= parts // 2)
    def _():
        fill(send_ref)


def down_grads_kernel(parts, place_ref, *refs):
    grad_ref, h_mid_ref, keep_ref, send_ref, low_turned, low_plain = refs
    step = pl.program_id(0)
    count, rows = keep_ref.shape[2:4]

    @pl.when(step == 0)
    def _():
        turned(place_ref, grad_ref, low_plain, low_turned, rows)

    def fill(target):
        grad = dot_nn(low_turned[...], h_mid_ref[0]).astype(BF16)
        target[:, 0] = grad.reshape(2, count, rows, -1)

    @pl.when(step < parts // 2)
    def _():
        fill(keep_ref)

    @pl.when(step >= parts // 2)
    def _():
        fill(send_ref)


def split_grads(kernel, name, places, turns, sides, block, outside, at_part):
    parts, rows, _ = sides[0].shape
    depth = turns[0].shape[1]
    half = parts // 2
    columns = sum(side.shape[2] for side in sides)
    whole = pl.BlockSpec((rows, depth), lambda i, place: (0, 0))
    return pl.pallas_call(
        functools.partial(kernel, parts),
        grid_spec=pltpu.PrefetchScalarGridSpec(
            num_scalar_prefetch=1,
            grid=(parts,),
            in_specs=[whole] * len(turns)
            + [pl.BlockSpec((1,) + side.shape[1:], lambda i, place: (i, 0, 0)) for side in sides],
            out_specs=[
                pl.BlockSpec(block, lambda i, place: at_part(jnp.minimum(i, half - 1))),
                pl.BlockSpec(block, lambda i, place: at_part(jnp.maximum(i - half, 0))),
            ],
            scratch_shapes=[pltpu.VMEM((depth, rows), BF16)] * (2 * len(turns)),
        ),
        out_shape=[jax.ShapeDtypeStruct(outside, BF16)] * 2,
        compiler_params=pltpu.CompilerParams(vmem_limit_bytes=VMEM_LIMIT),
        cost_estimate=pl.CostEstimate(
            flops=2 * rows * depth * parts * columns,
            bytes_accessed=16 << 20,
            transcendentals=0,
        ),
        name=name,
    )(places.dp_places, *turns, *sides)


def up_grads(places, h_ffn, grad_out, grad_pre, a_parts):
    a_all = jnp.stack(a_parts)
    half = len(a_parts) // 2
    count = places.dp_size // 2
    tail = (count, h_ffn.shape[1] // places.dp_size, grad_pre.shape[2] + a_all.shape[2])
    return split_grads(
        up_grads_kernel, "up_grads", places, [h_ffn, grad_out], [grad_pre, a_all],
        (1, 2) + tail, (half, 2) + tail, lambda part: (part, 0, 0, 0, 0),
    )


def down_grads(places, grad, h_mid):
    half = h_mid.shape[0] // 2
    count = places.dp_size // 2
    tail = (count, grad.shape[1] // places.dp_size, h_mid.shape[2])
    return split_grads(
        down_grads_kernel, "down_grads", places, [grad], [h_mid],
        (2, 1) + tail, (2, half) + tail, lambda part: (0, part, 0, 0, 0),
    )


def whole_grads_kernel(parts, place_ref, *refs):
    del place_ref
    low_ref, h_ffn_ref, grad_out_ref, grad_pre_ref, h_mid_ref, a_ref, matrix_ref = refs[:7]
    low_turned, h_turned, out_turned = refs[7:]
    wide = h_mid_ref.shape[2]
    shape = matrix_ref.shape[:3] + (-1,)

    @pl.when(pl.program_id(0) == 0)
    def _():
        for source, target in (
            (low_ref, low_turned), (h_ffn_ref, h_turned), (grad_out_ref, out_turned)
        ):
            target[...] = source[...].astype(F32).T.astype(BF16)

    grad = dot_nn(h_turned[...], grad_pre_ref[0]).astype(BF16)
    matrix_ref[:, :, :, :wide] = grad.reshape(shape)
    grad = dot_nn(low_turned[...], h_mid_ref[0]).astype(BF16)
    matrix_ref[:, :, :, wide : 2 * wide] = grad.reshape(shape)
    grad = dot_nn(out_turned[...], a_ref[0]).astype(BF16)
    matrix_ref[:, :, :, 2 * wide :] = grad.reshape(shape)


def whole_grads(places, low, h_ffn, grad_out, grad_pre, h_mid, a_parts):
    rows, depth = low.shape
    parts, _, wide = h_mid.shape
    narrow = a_parts[0].shape[1]
    block = depth // places.dp_size
    columns = 2 * wide + narrow
    whole = pl.BlockSpec((rows, depth), lambda i, place: (0, 0))
    each = pl.BlockSpec((1, rows, wide), lambda i, place: (i, 0, 0))
    return pl.pallas_call(
        functools.partial(whole_grads_kernel, parts),
        grid_spec=pltpu.PrefetchScalarGridSpec(
            num_scalar_prefetch=1,
            grid=(parts,),
            in_specs=[whole] * 3
            + [each] * 2
            + [pl.BlockSpec((1, rows, narrow), lambda i, place: (i, 0, 0))],
            out_specs=pl.BlockSpec(
                (places.dp_size, 1, block, columns), lambda i, place: (0, place[i], 0, 0)
            ),
            scratch_shapes=[pltpu.VMEM((depth, rows), BF16)] * 3,
        ),
        out_shape=jax.ShapeDtypeStruct((places.dp_size, parts, block, columns), BF16),
        compiler_params=pltpu.CompilerParams(vmem_limit_bytes=VMEM_LIMIT),
        cost_estimate=pl.CostEstimate(
            flops=2 * rows * depth * parts * columns,
            bytes_accessed=30 << 20,
            transcendentals=0,
        ),
        name="whole_grads",
    )(places.tensor_places, low, h_ffn, grad_out, grad_pre, h_mid, jnp.stack(a_parts))


def attn_grads_kernel(parts, place_ref, *refs):
    h_refs = refs[:parts]
    packed_ref, keep_ref, send_ref, total = refs[parts:]
    count, rows, _ = keep_ref.shape
    tokens = packed_ref.shape[0] // parts
    for part in range(parts):
        flipped = h_refs[part][...].astype(F32).T.astype(BF16)
        grad = dot_nn(flipped, packed_ref[part * tokens : (part + 1) * tokens, :])
        if part == 0:
            total[...] = grad
        else:
            total[...] += grad
    for at in range(count):
        keep_ref[at] = total[block_rows(place_ref, at, rows), :].astype(BF16)
        send_ref[at] = total[block_rows(place_ref, count + at, rows), :].astype(BF16)


def attn_grads(places, h_parts, packed):
    parts = len(h_parts)
    tokens, depth = h_parts[0].shape
    columns = packed.shape[1]
    count = places.dp_size // 2
    block = depth // places.dp_size
    vmem = pl.BlockSpec(memory_space=pltpu.VMEM)
    return pl.pallas_call(
        functools.partial(attn_grads_kernel, parts),
        in_specs=[pl.BlockSpec(memory_space=pltpu.SMEM)] + [vmem] * (parts + 1),
        out_specs=[vmem] * 2,
        out_shape=[jax.ShapeDtypeStruct((count, block, columns), BF16)] * 2,
        scratch_shapes=[
            pltpu.VMEM((depth, columns), F32),
        ],
        compiler_params=pltpu.CompilerParams(vmem_limit_bytes=VMEM_LIMIT),
        cost_estimate=pl.CostEstimate(
            flops=2 * tokens * parts * depth * columns,
            bytes_accessed=8 << 20,
            transcendentals=0,
        ),
        name="attn_grads",
    )(places.dp_places, *h_parts, packed)


def half_mask(shape, head):
    lane = lax.broadcasted_iota(jnp.int32, shape, len(shape) - 1)
    return (lane // HD) == (head % 2)


def place_rows(place_ref, pieces, target):
    for half, piece in enumerate(pieces):
        count, rows, _ = piece.shape
        for at in range(count):
            target[block_rows(place_ref, half * count + at, rows), :] = piece[at]


def forward_kernel(block_ref, place_ref, *refs):
    parts = block_ref.shape[0]
    rows_refs = refs[:parts]
    pieces = refs[parts : parts + 2]
    column_ref, row_ref, scale_ref = refs[parts + 2 : parts + 5]
    query_ref, key_ref, value_ref, mixture_ref, logsum_ref = refs[parts + 5 : parts + 10]
    scaled_refs = refs[parts + 10 : -2]
    score_ref, weight_ref = refs[-2:]
    width = query_ref.shape[1]
    length = query_ref.shape[0]
    rows = length // parts

    place_rows(place_ref, pieces, weight_ref)
    for part in range(parts):
        at = pl.ds(pl.multiple_of(block_ref[part] * rows, rows), rows)
        packed = dot_nn(rows_refs[part][...], weight_ref[...])
        query_ref[at, :] = packed[:, :width].astype(BF16) * jnp.asarray(0.125, BF16)
        key_ref[at, :] = packed[:, width : 2 * width].astype(BF16)
        value_ref[at, :] = packed[:, 2 * width :].astype(BF16)

    for query_block in range(length // BLOCK):
        here = pl.ds(query_block * BLOCK, BLOCK)

        def one_head(head, logsums, query_block=query_block, here=here):
            lanes = pl.ds(pl.multiple_of((head // 2) * 128, 128), 128)
            own = half_mask((BLOCK, 128), head)
            query = jnp.where(own, query_ref[here, lanes], jnp.asarray(0, BF16))
            highest = jnp.full((BLOCK, 128), MASKED_SCORE, F32)
            for key_block in range(query_block + 1):
                there = pl.ds(key_block * BLOCK, BLOCK)
                scores = dot_nt(query, key_ref[there, lanes])
                if key_block == query_block or key_block * BLOCK >= PROMPT:
                    first = lax.broadcasted_iota(jnp.int32, (BLOCK, BLOCK), 0)
                    second = lax.broadcasted_iota(jnp.int32, (BLOCK, BLOCK), 1)
                    seen = None
                    if key_block == query_block:
                        seen = second <= first
                    if key_block * BLOCK >= PROMPT:
                        query_at = pl.ds(query_block * BLOCK - PROMPT, BLOCK)
                        key_at = pl.ds(key_block * BLOCK - PROMPT, BLOCK)
                        same = column_ref[query_at, :] == row_ref[:, key_at]
                        seen = same if seen is None else seen & same
                    scores = jnp.where(seen, scores, MASKED_SCORE)
                score_ref[:, there] = scores
                for lane in range(0, BLOCK, 128):
                    highest = jnp.maximum(highest, scores[:, lane : lane + 128])
            top = jnp.max(highest, axis=1, keepdims=True)
            total = jnp.zeros((BLOCK, 128), F32)
            mixed = jnp.zeros((BLOCK, 128), F32)
            for key_block in range(query_block + 1):
                there = pl.ds(key_block * BLOCK, BLOCK)
                weights = jnp.exp(score_ref[:, there] - top)
                for lane in range(0, BLOCK, 128):
                    total = total + weights[:, lane : lane + 128]
                mixed = mixed + dot_nn(weights.astype(BF16), value_ref[there, lanes])
            denominator = jnp.sum(total, axis=1, keepdims=True)
            mixed = mixed / denominator
            mixture_ref[here, lanes] = jnp.where(own, mixed, mixture_ref[here, lanes])
            lane = lax.broadcasted_iota(jnp.int32, (BLOCK, 128), 1)
            return jnp.where(lane == head, top + jnp.log(denominator), logsums)

        logsums = lax.fori_loop(0, width // HD, one_head, jnp.zeros((BLOCK, 128), F32))
        logsum_ref[:, here] = logsums.T[: logsum_ref.shape[0], :]

    for part in range(parts):
        at = pl.ds(pl.multiple_of(block_ref[part] * rows, rows), rows)
        scaled_refs[part][...] = (mixture_ref[at, :] * scale_ref[...]).astype(BF16)


def attend_forward(places, rows, pieces, seg_column, seg_row, scale):
    parts = len(rows)
    length = parts * rows[0].shape[0]
    width = pieces[0].shape[2] // 3
    depth = rows[0].shape[1]
    heads = width // HD
    pairs = length * length * 5 // 8
    whole = pl.BlockSpec(memory_space=pltpu.VMEM)
    return pl.pallas_call(
        forward_kernel,
        in_specs=[pl.BlockSpec(memory_space=pltpu.SMEM)] * 2 + [whole] * (parts + 5),
        out_specs=[whole] * (5 + parts),
        out_shape=[jax.ShapeDtypeStruct((length, width), BF16)] * 3
        + [
            jax.ShapeDtypeStruct((length, width), F32),
            jax.ShapeDtypeStruct((8, length), F32),
        ]
        + [jax.ShapeDtypeStruct((length // parts, width), BF16)] * parts,
        scratch_shapes=[
            pltpu.VMEM((BLOCK, length), F32),
            pltpu.VMEM((depth, 3 * width), BF16),
        ],
        compiler_params=pltpu.CompilerParams(vmem_limit_bytes=VMEM_LIMIT),
        cost_estimate=pl.CostEstimate(
            flops=2 * length * depth * 3 * width + heads * pairs * 4 * 256,
            bytes_accessed=20 << 20,
            transcendentals=heads * pairs,
        ),
        name="attend_forward",
    )(places.tensor_places, places.dp_places, *rows, *pieces, seg_column, seg_row, scale)


def backward_kernel(block_ref, place_ref, open_ref, edge_ref, *refs):
    parts = block_ref.shape[0]
    grad_refs = refs[:parts]
    query_ref, key_ref, value_ref, mixture_ref, logsum_ref = refs[parts : parts + 5]
    column_ref, row_ref = refs[parts + 5 : parts + 7]
    pieces = refs[parts + 7 : parts + 9]
    packed_ref, inner_sum_ref, keep_ref, send_ref = refs[parts + 9 : parts + 13]
    dout_ref, inner_ref, dq_ref, dk_ref, dv_ref, weight_ref = refs[parts + 13 :]
    length, width = query_ref.shape
    rows = length // parts

    for part in range(parts):
        at = pl.ds(pl.multiple_of(block_ref[part] * rows, rows), rows)
        dout_ref[at, :] = grad_refs[part][...]
    picks = lax.broadcasted_iota(jnp.int32, (8, width), 1) // HD == lax.broadcasted_iota(
        jnp.int32, (8, width), 0
    )
    picks = jnp.where(picks, 1.0, 0.0)
    inner_sum = jnp.zeros((8, 128), F32)
    for part in range(length // BLOCK):
        at = pl.ds(part * BLOCK, BLOCK)
        product = dout_ref[at, :].astype(F32) * mixture_ref[at, :]
        inner = lax.dot_general(
            picks,
            product,
            (((1,), (1,)), ((), ())),
            precision=lax.Precision.HIGHEST,
            preferred_element_type=F32,
        )
        inner_ref[:, at] = inner
        for lane in range(0, BLOCK, 128):
            inner_sum = inner_sum + inner[:, lane : lane + 128]
    inner_sum_ref[...] = inner_sum
    dq_ref[...] = jnp.zeros_like(dq_ref)
    dk_ref[...] = jnp.zeros_like(dk_ref)
    dv_ref[...] = jnp.zeros_like(dv_ref)

    def one_pair(head, key_block, query_block, edge):
        lanes = pl.ds(pl.multiple_of((head // 2) * 128, 128), 128)
        there = pl.ds(pl.multiple_of(key_block * BLOCK, BLOCK), BLOCK)
        here = pl.ds(pl.multiple_of(query_block * BLOCK, BLOCK), BLOCK)
        own = half_mask((BLOCK, 128), head)
        none = jnp.asarray(0, BF16)
        query = jnp.where(own, query_ref[here, lanes], none)
        dout = jnp.where(own, dout_ref[here, lanes], none)
        key = key_ref[there, lanes]
        scores = dot_nt(key, query)
        weights = jnp.exp(scores - logsum_ref[pl.ds(head, 1), here])
        if edge:
            key_at = key_block * BLOCK + lax.broadcasted_iota(jnp.int32, (BLOCK, BLOCK), 0)
            query_at = query_block * BLOCK + lax.broadcasted_iota(jnp.int32, (BLOCK, BLOCK), 1)
            same = column_ref[there, :] == row_ref[:, here]
            weights = jnp.where((key_at <= query_at) & same, weights, 0.0)
        dv_ref[there, lanes] += dot_nn(weights.astype(BF16), dout)
        grad = dot_nt(value_ref[there, lanes], dout)
        grad = (weights * (grad - inner_ref[pl.ds(head, 1), here])).astype(BF16)
        dk_ref[there, lanes] += dot_nn(grad, query)
        dq_ref[here, lanes] += dot_tn(grad, jnp.where(own, key, none))

    def one_head(head, carry):
        def open_pair(at, inside):
            one_pair(head, open_ref[2 * at], open_ref[2 * at + 1], False)
            return inside

        def edge_pair(at, inside):
            one_pair(head, edge_ref[2 * at], edge_ref[2 * at + 1], True)
            return inside

        lax.fori_loop(0, open_ref.shape[0] // 2, open_pair, 0)
        lax.fori_loop(0, edge_ref.shape[0] // 2, edge_pair, 0)
        return carry

    lax.fori_loop(0, width // HD, one_head, 0)
    for part in range(parts):
        at = pl.ds(pl.multiple_of(block_ref[part] * rows, rows), rows)
        to = pl.ds(part * rows, rows)
        packed_ref[to, :width] = (dq_ref[at, :] * 0.125).astype(BF16)
        packed_ref[to, width : 2 * width] = dk_ref[at, :].astype(BF16)
        packed_ref[to, 2 * width :] = dv_ref[at, :].astype(BF16)
    place_rows(place_ref, pieces, weight_ref)
    for part in range(parts):
        grad = dot_nt(packed_ref[part * rows : (part + 1) * rows, :], weight_ref[...])
        half = parts // 2
        target = keep_ref if part < half else send_ref
        target[part % half] = grad.astype(BF16)


def attend_backward(
    places, grads, queries, keys, values, mixture, logsum, seg_column, seg_row, pieces
):
    parts = len(grads)
    length, width = queries.shape
    heads = width // HD
    depth = pieces[0].shape[0] * pieces[0].shape[1] * 2
    opened, edges = [], []
    for query_block in range(length // BLOCK):
        for key_block in range(query_block + 1):
            if key_block == query_block or key_block * BLOCK >= PROMPT:
                edges += [key_block, query_block]
            else:
                opened += [key_block, query_block]
    whole = pl.BlockSpec(memory_space=pltpu.VMEM)
    scalars = pl.BlockSpec(memory_space=pltpu.SMEM)
    pairs = length * length * 5 // 8
    return pl.pallas_call(
        backward_kernel,
        in_specs=[scalars] * 4 + [whole] * (parts + 9),
        out_specs=[whole] * 4,
        out_shape=[
            jax.ShapeDtypeStruct((length, 3 * width), BF16),
            jax.ShapeDtypeStruct((8, 128), F32),
            jax.ShapeDtypeStruct((parts // 2, length // parts, depth), BF16),
            jax.ShapeDtypeStruct((parts // 2, length // parts, depth), BF16),
        ],
        scratch_shapes=[
            pltpu.VMEM((length, width), BF16),
            pltpu.VMEM((8, length), F32),
            pltpu.VMEM((length, width), F32),
            pltpu.VMEM((length, width), F32),
            pltpu.VMEM((length, width), F32),
            pltpu.VMEM((depth, 3 * width), BF16),
        ],
        compiler_params=pltpu.CompilerParams(vmem_limit_bytes=VMEM_LIMIT),
        cost_estimate=pl.CostEstimate(
            flops=heads * pairs * 10 * 256 + 2 * length * depth * 3 * width,
            bytes_accessed=16 << 20,
            transcendentals=heads * pairs,
        ),
        name="attend_backward",
    )(
        places.tensor_places,
        places.dp_places,
        jnp.array(opened, jnp.int32),
        jnp.array(edges, jnp.int32),
        *grads,
        queries,
        keys,
        values,
        mixture,
        logsum,
        seg_column,
        seg_row,
        *pieces,
    )


def local(
    layer_input,
    segment_ids,
    ln_attn_gain,
    w_query,
    w_key,
    w_value,
    head_scale,
    w_out,
    ln_post_gain,
    ln_ffn_gain,
    w_up,
    ln_mid_gain,
    w_down,
    out_cotangent,
):
    places = Places()
    tensor_size = places.tensor_size
    tensor_order = places.tensor_order
    tensor_masks = places.tensor_masks
    local_heads = H // tensor_size
    width = local_heads * HD
    parts = range(tensor_size)

    seg_row = segment_ids[0][None, :]
    seg_column = segment_ids[0][:, None]
    prompt = jnp.zeros((PROMPT,), jnp.int32)
    long_row = jnp.concatenate([prompt, segment_ids[0]])[None, :]
    long_column = jnp.concatenate([prompt, segment_ids[0]])[:, None]

    attn_shards, matrix_set = [], []
    for layer in range(LAYERS):
        packed = jnp.concatenate([w_query[layer], w_key[layer], w_value[layer]], axis=1)
        attn_shards.append(packed.astype(BF16))
        packed = jnp.concatenate([w_up[layer], w_down[layer].T, w_out[layer].T], axis=1)
        packed = packed.astype(BF16)
        whole = lax.all_gather(packed, ("dp", "tensor"), axis=0, tiled=False)
        matrix_set.append(whole.reshape(places.dp_size, tensor_size, *packed.shape))
    attn_set = [gather_near(gather_far(attn_shards[0], places), places)]

    def exchange(blocks):
        return [
            block if at == 0 else swap(block, "tensor", tensor_order[at])
            for at, block in enumerate(blocks)
        ]

    stream = layer_input
    normed_one, _ = normalize(stream)
    h_attn = (normed_one * ln_attn_gain[0]).astype(BF16)
    saved = []
    for layer in range(LAYERS):
        last = layer == LAYERS - 1
        h_parts = gather_tensor([h_attn], tensor_masks)
        scale_all = head_scale[layer].reshape(tensor_size, local_heads)
        scale_rel = jnp.repeat(scale_all[places.tensor_places], HD, axis=1)
        queries, keys, values, mixture, logsum, *a_parts = attend_forward(
            places, h_parts, attn_set[layer], seg_column, seg_row, scale_rel[:1]
        )
        a_parts = exchange(a_parts)
        if not last:
            shard, _ = lax.optimization_barrier((attn_shards[layer + 1], logsum))
            pieces = gather_near(gather_far(shard, places), places)
            a_parts, pieces = lax.optimization_barrier((a_parts, pieces))
            attn_set.append(pieces)
        gain_mid = ln_mid_gain[layer].reshape(tensor_size, -1)[places.tensor_places]
        stream_in = stream
        attn_out, middle, stream, h_ffn, mean, factor, pre, h_mid, *h_next = ffn_forward(
            places, stream, a_parts, matrix_set[layer], ln_post_gain[layer], ln_ffn_gain[layer],
            gain_mid, ln_attn_gain[(layer + 1) % LAYERS], last,
        )
        if not last:
            h_attn = h_next[0]
        saved.append(
            (
                stream_in, h_parts, queries, keys, values, mixture, logsum, scale_rel, a_parts,
                attn_out, middle, h_ffn, mean, factor, gain_mid, pre, h_mid,
            )
        )

    grad_stream = out_cotangent
    matrix_grads = [None] * LAYERS
    small_grads = [None] * LAYERS
    core_hop = ("tensor", tensor_masks[-1])
    side_hops = [("tensor", mask) for mask in reversed(tensor_masks[:-1])]
    near_hop = ("dp", places.near_mask)
    for layer in reversed(range(LAYERS)):
        (
            stream_in, h_parts, queries, keys, values, mixture, logsum, scale_rel, a_parts,
            attn_out, middle, h_ffn, mean, factor, gain_mid, pre, h_mid,
        ) = saved[layer]
        if layer == 0:
            down_keep, down_send = down_grads(places, grad_stream, h_mid)
            grad_stream, down_keep, down_send = lax.optimization_barrier(
                (grad_stream, down_keep, down_send)
            )
            down_arrived = swap(down_send, *core_hop)
        grad_low, grad_middle, grad_out, *rest = ffn_backward(
            places, grad_stream, attn_out, middle, mean, factor, pre, matrix_set[layer],
            ln_post_gain[layer], ln_ffn_gain[layer], gain_mid, scale_rel,
        )
        if layer == 0:
            rest, down_arrived, above = lax.optimization_barrier(
                (rest, down_arrived, matrix_grads[1][:3])
            )
            matrix_grads[1] = above + matrix_grads[1][3:]
        dout_parts = exchange(rest[:tensor_size])
        grad_pre, mid_sum, ffn_sum, post_sum = rest[tensor_size:]
        wide = h_mid.shape[2]
        if layer > 0:
            whole = whole_grads(places, grad_low, h_ffn, grad_out, grad_pre, h_mid, a_parts)
            dout_parts, whole = lax.optimization_barrier((dout_parts, whole))
            whole = whole.reshape(-1, *whole.shape[2:])
            rows = lax.psum_scatter(whole, ("dp", "tensor"), scatter_dimension=0, tiled=False)
            rows = rows.astype(F32)
            up_rows, down_rows, out_rows = (
                rows[:, :wide], rows[:, wide : 2 * wide], rows[:, 2 * wide :]
            )
        else:
            up_keep, up_send = up_grads(places, h_ffn, grad_out, grad_pre, a_parts)
            ups = add_halves(up_keep, swap(up_send, *core_hop))
            downs = add_halves(down_keep, down_arrived)
            dout_parts, ups, downs = lax.optimization_barrier((dout_parts, ups, downs))
            side_arrived = swap(ups[1], *side_hops[0])
            near_arrived = swap(downs[1], *near_hop)
        packed, inner_sum, keep, send = attend_backward(
            places, dout_parts, queries, keys, values, mixture, logsum, long_column, long_row,
            attn_set[layer],
        )
        if layer == 0:
            send, side_arrived, near_arrived = lax.optimization_barrier(
                (send, side_arrived, near_arrived)
            )
            ups = split_add(ups[0], side_arrived)
            downs = split_add(downs[0], near_arrived)
        grad_head = jnp.sum(inner_sum[:local_heads], 1) / scale_rel[0, ::HD]
        arrived = swap(send, *core_hop)
        if layer == 0:
            packed, arrived, ups, downs = lax.optimization_barrier((packed, arrived, ups, downs))
        for hop in side_hops:
            keep, send = add_halves(keep, arrived)
            arrived = swap(send, *hop)
        if layer == 0:
            packed, arrived = lax.optimization_barrier((packed, arrived))
        attn_keep, attn_send = attn_grads(places, h_parts, packed)
        attn_arrived = swap(attn_send, *near_hop)
        if layer > 0:
            arrived, attn_arrived = lax.optimization_barrier((arrived, attn_arrived))
        grad_h = (keep.astype(F32) + arrived.astype(F32)).reshape(stream_in.shape)
        normed_one, factor_one = normalize(stream_in)
        grad_attn_gain = jnp.sum(grad_h * normed_one, 0)
        grad_stream = grad_middle + norm_back(
            grad_h * ln_attn_gain[layer], normed_one, factor_one
        )
        attn_rows = scatter_rest(attn_keep, attn_arrived, places.far_hops)
        if layer == 0:
            hops = side_hops[1:] + [near_hop] + places.far_hops
            upper_rows = scatter_rest(ups[0], swap(ups[1], *hops[0]), hops[1:])
            up_rows, out_rows = upper_rows[:, :wide], upper_rows[:, wide:]
            hops = side_hops + places.far_hops
            down_rows = scatter_rest(downs[0], swap(downs[1], *hops[0]), hops[1:])
        matrix_grads[layer] = (
            attn_rows[:, :width],
            attn_rows[:, width : 2 * width],
            attn_rows[:, 2 * width :],
            out_rows.T,
            up_rows,
            down_rows.T,
        )
        grad_head_all = lax.dynamic_update_slice_in_dim(
            jnp.zeros((H,), F32), grad_head, places.tensor_index * local_heads, 0
        )
        grad_mid_all = jnp.sum(mid_sum, 1)[places.tensor_sources].reshape(-1)
        small_grads[layer] = (
            grad_attn_gain, grad_head_all, jnp.sum(post_sum, 0), jnp.sum(ffn_sum, 0),
            grad_mid_all,
        )
    sizes = [part.shape[0] for part in small_grads[0]]
    vector = jnp.concatenate([part for layer in range(LAYERS) for part in small_grads[layer]])
    count = vector.shape[0]
    vector = jnp.pad(vector, (0, -count % 1024)).reshape(-1, 128)
    vector = sum_everywhere(vector).reshape(-1)
    smalls, start = [], 0
    for layer in range(LAYERS):
        found = []
        for size in sizes:
            found.append(lax.slice_in_dim(vector, start, start + size))
            start += size
        smalls.append(found)
    small = [jnp.stack([smalls[layer][at] for layer in range(LAYERS)]) for at in range(5)]
    stacked = [
        jnp.stack([matrix_grads[layer][at] for layer in range(LAYERS)]) for at in range(6)
    ]
    return (
        stream, grad_stream, small[0], stacked[0], stacked[1], stacked[2], small[1], stacked[3],
        small[2], small[3], stacked[4], small[4], stacked[5],
    )


def solution(mesh):
    rows = P(("dp", "tensor"), None)
    first = P(None, "dp", "tensor")
    second = P(None, "tensor", "dp")
    in_specs = (
        rows, P("dp", None), P(), first, first, first, P(), second, P(), P(), first, P(), second,
        rows,
    )
    out_specs = (
        rows, rows, P(), first, first, first, P(), second, P(), P(), first, P(), second,
    )
    return jax.shard_map(local, mesh=mesh, in_specs=in_specs, out_specs=out_specs, check_vma=False)
```
